128 devices in a mesh: ty: 8 (over y, core), tx: 16 (over z, x).
Axes of the slice: x: 4, y: 4, z: 4, core: 2. Of those that a mesh axis runs over, the one named last changes fastest.
Arguments:
- covariates: bfloat16 [262144, 512], P(('ty', 'tx')), may hold values from -24 to 24
- w_in: bfloat16 [512, 2048], replicated, may hold values from -0.25 to 0.25
- b_in: float32 [2048], replicated, may hold values from -3 to 3
- w_out: bfloat16 [2048, 128], replicated, may hold values from -0.125 to 0.125
- b_out: float32 [128], replicated, may hold values from -2 to 2
- owner: int32 [262144, 1], P(('ty', 'tx')), may hold values from 0 to 127; in each aligned block of 2048 rows (0 to 2047, 2048 to 4095, ...) at most 32 rows name the same one
- land_cell: int32 [262144], P(('ty', 'tx')), may hold values from 0 to 2047
- row_taps: float32 [128, 9], replicated, may hold values from 0.2 to 1
- col_taps: float32 [128, 9], replicated, may hold values from 0.2 to 1
- rate: float32 [128], replicated, may hold values from 0.2 to 1.5
- capacity: float32 [128], replicated, may hold values from 0.5 to 4
- observed: int32 [128, 2048, 128], P('ty', 'tx'), may hold values from 0 to 2
- surveyed: int32 [128, 2048], P('ty', 'tx'), may hold values 0 or 1
Outputs:
- density: float32 [128, 2048, 128], P('ty', 'tx')
- grad_w_in: float32 [512, 2048], P(('ty', 'tx'))
- grad_w_out: float32 [2048, 128], P(('ty', 'tx'))
The draws below stay inside these ranges and needn't reach their ends.
Inputs may be any that keep to these rules, and one draw needn't show every extreme that they name: `owner`: among the land cells of one device, no tile owns more than 32, and some tile owns exactly 32.
All inputs are finite; a program needn't handle non-finite values. No bound on the sum of `surveyed` on one device may be relied on, other than what follows from the above.
Results may differ from the reference program's by a relative error of at most 0.0017.
Values may be sent and summed in bfloat16 or wider, within the bound.
No kernel may reach another device: no remote copies, remote signals or barrier semaphores. Data moves between devices by JAX's collectives and lax.ppermute only.
A program may use at most 128 MiB of HBM per device.

```python
import math
import jax
import jax.numpy as jnp
import numpy as np
from jax import lax

COV = 512
HID = 2048
S = 128
STEPS = 4
ROWS_DEV = 2048
TH = 16
TW = 128
CAP = 32
LAND = 262144
NR = 128
NC = 2048
N_TX = 16
DEVICES = 128


def set_ends(array, stream_key, least, high):
    dims = array.shape
    index_at = [jax.random.randint(jax.random.fold_in(stream_key, axis), (), 0, dims[axis]) for axis in range(len(dims))]
    array = array.at[tuple(index_at)].set(least)
    longest = dims.index(max(dims))
    index_at[longest] = (index_at[longest] + 1) % dims[longest]
    return array.at[tuple(index_at)].set(high)


def spiked(drawn, own_key, source, target, parts, factor):
    def block_of(position):
        return (jnp.arange(drawn.shape[position]) // (drawn.shape[position] // parts)).reshape((-1,) + (1,) * (drawn.ndim - 1 - position))

    near = jax.random.permutation(own_key, parts)[block_of(target)]
    far = (block_of(target) + parts // 2) % parts
    return jnp.where((block_of(source) == near) | (block_of(source) == far), factor * drawn, drawn)


def levels(key, extent, cuts, smallest, top_value):
    factor_of, own = 1.0, jax.random.fold_in(key, 6)
    for position, parts in cuts:
        steps = jnp.exp(jax.random.uniform(jax.random.fold_in(own, position), (parts,), jnp.float32, smallest / len(cuts), top_value / len(cuts)))
        factor_of = factor_of * jnp.repeat(steps, extent[position] // parts).reshape([-1 if axis == position else 1 for axis in range(len(extent))])
    return factor_of


def deal_out(own_key, own, number, rows, number_of, top, bound, skew):
    sequence = jax.random.permutation(own_key, number_of)
    heavy_load, usual = load_shares(number_of, rows * top, bound, skew, True), load_shares(number_of, rows * top, bound, skew, False)
    places = jnp.arange(number_of)

    def named(tallies, rotation):
        used = int((tallies > 0).sum())
        fixed = max(1, used // 4)
        moved = fixed + (places - fixed + rotation * (used - fixed)) % max(1, number_of - fixed)
        return jnp.zeros((number_of,), jnp.int32).at[sequence[jnp.where(places < fixed, places, moved)]].set(jnp.asarray(tallies, jnp.int32))

    tallies = jnp.where(number % 4 == 0, named(heavy_load, number // 4), named(usual, number - number // 4 - 1))
    mixed = jax.random.permutation(jax.random.fold_in(own, 3), number_of)
    source_of, sink = mixed[0:number_of // 2 * 2:2], mixed[1:number_of // 2 * 2:2]
    room = jnp.minimum(tallies[source_of] - 1, bound - tallies[sink]) // 2
    room = jnp.where((source_of == sequence[0]) | (sink == sequence[0]) | (tallies[sink] == 0), 0, jnp.maximum(room, 0))
    moved = jax.random.randint(jax.random.fold_in(own, 4), (number_of // 2,), 0, 1 << 20) % (room + 1)
    tallies = tallies.at[source_of].add(-moved).at[sink].add(moved)
    members = jnp.searchsorted(jnp.cumsum(tallies), jnp.arange(rows * top), side="right").astype(jnp.int32)
    table = members.reshape(top, rows).T
    table = table[jax.random.permutation(jax.random.fold_in(own, 1), rows)]
    rotation = jax.random.randint(jax.random.fold_in(own, 2), (rows, 1), 0, top)
    return jnp.take_along_axis(table, (jnp.arange(top)[None, :] + rotation) % top, axis=1)


def load_shares(amount, total, bound, slope, full):
    portions = [(1 << 20) // math.isqrt(rank ** slope) + 1 for rank in range(1, amount + 1)]
    largest = bound if full else min(bound, max(-(-total // amount), total * portions[0] // sum(portions)))
    least = 1 if total - largest >= amount - 1 else 0
    given, surplus = [largest] + [least] * (amount - 1), total - largest - least * (amount - 1)
    while surplus > 0:
        candidates = [i for i in range(1, amount) if given[i] < largest] or [i for i in range(1, amount) if given[i] < bound]
        whole, left = sum([portions[i] for i in candidates]), surplus
        for i in candidates:
            addition = min(bound - given[i], max(1, left * portions[i] // whole), surplus)
            given[i] = given[i] + addition
            surplus = surplus - addition
    return np.array(given)


def bell_draw(stream_key, dims, scale, limit, pieces=(), dtype=jnp.bfloat16):
    factor_of = levels(stream_key, dims, pieces, -0.22, 0.18) if pieces else 1.0
    values = jax.random.normal(stream_key, dims, jnp.float32) * scale * factor_of
    return jnp.minimum(jnp.maximum(values, -limit), limit).astype(dtype)


def bell_draw_with(stream_key, dims, width, bound, pieces, heavy, held_as=jnp.bfloat16):
    array = width * jax.random.normal(stream_key, dims, jnp.float32)
    if pieces:
        array = array * levels(stream_key, dims, pieces, -0.22, 0.18)
    return jnp.clip(spiked(array, jax.random.fold_in(stream_key, 3), *heavy), -bound, bound).astype(held_as)


def setup_inputs(seed: int = 0) -> dict:
    key_list = jax.random.split(jax.random.key(seed), 14)
    covariates = bell_draw_with(key_list[0], (LAND, COV), 1.0, 24.0, ((0, 128),), (0, 1, 128, 5.5))
    w_in = bell_draw(key_list[1], (COV, HID), COV ** -0.5, 0.25)
    b_in = bell_draw(key_list[2], (HID,), 0.5, 3.0, (), jnp.float32)
    w_out = bell_draw(key_list[3], (HID, S), HID ** -0.5, 0.125)
    b_out = bell_draw(key_list[4], (S,), 0.5, 2.0, (), jnp.float32)
    owner_keys = jax.random.split(jax.random.fold_in(key_list[5], 1), LAND // ROWS_DEV)
    owner_turns = jax.random.permutation(jax.random.fold_in(key_list[5], 3), LAND // ROWS_DEV)
    owner = jax.vmap(lambda own, number: deal_out(jax.random.fold_in(key_list[5], 2), own, number, ROWS_DEV, DEVICES, 1, CAP, 2))(owner_keys, owner_turns).reshape((LAND, 1))
    land_cell = set_ends(jax.random.randint(key_list[6], (LAND,), 0, TH * TW), jax.random.fold_in(key_list[6], 1), 0, (TH * TW) - 1).astype(jnp.int32)
    row_taps = jnp.clip(jnp.exp(jax.random.uniform(key_list[7], (S, 9), jnp.float32, math.log(0.2), math.log(1.0))), 0.2, 1.0)
    col_taps = jnp.clip(jnp.exp(jax.random.uniform(key_list[8], (S, 9), jnp.float32, math.log(0.2), math.log(1.0))), 0.2, 1.0)
    rate = jnp.clip(jnp.exp(jax.random.uniform(key_list[9], (S,), jnp.float32, math.log(0.2), math.log(1.5))), 0.2, 1.5)
    capacity = jnp.clip(jnp.exp(jax.random.uniform(key_list[10], (S,), jnp.float32, math.log(0.5), math.log(4.0))), 0.5, 4.0)
    observed = set_ends(jax.random.randint(key_list[11], (NR, NC, S), 0, 3), jax.random.fold_in(key_list[11], 1), 0, 2).astype(jnp.int32)
    surveyed = set_ends((jax.random.randint(key_list[12], (NR, NC), 0, 2) < 1).astype(jnp.int32), jax.random.fold_in(key_list[12], 1), 0, 1)
    return {"covariates": covariates, "w_in": w_in, "b_in": b_in, "w_out": w_out, "b_out": b_out, "owner": owner, "land_cell": land_cell, "row_taps": row_taps, "col_taps": col_taps, "rate": rate, "capacity": capacity, "observed": observed, "surveyed": surveyed}


def normalize(taps):
    return taps / lax.optimization_barrier(jnp.sum(taps, axis=1, keepdims=True))

def disperse_valid(padded, taps_y, taps_x):
    height = padded.shape[0] - 8
    width_out = padded.shape[1] - 8
    partial_rows = taps_y[:, 0] * padded[0:height]
    for offset in range(1, 9):
        partial_rows = partial_rows + taps_y[:, offset] * padded[offset:offset + height]
    result = taps_x[:, 0] * partial_rows[:, 0:width_out]
    for offset in range(1, 9):
        result = result + taps_x[:, offset] * partial_rows[:, offset:offset + width_out]
    return result

def silu_slope(value):
    sigmoid_v = jax.nn.sigmoid(value)
    return sigmoid_v + value * sigmoid_v * (1.0 - sigmoid_v)

def reference(covariates, w_in, b_in, w_out, b_out, owner, land_cell, row_taps, col_taps, rate, capacity, observed, surveyed):
    blocks = covariates.reshape(-1, ROWS_DEV, COV)

    def forward_block(block_rows):
        preact = jnp.dot(block_rows, w_in, preferred_element_type=jnp.float32) + b_in
        hidden = jax.nn.silu(preact).astype(jnp.bfloat16)
        log_rate = jnp.dot(hidden, w_out, preferred_element_type=jnp.float32) + b_out
        return jnp.exp(log_rate)
    intensity = lax.map(forward_block, blocks)
    sent = intensity.astype(jnp.bfloat16).reshape(-1, S)
    owner_flat = owner[:, 0]
    raster_row = (owner_flat // N_TX * TH + land_cell // TW).astype(jnp.int32)
    raster_col = (owner_flat % N_TX * TW + land_cell % TW).astype(jnp.int32)
    field = 0.1 + jnp.zeros((NR, NC, S), jnp.float32).at[raster_row, raster_col].add(sent.astype(jnp.float32))
    taps_y = normalize(row_taps)
    taps_x = normalize(col_taps)
    stored = []
    for step in range(STEPS):
        padded = jnp.pad(field, ((4, 4), (4, 4), (0, 0)))
        mid_value = disperse_valid(padded, taps_y, taps_x)
        stored.append(mid_value)
        field = mid_value * (1.0 + rate) / (1.0 + rate * mid_value / capacity)
    density = field
    scale = 1.0 / math.sqrt(LAND)
    grad_field = surveyed[:, :, None].astype(jnp.float32) * (1.0 - observed.astype(jnp.float32) / density) * scale
    for step in range(STEPS - 1, -1, -1):
        mid_value = stored[step]
        denom = 1.0 + rate * mid_value / capacity
        grad_mid = grad_field * (1.0 + rate) / (denom * denom)
        padded = jnp.pad(grad_mid, ((4, 4), (4, 4), (0, 0)))
        grad_field = disperse_valid(padded, taps_y[:, ::-1], taps_x[:, ::-1])
    returned = grad_field[raster_row, raster_col].astype(jnp.bfloat16)

    def backward_block(carry, items):
        block_rows, block_back = items
        preact = jnp.dot(block_rows, w_in, preferred_element_type=jnp.float32) + b_in
        hidden = jax.nn.silu(preact).astype(jnp.bfloat16)
        log_rate = jnp.dot(hidden, w_out, preferred_element_type=jnp.float32) + b_out
        dlog = (block_back.astype(jnp.float32) * jnp.exp(log_rate)).astype(jnp.bfloat16)
        grad_out = carry[1] + lax.dot_general(hidden, dlog, (((0,), (0,)), ((), ())), preferred_element_type=jnp.float32)
        dhidden = lax.dot_general(dlog, w_out, (((1,), (1,)), ((), ())), preferred_element_type=jnp.float32)
        dpre = (dhidden * silu_slope(preact)).astype(jnp.bfloat16)
        grad_in = carry[0] + lax.dot_general(block_rows, dpre, (((0,), (0,)), ((), ())), preferred_element_type=jnp.float32)
        return ((grad_in, grad_out), None)
    initial = (jnp.zeros((COV, HID), jnp.float32), jnp.zeros((HID, S), jnp.float32))
    totals, unused = lax.scan(backward_block, initial, (blocks, returned.reshape(-1, ROWS_DEV, S)))
    return (density, totals[0], totals[1])
```

```python
import math

import jax
import jax.numpy as jnp
from jax import lax
from jax.sharding import Mesh
from jax.sharding import PartitionSpec as P

STEPS = 4
REACH = 4
TY = ("y", "core")
TX = ("z", "x")
ALL = TY + TX
F32 = jnp.float32
BF16 = jnp.bfloat16


def shift(cells, axes, count, forward):
    pairs = [(i, i + 1) for i in range(count - 1)]
    if not forward:
        pairs = [(b, a) for a, b in pairs]
    return lax.ppermute(cells, axes, pairs)


def with_halo(cells, width, tiles_y, tiles_x):
    for axes, count, dim in ((TY, tiles_y, 0), (TX, tiles_x, 1)):
        size = cells.shape[dim]
        head = lax.slice_in_dim(cells, 0, width, axis=dim).astype(BF16)
        tail = lax.slice_in_dim(cells, size - width, size, axis=dim).astype(BF16)
        cells = jnp.concatenate(
            [
                shift(tail, axes, count, True).astype(cells.dtype),
                cells,
                shift(head, axes, count, False).astype(cells.dtype),
            ],
            axis=dim,
        )
    return cells


def normalize(taps):
    return taps / jnp.sum(taps, axis=1, keepdims=True)


def disperse_valid(padded, taps_y, taps_x):
    height = padded.shape[0] - 8
    width_out = padded.shape[1] - 8
    partial_rows = taps_y[:, 0] * padded[0:height]
    for offset in range(1, 9):
        partial_rows = partial_rows + taps_y[:, offset] * padded[offset : offset + height]
    result = taps_x[:, 0] * partial_rows[:, 0:width_out]
    for offset in range(1, 9):
        result = result + taps_x[:, offset] * partial_rows[:, offset : offset + width_out]
    return result


def silu_slope(value):
    sigmoid_v = jax.nn.sigmoid(value)
    return sigmoid_v + value * sigmoid_v * (1.0 - sigmoid_v)


def crop(cells, margin):
    return cells[margin : cells.shape[0] - margin, margin : cells.shape[1] - margin]


def reduce_scatter(part):
    n_y = lax.axis_size("y")
    peers = n_y * lax.axis_size("z") * lax.axis_size("x")
    rows, cols = part.shape
    parts = part.reshape(n_y, 2, rows // n_y // 2, cols)
    core = lax.axis_index("core")
    mine = lax.dynamic_index_in_dim(parts, core, 1, keepdims=False)
    other = lax.dynamic_index_in_dim(parts, 1 - core, 1, keepdims=False)
    both = mine + lax.ppermute(other, "core", [(0, 1), (1, 0)])
    both = both.reshape(peers, rows // peers // 2, cols)
    return jnp.sum(lax.all_to_all(both, ("y", "z", "x"), 0, 0), axis=0)


def local(
    covariates,
    w_in,
    b_in,
    w_out,
    b_out,
    owner,
    land_cell,
    row_taps,
    col_taps,
    rate,
    capacity,
    observed,
    surveyed,
):
    row_count = covariates.shape[0]
    tiles_y = lax.axis_size("y") * lax.axis_size("core")
    tiles_x = lax.axis_size("z") * lax.axis_size("x")
    devices = tiles_y * tiles_x
    slot_count = 2 * row_count // devices
    slots = devices * slot_count
    height, tile_width, species = observed.shape
    cell_count = height * tile_width
    preact = jnp.dot(covariates, w_in, preferred_element_type=F32) + b_in
    hidden = jax.nn.silu(preact).astype(BF16)
    log_rate = jnp.dot(hidden, w_out, preferred_element_type=F32) + b_out
    intensity = jnp.exp(log_rate)
    sent = intensity.astype(BF16)

    owner_rows = owner[:, 0]
    owner_hot = owner_rows[:, None] == jnp.arange(devices, dtype=jnp.int32)[None, :]
    row_ids = jnp.arange(row_count, dtype=jnp.int32)
    earlier = (row_ids[None, :] < row_ids[:, None]).astype(BF16)
    before = jnp.dot(earlier, owner_hot.astype(BF16), preferred_element_type=F32)
    slot_idx = jnp.sum(jnp.where(owner_hot, before, 0.0), axis=1).astype(jnp.int32)
    flat_slot = owner_rows * slot_count + slot_idx

    slot_ids = jnp.arange(slots, dtype=jnp.int32)
    pack = (flat_slot[None, :] == slot_ids[:, None]).astype(BF16)
    send_values = jnp.dot(pack, sent, preferred_element_type=F32).astype(BF16)
    slot_hot = slot_idx[:, None] == jnp.arange(slot_count, dtype=jnp.int32)[None, :]
    place_row = (land_cell // tile_width + 1).astype(F32)[:, None]
    place_col = (land_cell % tile_width).astype(F32)[:, None]
    places = jnp.concatenate(
        [jnp.where(slot_hot, place_row, 0.0), jnp.where(slot_hot, place_col, 0.0)], axis=1
    ).astype(BF16)
    table = lax.dot_general(
        owner_hot.astype(BF16), places, (((0,), (0,)), ((), ())), preferred_element_type=F32
    ).astype(BF16)
    table = jnp.pad(table[:, None, :], ((0, 0), (0, 7), (0, species - 2 * slot_count)))
    send = jnp.concatenate([send_values.reshape(devices, slot_count, species), table], axis=1)
    got = lax.all_to_all(send, ALL, split_axis=0, concat_axis=0, tiled=True)
    got_values = got[:, :slot_count].reshape(slots, species)
    got_row = got[:, slot_count, :slot_count].astype(jnp.int32)
    got_col = got[:, slot_count, slot_count : 2 * slot_count].astype(jnp.int32)
    cell_list = jnp.where(got_row > 0, (got_row - 1) * tile_width + got_col, -1).reshape(-1)
    cell_ids = jnp.arange(cell_count, dtype=jnp.int32)
    place = (cell_list[None, :] == cell_ids[:, None]).astype(BF16)
    start_field = jnp.dot(place, got_values, preferred_element_type=F32)
    start_field = start_field.reshape(height, tile_width, species)

    taps_y = normalize(row_taps)
    taps_x = normalize(col_taps)
    back_y = taps_y[:, ::-1]
    back_x = taps_x[:, ::-1]
    scale = 1.0 / math.sqrt(row_count * devices)
    tile_y = lax.axis_index(TY)
    tile_x = lax.axis_index(TX)

    def on_raster(cells, margin):
        rows = tile_y * height - margin + jnp.arange(cells.shape[0])
        cols = tile_x * tile_width - margin + jnp.arange(cells.shape[1])
        ok_rows = (rows >= 0) & (rows < tiles_y * height)
        ok_cols = (cols >= 0) & (cols < tiles_x * tile_width)
        return jnp.where((ok_rows[:, None] & ok_cols[None, :])[:, :, None], cells, 0.0)

    margin = STEPS * REACH
    field = on_raster(0.1 + with_halo(start_field, margin, tiles_y, tiles_x), margin)
    stored = []
    for step in range(STEPS):
        margin -= REACH
        mid_value = disperse_valid(field, taps_y, taps_x)
        stored.append(mid_value)
        field = mid_value * (1.0 + rate) / (1.0 + rate * mid_value / capacity)
        if margin:
            field = on_raster(field, margin)
    grad_field = (
        surveyed[:, :, None].astype(F32) * (1.0 - observed.astype(F32) / field) * scale
    )

    def grown(grad, step, margin):
        mid_value = crop(stored[step], (STEPS - 1 - step) * REACH - margin)
        denom = 1.0 + rate * mid_value / capacity
        return grad * (1.0 + rate) / (denom * denom)

    for step in range(STEPS - 1, 0, -2):
        wide = with_halo(grown(grad_field, step, 0), 2 * REACH, tiles_y, tiles_x)
        grad_field = disperse_valid(wide, back_y, back_x)
        grad_mid = on_raster(grown(grad_field, step - 1, REACH), REACH)
        grad_field = disperse_valid(grad_mid, back_y, back_x)

    take = (cell_list[:, None] == cell_ids[None, :]).astype(BF16)
    back_values = jnp.dot(
        take, grad_field.reshape(cell_count, species).astype(BF16), preferred_element_type=F32
    ).astype(BF16)
    home_values = lax.all_to_all(
        back_values.reshape(devices, slot_count, species),
        ALL,
        split_axis=0,
        concat_axis=0,
        tiled=True,
    )
    unpack = (flat_slot[:, None] == slot_ids[None, :]).astype(BF16)
    returned = jnp.dot(unpack, home_values.reshape(slots, species), preferred_element_type=F32)
    dlog = (returned * intensity).astype(BF16)
    dhidden = lax.dot_general(dlog, w_out, (((1,), (1,)), ((), ())), preferred_element_type=F32)
    dpre = (dhidden * silu_slope(preact)).astype(BF16)
    grad_w_out = reduce_scatter(
        lax.dot_general(hidden, dlog, (((0,), (0,)), ((), ())), preferred_element_type=F32)
    )
    grad_w_in = reduce_scatter(
        lax.dot_general(covariates, dpre, (((0,), (0,)), ((), ())), preferred_element_type=F32)
    )
    return (field, grad_w_in, grad_w_out)


def solution(mesh):
    tiles_y, tiles_x = mesh.devices.shape
    split = Mesh(mesh.devices.reshape(tiles_y // 2, 2, tiles_x // 4, 4), ALL)
    in_specs = (
        P(ALL, None),
        P(),
        P(),
        P(),
        P(),
        P(ALL, None),
        P(ALL),
        P(),
        P(),
        P(),
        P(),
        P(TY, TX, None),
        P(TY, TX),
    )
    out_specs = (P(TY, TX, None), P(ALL, None), P(ALL, None))
    return jax.shard_map(local, mesh=split, in_specs=in_specs, out_specs=out_specs, check_vma=False)
```

```python
import math

import jax
import jax.numpy as jnp
from jax import lax
from jax.experimental import pallas as pl
from jax.experimental.pallas import tpu as pltpu
from jax.sharding import Mesh
from jax.sharding import PartitionSpec as P

STEPS = 4
REACH = 4
TY = ("y", "core")
TX = ("z", "x")
ALL = TY + TX
F32 = jnp.float32
BF16 = jnp.bfloat16


def shift(cells, axes, count, forward):
    pairs = [(i, i + 1) for i in range(count - 1)]
    if not forward:
        pairs = [(b, a) for a, b in pairs]
    return lax.ppermute(cells, axes, pairs)


def with_halo(cells, width, tiles_y, tiles_x):
    for axes, count, dim in ((TY, tiles_y, 0), (TX, tiles_x, 1)):
        size = cells.shape[dim]
        head = lax.slice_in_dim(cells, 0, width, axis=dim).astype(BF16)
        tail = lax.slice_in_dim(cells, size - width, size, axis=dim).astype(BF16)
        cells = jnp.concatenate(
            [
                shift(tail, axes, count, True).astype(cells.dtype),
                cells,
                shift(head, axes, count, False).astype(cells.dtype),
            ],
            axis=dim,
        )
    return cells


def normalize(taps):
    return taps / jnp.sum(taps, axis=1, keepdims=True)


def disperse_valid(padded, taps_y, taps_x):
    height = padded.shape[0] - 8
    width_out = padded.shape[1] - 8
    partial_rows = taps_y[:, 0] * padded[0:height]
    for offset in range(1, 9):
        partial_rows = partial_rows + taps_y[:, offset] * padded[offset : offset + height]
    result = taps_x[:, 0] * partial_rows[:, 0:width_out]
    for offset in range(1, 9):
        result = result + taps_x[:, offset] * partial_rows[:, offset : offset + width_out]
    return result


def crop(cells, margin):
    return cells[margin : cells.shape[0] - margin, margin : cells.shape[1] - margin]


def forward_body(x_ref, w_in_ref, b_in_ref, w_out_ref, b_out_ref, intensity_ref):
    chunk = 512
    x = x_ref[...]
    log_rate = b_out_ref[...]
    for at in range(0, w_in_ref.shape[1], chunk):
        pre = jnp.dot(x, w_in_ref[:, at : at + chunk], preferred_element_type=F32)
        pre = pre + b_in_ref[:, at : at + chunk]
        hidden = (pre / (1.0 + jnp.exp(-pre))).astype(BF16)
        log_rate = log_rate + jnp.dot(
            hidden, w_out_ref[at : at + chunk, :], preferred_element_type=F32
        )
    intensity_ref[...] = jnp.exp(log_rate)


def forward(x, w_in, b_in, w_out, b_out, block=512):
    rows, cov = x.shape
    hid, species = w_out.shape

    def whole(shape):
        return pl.BlockSpec(shape, lambda i: (0, 0), pipeline_mode=pl.Buffered(1))

    return pl.pallas_call(
        forward_body,
        out_shape=jax.ShapeDtypeStruct((rows, species), F32),
        grid=(rows // block,),
        in_specs=[
            pl.BlockSpec((block, cov), lambda i: (i, 0)),
            whole((cov, hid)),
            whole((1, hid)),
            whole((hid, species)),
            whole((1, species)),
        ],
        out_specs=pl.BlockSpec((block, species), lambda i: (i, 0)),
        compiler_params=pltpu.CompilerParams(vmem_limit_bytes=40 << 20),
        name="land_forward",
    )(x, w_in, b_in[None, :], w_out, b_out[None, :])


def backward_body(
    core_ref, x_ref, dlog_ref, w_in_ref, b_in_ref, w_out_ref, out_ref, in_acc, out_acc
):
    j, i = pl.program_id(0), pl.program_id(1)
    x, dlog = x_ref[...], dlog_ref[...]
    pre = jnp.dot(x, w_in_ref[...], preferred_element_type=F32) + b_in_ref[...]
    gate = 1.0 / (1.0 + jnp.exp(-pre))
    scaled = pre * gate
    slope = gate + scaled * (1.0 - gate)
    dhidden = lax.dot_general(
        dlog, w_out_ref[...], (((1,), (1,)), ((), ())), preferred_element_type=F32
    )
    dpre = (dhidden * slope).astype(BF16)
    in_part = lax.dot_general(x, dpre, (((0,), (0,)), ((), ())), preferred_element_type=F32)
    out_part = lax.dot_general(
        scaled.astype(BF16), dlog, (((0,), (0,)), ((), ())), preferred_element_type=F32
    )

    @pl.when(i == 0)
    def _():
        in_acc[...] = in_part
        out_acc[...] = out_part

    @pl.when(i > 0)
    def _():
        in_acc[...] += in_part
        out_acc[...] += out_part

    @pl.when(i == pl.num_programs(1) - 1)
    def _():
        n_y = 4
        zx = out_ref.shape[0] // n_y
        tiles = in_acc.shape[1] // 128
        rows = in_acc.shape[0] // out_ref.shape[0] // 2
        units = out_acc.shape[0] // zx
        for y in range(n_y):
            for p in range(zx):
                for c in range(2):
                    for k in range(tiles):
                        out_ref[
                            y * zx + p, pl.ds((j * tiles + k) * 2 * rows + c * rows, rows), :
                        ] = in_acc[
                            pl.ds((y * 2 * zx + c * zx + p) * rows, rows),
                            k * 128 : (k + 1) * 128,
                        ]
        base = 2 * rows * tiles * n_y
        for p in range(zx):
            out_ref[j * zx + p, base : base + units, :] = out_acc[p * units : (p + 1) * units, :]


def backward(core, x, dlog, w_in, b_in, w_out, peers, block=2048):
    n_y = 4
    rows, cov = x.shape
    hid, species = w_out.shape
    width = hid // n_y // 2
    send_rows = cov // peers * (hid // 2 // 128) + hid // 2 // peers
    grid_spec = pltpu.PrefetchScalarGridSpec(
        num_scalar_prefetch=1,
        grid=(n_y, rows // block),
        in_specs=[
            pl.BlockSpec((block, cov), lambda j, i, c: (i, 0)),
            pl.BlockSpec((block, species), lambda j, i, c: (i, 0)),
            pl.BlockSpec((cov, width), lambda j, i, c: (0, 2 * j + c[0])),
            pl.BlockSpec((1, width), lambda j, i, c: (0, 2 * j + c[0])),
            pl.BlockSpec((width, species), lambda j, i, c: (2 * j + c[0], 0)),
        ],
        out_specs=pl.BlockSpec(
            (peers, send_rows, 128), lambda j, i, c: (0, 0, 0), pipeline_mode=pl.Buffered(1)
        ),
        scratch_shapes=[pltpu.VMEM((cov, width), F32), pltpu.VMEM((width, species), F32)],
    )
    return pl.pallas_call(
        backward_body,
        out_shape=jax.ShapeDtypeStruct((peers, send_rows, 128), F32),
        grid_spec=grid_spec,
        compiler_params=pltpu.CompilerParams(vmem_limit_bytes=50 << 20),
        name="land_backward",
    )(core, x, dlog, w_in, b_in[None, :], w_out)


def other_core(values):
    return lax.ppermute(values, "core", [(0, 1), (1, 0)])


def local(
    covariates,
    w_in,
    b_in,
    w_out,
    b_out,
    owner,
    land_cell,
    row_taps,
    col_taps,
    rate,
    capacity,
    observed,
    surveyed,
):
    row_count = covariates.shape[0]
    tiles_y = lax.axis_size("y") * lax.axis_size("core")
    tiles_x = lax.axis_size("z") * lax.axis_size("x")
    devices = tiles_y * tiles_x
    slot_count = 2 * row_count // devices
    slots = devices * slot_count
    height, tile_width, species = observed.shape
    cell_count = height * tile_width
    both_covariates = jnp.concatenate([covariates, other_core(covariates)])
    intensity = forward(covariates, w_in, b_in, w_out, b_out)
    sent = intensity.astype(BF16)

    owner_rows = owner[:, 0]
    owner_hot = owner_rows[:, None] == jnp.arange(devices, dtype=jnp.int32)[None, :]
    row_ids = jnp.arange(row_count, dtype=jnp.int32)
    earlier = (row_ids[None, :] < row_ids[:, None]).astype(BF16)
    before = jnp.dot(earlier, owner_hot.astype(BF16), preferred_element_type=F32)
    slot_idx = jnp.sum(jnp.where(owner_hot, before, 0.0), axis=1).astype(jnp.int32)
    flat_slot = owner_rows * slot_count + slot_idx

    slot_ids = jnp.arange(slots, dtype=jnp.int32)
    pack = (flat_slot[None, :] == slot_ids[:, None]).astype(BF16)
    send_values = jnp.dot(pack, sent, preferred_element_type=F32).astype(BF16)
    slot_hot = slot_idx[:, None] == jnp.arange(slot_count, dtype=jnp.int32)[None, :]
    place_row = (land_cell // tile_width + 1).astype(F32)[:, None]
    place_col = (land_cell % tile_width).astype(F32)[:, None]
    places = jnp.concatenate(
        [jnp.where(slot_hot, place_row, 0.0), jnp.where(slot_hot, place_col, 0.0)], axis=1
    ).astype(BF16)
    table = lax.dot_general(
        owner_hot.astype(BF16), places, (((0,), (0,)), ((), ())), preferred_element_type=F32
    ).astype(BF16)
    table = jnp.pad(table[:, None, :], ((0, 0), (0, 7), (0, species - 2 * slot_count)))
    send = jnp.concatenate([send_values.reshape(devices, slot_count, species), table], axis=1)
    got = lax.all_to_all(send, ALL, split_axis=0, concat_axis=0, tiled=True)
    got_values = got[:, :slot_count].reshape(slots, species)
    got_row = got[:, slot_count, :slot_count].astype(jnp.int32)
    got_col = got[:, slot_count, slot_count : 2 * slot_count].astype(jnp.int32)
    cell_list = jnp.where(got_row > 0, (got_row - 1) * tile_width + got_col, -1).reshape(-1)
    cell_ids = jnp.arange(cell_count, dtype=jnp.int32)
    place = (cell_list[None, :] == cell_ids[:, None]).astype(BF16)
    start_field = jnp.dot(place, got_values, preferred_element_type=F32)
    start_field = start_field.reshape(height, tile_width, species)

    taps_y = normalize(row_taps)
    taps_x = normalize(col_taps)
    back_y = taps_y[:, ::-1]
    back_x = taps_x[:, ::-1]
    scale = 1.0 / math.sqrt(row_count * devices)
    tile_y = lax.axis_index(TY)
    tile_x = lax.axis_index(TX)

    def on_raster(cells, margin):
        rows = tile_y * height - margin + jnp.arange(cells.shape[0])
        cols = tile_x * tile_width - margin + jnp.arange(cells.shape[1])
        ok_rows = (rows >= 0) & (rows < tiles_y * height)
        ok_cols = (cols >= 0) & (cols < tiles_x * tile_width)
        return jnp.where((ok_rows[:, None] & ok_cols[None, :])[:, :, None], cells, 0.0)

    margin = STEPS * REACH
    field = on_raster(0.1 + with_halo(start_field, margin, tiles_y, tiles_x), margin)
    stored = []
    for step in range(STEPS):
        margin -= REACH
        mid_value = disperse_valid(field, taps_y, taps_x)
        stored.append(mid_value)
        field = mid_value * (1.0 + rate) / (1.0 + rate * mid_value / capacity)
        if margin:
            field = on_raster(field, margin)
    grad_field = (
        surveyed[:, :, None].astype(F32) * (1.0 - observed.astype(F32) / field) * scale
    )

    def grown(grad, step, margin):
        mid_value = crop(stored[step], (STEPS - 1 - step) * REACH - margin)
        denom = 1.0 + rate * mid_value / capacity
        return grad * (1.0 + rate) / (denom * denom)

    for step in range(STEPS - 1, 0, -2):
        wide = with_halo(grown(grad_field, step, 0), 2 * REACH, tiles_y, tiles_x)
        grad_field = disperse_valid(wide, back_y, back_x)
        grad_mid = on_raster(grown(grad_field, step - 1, REACH), REACH)
        grad_field = disperse_valid(grad_mid, back_y, back_x)

    take = (cell_list[:, None] == cell_ids[None, :]).astype(BF16)
    back_values = jnp.dot(
        take, grad_field.reshape(cell_count, species).astype(BF16), preferred_element_type=F32
    ).astype(BF16)
    home_values = lax.all_to_all(
        back_values.reshape(devices, slot_count, species),
        ALL,
        split_axis=0,
        concat_axis=0,
        tiled=True,
    )
    unpack = (flat_slot[:, None] == slot_ids[None, :]).astype(BF16)
    returned = jnp.dot(unpack, home_values.reshape(slots, species), preferred_element_type=F32)
    dlog = (returned * intensity).astype(BF16)
    core = lax.axis_index("core")
    peers = devices // 2
    both_dlog = jnp.concatenate([dlog, other_core(dlog)])
    pieces = backward(core[None], both_covariates, both_dlog, w_in, b_in, w_out, peers)
    pieces = jnp.sum(lax.all_to_all(pieces, ("y", "z", "x"), 0, 0), axis=0)
    hid, cov = w_in.shape[1], w_in.shape[0]
    rows_in = cov // devices
    in_rows = 2 * rows_in * (hid // 2 // species)
    grad_w_out = pieces[in_rows:]
    halves = pieces[:in_rows].reshape(4, hid // 8 // species, 2, rows_in, species)
    mine = lax.dynamic_index_in_dim(halves, core, 2, keepdims=False)
    theirs = other_core(lax.dynamic_index_in_dim(halves, 1 - core, 2, keepdims=False))
    first, second = jnp.where(core == 0, mine, theirs), jnp.where(core == 0, theirs, mine)
    grad_w_in = jnp.stack([first, second], axis=1)
    grad_w_in = grad_w_in.transpose(3, 0, 1, 2, 4).reshape(rows_in, hid)
    return (field, grad_w_in, grad_w_out)


def solution(mesh):
    tiles_y, tiles_x = mesh.devices.shape
    split = Mesh(mesh.devices.reshape(tiles_y // 2, 2, tiles_x // 4, 4), ALL)
    in_specs = (
        P(ALL, None),
        P(),
        P(),
        P(),
        P(),
        P(ALL, None),
        P(ALL),
        P(),
        P(),
        P(),
        P(),
        P(TY, TX, None),
        P(TY, TX),
    )
    out_specs = (P(TY, TX, None), P(ALL, None), P(ALL, None))
    return jax.shard_map(local, mesh=split, in_specs=in_specs, out_specs=out_specs, check_vma=False)
```

```python
import math

import jax
import jax.numpy as jnp
from jax import lax
from jax.experimental import pallas as pl
from jax.experimental.pallas import tpu as pltpu
from jax.sharding import Mesh
from jax.sharding import PartitionSpec as P

STEPS = 4
REACH = 4
TY = ("y", "core")
TX = ("z", "x")
ALL = TY + TX
F32 = jnp.float32
BF16 = jnp.bfloat16


def shift(cells, axes, count, forward):
    pairs = [(i, i + 1) for i in range(count - 1)]
    if not forward:
        pairs = [(b, a) for a, b in pairs]
    return lax.ppermute(cells, axes, pairs)


def with_halo(cells, width, tiles_y, tiles_x):
    for axes, count, dim in ((TY, tiles_y, 0), (TX, tiles_x, 1)):
        size = cells.shape[dim]
        head = lax.slice_in_dim(cells, 0, width, axis=dim).astype(BF16)
        tail = lax.slice_in_dim(cells, size - width, size, axis=dim).astype(BF16)
        cells = jnp.concatenate(
            [
                shift(tail, axes, count, True).astype(cells.dtype),
                cells,
                shift(head, axes, count, False).astype(cells.dtype),
            ],
            axis=dim,
        )
    return cells


def normalize(taps):
    return taps / jnp.sum(taps, axis=1, keepdims=True)


def disperse_valid(padded, taps_y, taps_x):
    height = padded.shape[0] - 8
    width_out = padded.shape[1] - 8
    partial_rows = taps_y[:, 0] * padded[0:height]
    for offset in range(1, 9):
        partial_rows = partial_rows + taps_y[:, offset] * padded[offset : offset + height]
    result = taps_x[:, 0] * partial_rows[:, 0:width_out]
    for offset in range(1, 9):
        result = result + taps_x[:, offset] * partial_rows[:, offset : offset + width_out]
    return result


def crop(cells, margin):
    return cells[margin : cells.shape[0] - margin, margin : cells.shape[1] - margin]


def forward_body(x_ref, w_in_ref, b_in_ref, w_out_ref, b_out_ref, intensity_ref):
    chunk = 512
    x = x_ref[...]
    log_rate = b_out_ref[...]
    for at in range(0, w_in_ref.shape[1], chunk):
        pre = jnp.dot(x, w_in_ref[:, at : at + chunk], preferred_element_type=F32)
        pre = pre + b_in_ref[:, at : at + chunk]
        hidden = (pre / (1.0 + jnp.exp(-pre))).astype(BF16)
        log_rate = log_rate + jnp.dot(
            hidden, w_out_ref[at : at + chunk, :], preferred_element_type=F32
        )
    intensity_ref[...] = jnp.exp(log_rate)


def forward(x, w_in, b_in, w_out, b_out, block=512):
    rows, cov = x.shape
    hid, species = w_out.shape

    def whole(shape):
        return pl.BlockSpec(shape, lambda i: (0, 0), pipeline_mode=pl.Buffered(1))

    return pl.pallas_call(
        forward_body,
        out_shape=jax.ShapeDtypeStruct((rows, species), F32),
        grid=(rows // block,),
        in_specs=[
            pl.BlockSpec((block, cov), lambda i: (i, 0)),
            whole((cov, hid)),
            whole((1, hid)),
            whole((hid, species)),
            whole((1, species)),
        ],
        out_specs=pl.BlockSpec((block, species), lambda i: (i, 0)),
        compiler_params=pltpu.CompilerParams(vmem_limit_bytes=40 << 20),
        name="land_forward",
    )(x, w_in, b_in[None, :], w_out, b_out[None, :])


def gates_body(core_ref, x_ref, w_in_ref, b_in_ref, hidden_ref, slope_ref):
    pre = jnp.dot(x_ref[...], w_in_ref[...], preferred_element_type=F32) + b_in_ref[...]
    gate = 1.0 / (1.0 + jnp.exp(-pre))
    scaled = pre * gate
    hidden_ref[...] = scaled.astype(BF16)
    slope_ref[...] = gate + scaled * (1.0 - gate)


def gates(core, x, w_in, b_in):
    n_y = 4
    rows, cov = x.shape
    hid = w_in.shape[1]
    width = hid // n_y // 2
    block = pl.BlockSpec((rows, width), lambda j, c: (0, j))
    return pl.pallas_call(
        gates_body,
        out_shape=[
            jax.ShapeDtypeStruct((rows, hid // 2), BF16),
            jax.ShapeDtypeStruct((rows, hid // 2), F32),
        ],
        grid_spec=pltpu.PrefetchScalarGridSpec(
            num_scalar_prefetch=1,
            grid=(n_y,),
            in_specs=[
                pl.BlockSpec((rows, cov), lambda j, c: (0, 0), pipeline_mode=pl.Buffered(1)),
                pl.BlockSpec((cov, width), lambda j, c: (0, 2 * j + c[0])),
                pl.BlockSpec((1, width), lambda j, c: (0, 2 * j + c[0])),
            ],
            out_specs=[block, block],
        ),
        compiler_params=pltpu.CompilerParams(vmem_limit_bytes=40 << 20),
        name="land_gates",
    )(core, x, w_in, b_in[None, :])


def backward_body(
    core_ref,
    x_own,
    x_other,
    dlog_own,
    dlog_other,
    hidden_own,
    hidden_other,
    slope_own,
    slope_other,
    w_out_ref,
    out_ref,
    in_acc,
    out_acc,
):
    j = pl.program_id(0)
    w_out = w_out_ref[...]

    def parts(x_ref, dlog_ref, hidden_ref, slope_ref):
        dlog = dlog_ref[...]
        dhidden = lax.dot_general(
            dlog, w_out, (((1,), (1,)), ((), ())), preferred_element_type=F32
        )
        dpre = (dhidden * slope_ref[...]).astype(BF16)
        rows = (((0,), (0,)), ((), ()))
        return (
            lax.dot_general(x_ref[...], dpre, rows, preferred_element_type=F32),
            lax.dot_general(hidden_ref[...], dlog, rows, preferred_element_type=F32),
        )

    in_acc[...], out_acc[...] = parts(x_own, dlog_own, hidden_own, slope_own)
    in_part, out_part = parts(x_other, dlog_other, hidden_other, slope_other)
    in_acc[...] += in_part
    out_acc[...] += out_part
    n_y = 4
    zx = out_ref.shape[0] // n_y
    tiles = in_acc.shape[1] // 128
    rows = in_acc.shape[0] // out_ref.shape[0] // 2
    units = out_acc.shape[0] // zx
    for y in range(n_y):
        for p in range(zx):
            for c in range(2):
                for k in range(tiles):
                    out_ref[
                        y * zx + p, pl.ds((j * tiles + k) * 2 * rows + c * rows, rows), :
                    ] = in_acc[
                        pl.ds((y * 2 * zx + c * zx + p) * rows, rows),
                        k * 128 : (k + 1) * 128,
                    ]
    base = 2 * rows * tiles * n_y
    for p in range(zx):
        out_ref[j * zx + p, base : base + units, :] = out_acc[p * units : (p + 1) * units, :]


def backward(core, x, dlog, hidden, slope, w_out, peers):
    n_y = 4
    rows, cov = x[0].shape
    hid, species = w_out.shape
    width = hid // n_y // 2
    send_rows = cov // peers * (hid // 2 // 128) + hid // 2 // peers

    def fixed(shape):
        return pl.BlockSpec(
            shape, lambda j, c: (0,) * len(shape), pipeline_mode=pl.Buffered(1)
        )

    grid_spec = pltpu.PrefetchScalarGridSpec(
        num_scalar_prefetch=1,
        grid=(n_y,),
        in_specs=[fixed((rows, cov))] * 2
        + [fixed((rows, species))] * 2
        + [pl.BlockSpec((rows, width), lambda j, c: (0, j))] * 4
        + [pl.BlockSpec((width, species), lambda j, c: (2 * j + c[0], 0))],
        out_specs=fixed((peers, send_rows, 128)),
        scratch_shapes=[pltpu.VMEM((cov, width), F32), pltpu.VMEM((width, species), F32)],
    )
    return pl.pallas_call(
        backward_body,
        out_shape=jax.ShapeDtypeStruct((peers, send_rows, 128), F32),
        grid_spec=grid_spec,
        compiler_params=pltpu.CompilerParams(vmem_limit_bytes=50 << 20),
        name="land_backward",
    )(core, *x, *dlog, *hidden, *slope, w_out)


def other_core(values):
    return lax.ppermute(values, "core", [(0, 1), (1, 0)])


def local(
    covariates,
    w_in,
    b_in,
    w_out,
    b_out,
    owner,
    land_cell,
    row_taps,
    col_taps,
    rate,
    capacity,
    observed,
    surveyed,
):
    row_count = covariates.shape[0]
    tiles_y = lax.axis_size("y") * lax.axis_size("core")
    tiles_x = lax.axis_size("z") * lax.axis_size("x")
    devices = tiles_y * tiles_x
    slot_count = 2 * row_count // devices
    slots = devices * slot_count
    height, tile_width, species = observed.shape
    cell_count = height * tile_width
    core = lax.axis_index("core")
    theirs = other_core(covariates)
    intensity = forward(covariates, w_in, b_in, w_out, b_out)
    sent = intensity.astype(BF16)

    owner_rows = owner[:, 0]
    owner_hot = owner_rows[:, None] == jnp.arange(devices, dtype=jnp.int32)[None, :]
    row_ids = jnp.arange(row_count, dtype=jnp.int32)
    earlier = (row_ids[None, :] < row_ids[:, None]).astype(BF16)
    before = jnp.dot(earlier, owner_hot.astype(BF16), preferred_element_type=F32)
    slot_idx = jnp.sum(jnp.where(owner_hot, before, 0.0), axis=1).astype(jnp.int32)
    flat_slot = owner_rows * slot_count + slot_idx

    slot_ids = jnp.arange(slots, dtype=jnp.int32)
    pack = (flat_slot[None, :] == slot_ids[:, None]).astype(BF16)
    send_values = jnp.dot(pack, sent, preferred_element_type=F32).astype(BF16)
    slot_hot = slot_idx[:, None] == jnp.arange(slot_count, dtype=jnp.int32)[None, :]
    place_row = (land_cell // tile_width + 1).astype(F32)[:, None]
    place_col = (land_cell % tile_width).astype(F32)[:, None]
    places = jnp.concatenate(
        [jnp.where(slot_hot, place_row, 0.0), jnp.where(slot_hot, place_col, 0.0)], axis=1
    ).astype(BF16)
    table = lax.dot_general(
        owner_hot.astype(BF16), places, (((0,), (0,)), ((), ())), preferred_element_type=F32
    ).astype(BF16)
    table = jnp.pad(table[:, None, :], ((0, 0), (0, 7), (0, species - 2 * slot_count)))
    send = jnp.concatenate([send_values.reshape(devices, slot_count, species), table], axis=1)
    got = lax.all_to_all(send, ALL, split_axis=0, concat_axis=0, tiled=True)
    send, theirs = lax.optimization_barrier((send, theirs))
    own_gates = gates(core[None], covariates, w_in, b_in)
    their_gates = gates(core[None], theirs, w_in, b_in)
    got, own_gates, their_gates = lax.optimization_barrier((got, own_gates, their_gates))
    got_values = got[:, :slot_count].reshape(slots, species)
    got_row = got[:, slot_count, :slot_count].astype(jnp.int32)
    got_col = got[:, slot_count, slot_count : 2 * slot_count].astype(jnp.int32)
    cell_list = jnp.where(got_row > 0, (got_row - 1) * tile_width + got_col, -1).reshape(-1)
    cell_ids = jnp.arange(cell_count, dtype=jnp.int32)
    place = (cell_list[None, :] == cell_ids[:, None]).astype(BF16)
    start_field = jnp.dot(place, got_values, preferred_element_type=F32)
    start_field = start_field.reshape(height, tile_width, species)

    taps_y = normalize(row_taps)
    taps_x = normalize(col_taps)
    back_y = taps_y[:, ::-1]
    back_x = taps_x[:, ::-1]
    scale = 1.0 / math.sqrt(row_count * devices)
    tile_y = lax.axis_index(TY)
    tile_x = lax.axis_index(TX)

    def on_raster(cells, margin):
        rows = tile_y * height - margin + jnp.arange(cells.shape[0])
        cols = tile_x * tile_width - margin + jnp.arange(cells.shape[1])
        ok_rows = (rows >= 0) & (rows < tiles_y * height)
        ok_cols = (cols >= 0) & (cols < tiles_x * tile_width)
        return jnp.where((ok_rows[:, None] & ok_cols[None, :])[:, :, None], cells, 0.0)

    margin = STEPS * REACH
    field = on_raster(0.1 + with_halo(start_field, margin, tiles_y, tiles_x), margin)
    stored = []
    for step in range(STEPS):
        margin -= REACH
        mid_value = disperse_valid(field, taps_y, taps_x)
        stored.append(mid_value)
        field = mid_value * (1.0 + rate) / (1.0 + rate * mid_value / capacity)
        if margin:
            field = on_raster(field, margin)
    grad_field = (
        surveyed[:, :, None].astype(F32) * (1.0 - observed.astype(F32) / field) * scale
    )

    def grown(grad, step, margin):
        mid_value = crop(stored[step], (STEPS - 1 - step) * REACH - margin)
        denom = 1.0 + rate * mid_value / capacity
        return grad * (1.0 + rate) / (denom * denom)

    for step in range(STEPS - 1, 0, -2):
        wide = with_halo(grown(grad_field, step, 0), 2 * REACH, tiles_y, tiles_x)
        grad_field = disperse_valid(wide, back_y, back_x)
        grad_mid = on_raster(grown(grad_field, step - 1, REACH), REACH)
        grad_field = disperse_valid(grad_mid, back_y, back_x)

    take = (cell_list[:, None] == cell_ids[None, :]).astype(BF16)
    back_values = jnp.dot(
        take, grad_field.reshape(cell_count, species).astype(BF16), preferred_element_type=F32
    ).astype(BF16)
    home_values = lax.all_to_all(
        back_values.reshape(devices, slot_count, species),
        ALL,
        split_axis=0,
        concat_axis=0,
        tiled=True,
    )
    unpack = (flat_slot[:, None] == slot_ids[None, :]).astype(BF16)
    returned = jnp.dot(unpack, home_values.reshape(slots, species), preferred_element_type=F32)
    dlog = (returned * intensity).astype(BF16)
    peers = devices // 2
    pieces = backward(
        core[None],
        (covariates, theirs),
        (dlog, other_core(dlog)),
        (own_gates[0], their_gates[0]),
        (own_gates[1], their_gates[1]),
        w_out,
        peers,
    )
    pieces = jnp.sum(lax.all_to_all(pieces, ("y", "z", "x"), 0, 0), axis=0)
    hid, cov = w_in.shape[1], w_in.shape[0]
    rows_in = cov // devices
    in_rows = 2 * rows_in * (hid // 2 // species)
    grad_w_out = pieces[in_rows:]
    halves = pieces[:in_rows].reshape(4, hid // 8 // species, 2, rows_in, species)
    mine = lax.dynamic_index_in_dim(halves, core, 2, keepdims=False)
    sent_over = other_core(lax.dynamic_index_in_dim(halves, 1 - core, 2, keepdims=False))
    first, second = jnp.where(core == 0, mine, sent_over), jnp.where(core == 0, sent_over, mine)
    grad_w_in = jnp.stack([first, second], axis=1)
    grad_w_in = grad_w_in.transpose(3, 0, 1, 2, 4).reshape(rows_in, hid)
    return (field, grad_w_in, grad_w_out)


def solution(mesh):
    tiles_y, tiles_x = mesh.devices.shape
    split = Mesh(mesh.devices.reshape(tiles_y // 2, 2, tiles_x // 4, 4), ALL)
    in_specs = (
        P(ALL, None),
        P(),
        P(),
        P(),
        P(),
        P(ALL, None),
        P(ALL),
        P(),
        P(),
        P(),
        P(),
        P(TY, TX, None),
        P(TY, TX),
    )
    out_specs = (P(TY, TX, None), P(ALL, None), P(ALL, None))
    return jax.shard_map(local, mesh=split, in_specs=in_specs, out_specs=out_specs, check_vma=False)
```

```python
import functools
import math

import jax
import jax.numpy as jnp
from jax import lax
from jax.experimental import pallas as pl
from jax.experimental.pallas import tpu as pltpu
from jax.sharding import Mesh
from jax.sharding import PartitionSpec as P

STEPS = 4
REACH = 4
CHUNK = 64
TY = ("y", "core")
TX = ("z", "x")
ALL = TY + TX
F32 = jnp.float32
BF16 = jnp.bfloat16


def normalize(taps):
    return taps / jnp.sum(taps, axis=1, keepdims=True)


def raster_body(scale, species_ref, got_ref, density_ref, grad_ref, cells, mids, codes):
    rows, across, lanes = codes.shape
    tall = grad_ref.shape[1]
    taps_y = [species_ref[0, k] for k in range(9)]
    taps_x = [species_ref[0, 9 + k] for k in range(9)]
    rate, capacity = species_ref[0, 18], species_ref[0, 19]
    for slot in range(2):
        cells[slot, 0:REACH] = jnp.zeros((REACH, across, lanes), F32)
        cells[slot, REACH + rows :] = jnp.zeros((REACH, across, lanes), F32)
    for band in range(rows // tall):
        at = band * tall
        tiles = slice(band * across, (band + 1) * across)
        start = jnp.swapaxes(got_ref[tiles, 0:tall, :].astype(F32), 0, 1)
        cells[0, REACH + at : REACH + at + tall] = 0.1 + start
        codes[at : at + tall] = jnp.swapaxes(got_ref[tiles, tall : 2 * tall, :].astype(F32), 0, 1)
    block = (CHUNK, across, lanes)
    lane = lax.broadcasted_iota(jnp.int32, block, 2)
    tile = lax.broadcasted_iota(jnp.int32, block, 1)
    from_right = (lane < REACH) & (tile < across - 1)
    from_left = (lane >= lanes - REACH) & (tile > 0)

    def spread(along_x):
        came = lax.broadcasted_iota(jnp.int32, (2 * lanes, lanes), 0)
        goes = lax.broadcasted_iota(jnp.int32, (2 * lanes, lanes), 1)
        beside = jnp.where(came < lanes + lanes // 2, came, came - 2 * lanes)
        tap = jnp.where(came < lanes, came, beside) - goes + REACH
        matrix = jnp.zeros((2 * lanes, lanes), F32)
        for k in range(9):
            matrix = jnp.where(tap == k, along_x[k], matrix)
        high = matrix.astype(BF16)
        return high, (matrix - high.astype(F32)).astype(BF16)

    def disperse(slot, at, along_y, along_x):
        total = None
        for k in range(9):
            part = along_y[k] * cells[slot, pl.ds(at + k, CHUNK)]
            total = part if total is None else total + part
        right = pltpu.roll(total, across - 1, axis=1)
        left = pltpu.roll(total, 1, axis=1)
        edge = jnp.where(from_right, right, jnp.where(from_left, left, 0.0))
        both = jnp.concatenate([total, edge], axis=2).reshape(CHUNK * across, 2 * lanes)
        high = both.astype(BF16)
        low = (both - high.astype(F32)).astype(BF16)
        result = jnp.dot(high, along_x[0], preferred_element_type=F32)
        result = result + jnp.dot(low, along_x[0], preferred_element_type=F32)
        result = result + jnp.dot(high, along_x[1], preferred_element_type=F32)
        return result.reshape(block)

    forth, back = spread(taps_x), spread(taps_x[::-1])

    def each_chunk(do):
        def step(chunk, carry):
            do(chunk * CHUNK)
            return carry

        lax.fori_loop(0, rows // CHUNK, step, 0)

    def forward_step(step, carry):
        slot = step % 2

        def do(at):
            mid = disperse(slot, at, taps_y, forth)
            mids[step, pl.ds(at, CHUNK)] = mid
            field = mid * (1.0 + rate) / (1.0 + mid * (rate / capacity))
            cells[1 - slot, pl.ds(REACH + at, CHUNK)] = field

        each_chunk(do)
        return carry

    lax.fori_loop(0, STEPS, forward_step, 0)
    last = STEPS % 2

    def grown(grad, step, at):
        denom = 1.0 + mids[step, pl.ds(at, CHUNK)] * (rate / capacity)
        return grad * (1.0 + rate) / (denom * denom)

    def loss(at):
        field = cells[last, pl.ds(REACH + at, CHUNK)]
        code = codes[pl.ds(at, CHUNK)]
        grad = jnp.where(code >= 0.0, (1.0 - code / field) * scale, 0.0)
        cells[1 - last, pl.ds(REACH + at, CHUNK)] = grown(grad, STEPS - 1, at)

    each_chunk(loss)
    for band in range(rows // tall):
        at = band * tall
        density_ref[band * across : (band + 1) * across] = jnp.swapaxes(
            cells[last, REACH + at : REACH + at + tall], 0, 1
        )

    def backward_step(step, carry):
        slot = (1 - last + step) % 2

        def do(at):
            grad = disperse(slot, at, taps_y[::-1], back)
            cells[1 - slot, pl.ds(REACH + at, CHUNK)] = grown(grad, STEPS - 2 - step, at)

        each_chunk(do)
        return carry

    lax.fori_loop(0, STEPS - 1, backward_step, 0)
    slot = (1 - last + STEPS - 1) % 2

    def final(at):
        codes[pl.ds(at, CHUNK)] = disperse(slot, at, taps_y[::-1], back)

    each_chunk(final)
    for band in range(rows // tall):
        at = band * tall
        grad_ref[band * across : (band + 1) * across] = jnp.swapaxes(
            codes[at : at + tall], 0, 1
        ).astype(BF16)


def raster(species, got, scale, tiles_y, tiles_x):
    tiles, two, lanes = got.shape
    tall = two // 2
    rows = tiles_y * tall

    def whole(shape):
        return pl.BlockSpec(shape, lambda: (0,) * len(shape))

    return pl.pallas_call(
        functools.partial(raster_body, scale),
        out_shape=[
            jax.ShapeDtypeStruct((tiles, tall, lanes), F32),
            jax.ShapeDtypeStruct((tiles, tall, lanes), BF16),
        ],
        in_specs=[pl.BlockSpec(memory_space=pltpu.SMEM), whole(got.shape)],
        out_specs=[whole((tiles, tall, lanes))] * 2,
        scratch_shapes=[
            pltpu.VMEM((2, rows + 2 * REACH, tiles_x, lanes), F32),
            pltpu.VMEM((STEPS, rows, tiles_x, lanes), F32),
            pltpu.VMEM((rows, tiles_x, lanes), F32),
        ],
        compiler_params=pltpu.CompilerParams(vmem_limit_bytes=48 << 20),
        name="raster_steps",
    )(species, got)


def forward_body(x_ref, w_in_ref, b_in_ref, w_out_ref, b_out_ref, intensity_ref):
    chunk = 512
    x = x_ref[...]
    log_rate = b_out_ref[...]
    for at in range(0, w_in_ref.shape[1], chunk):
        pre = jnp.dot(x, w_in_ref[:, at : at + chunk], preferred_element_type=F32)
        pre = pre + b_in_ref[:, at : at + chunk]
        hidden = (pre / (1.0 + jnp.exp(-pre))).astype(BF16)
        log_rate = log_rate + jnp.dot(
            hidden, w_out_ref[at : at + chunk, :], preferred_element_type=F32
        )
    intensity_ref[...] = jnp.exp(log_rate)


def forward(x, w_in, b_in, w_out, b_out, block=512):
    rows, cov = x.shape
    hid, species = w_out.shape

    def whole(shape):
        return pl.BlockSpec(shape, lambda i: (0, 0), pipeline_mode=pl.Buffered(1))

    return pl.pallas_call(
        forward_body,
        out_shape=jax.ShapeDtypeStruct((rows, species), F32),
        grid=(rows // block,),
        in_specs=[
            pl.BlockSpec((block, cov), lambda i: (i, 0)),
            whole((cov, hid)),
            whole((1, hid)),
            whole((hid, species)),
            whole((1, species)),
        ],
        out_specs=pl.BlockSpec((block, species), lambda i: (i, 0)),
        compiler_params=pltpu.CompilerParams(vmem_limit_bytes=40 << 20),
        name="land_forward",
    )(x, w_in, b_in[None, :], w_out, b_out[None, :])


def gates_body(core_ref, x_ref, w_in_ref, b_in_ref, hidden_ref, slope_ref):
    pre = jnp.dot(x_ref[...], w_in_ref[...], preferred_element_type=F32) + b_in_ref[...]
    gate = 1.0 / (1.0 + jnp.exp(-pre))
    scaled = pre * gate
    hidden_ref[...] = scaled.astype(BF16)
    slope_ref[...] = gate + scaled * (1.0 - gate)


def gates(core, x, w_in, b_in):
    n_y = 4
    rows, cov = x.shape
    hid = w_in.shape[1]
    width = hid // n_y // 2
    block = pl.BlockSpec((rows, width), lambda j, c: (0, j))
    return pl.pallas_call(
        gates_body,
        out_shape=[
            jax.ShapeDtypeStruct((rows, hid // 2), BF16),
            jax.ShapeDtypeStruct((rows, hid // 2), F32),
        ],
        grid_spec=pltpu.PrefetchScalarGridSpec(
            num_scalar_prefetch=1,
            grid=(n_y,),
            in_specs=[
                pl.BlockSpec((rows, cov), lambda j, c: (0, 0), pipeline_mode=pl.Buffered(1)),
                pl.BlockSpec((cov, width), lambda j, c: (0, 2 * j + c[0])),
                pl.BlockSpec((1, width), lambda j, c: (0, 2 * j + c[0])),
            ],
            out_specs=[block, block],
        ),
        compiler_params=pltpu.CompilerParams(vmem_limit_bytes=40 << 20),
        name="land_gates",
    )(core, x, w_in, b_in[None, :])


def backward_body(
    core_ref,
    x_own,
    x_other,
    dlog_own,
    dlog_other,
    hidden_own,
    hidden_other,
    slope_own,
    slope_other,
    w_out_ref,
    out_ref,
    in_acc,
    out_acc,
):
    j = pl.program_id(0)
    w_out = w_out_ref[...]

    def parts(x_ref, dlog_ref, hidden_ref, slope_ref):
        dlog = dlog_ref[...]
        dhidden = lax.dot_general(
            dlog, w_out, (((1,), (1,)), ((), ())), preferred_element_type=F32
        )
        dpre = (dhidden * slope_ref[...]).astype(BF16)
        rows = (((0,), (0,)), ((), ()))
        return (
            lax.dot_general(x_ref[...], dpre, rows, preferred_element_type=F32),
            lax.dot_general(hidden_ref[...], dlog, rows, preferred_element_type=F32),
        )

    in_acc[...], out_acc[...] = parts(x_own, dlog_own, hidden_own, slope_own)
    in_part, out_part = parts(x_other, dlog_other, hidden_other, slope_other)
    in_acc[...] += in_part
    out_acc[...] += out_part
    n_y = 4
    zx = out_ref.shape[0] // n_y
    tiles = in_acc.shape[1] // 128
    rows = in_acc.shape[0] // out_ref.shape[0] // 2
    units = out_acc.shape[0] // zx
    for y in range(n_y):
        for p in range(zx):
            for c in range(2):
                for k in range(tiles):
                    out_ref[
                        y * zx + p, pl.ds((j * tiles + k) * 2 * rows + c * rows, rows), :
                    ] = in_acc[
                        pl.ds((y * 2 * zx + c * zx + p) * rows, rows),
                        k * 128 : (k + 1) * 128,
                    ]
    base = 2 * rows * tiles * n_y
    for p in range(zx):
        out_ref[j * zx + p, base : base + units, :] = out_acc[p * units : (p + 1) * units, :]


def backward(core, x, dlog, hidden, slope, w_out, peers):
    n_y = 4
    rows, cov = x[0].shape
    hid, species = w_out.shape
    width = hid // n_y // 2
    send_rows = cov // peers * (hid // 2 // 128) + hid // 2 // peers

    def fixed(shape):
        return pl.BlockSpec(
            shape, lambda j, c: (0,) * len(shape), pipeline_mode=pl.Buffered(1)
        )

    grid_spec = pltpu.PrefetchScalarGridSpec(
        num_scalar_prefetch=1,
        grid=(n_y,),
        in_specs=[fixed((rows, cov))] * 2
        + [fixed((rows, species))] * 2
        + [pl.BlockSpec((rows, width), lambda j, c: (0, j))] * 4
        + [pl.BlockSpec((width, species), lambda j, c: (2 * j + c[0], 0))],
        out_specs=fixed((peers, send_rows, 128)),
        scratch_shapes=[pltpu.VMEM((cov, width), F32), pltpu.VMEM((width, species), F32)],
    )
    return pl.pallas_call(
        backward_body,
        out_shape=jax.ShapeDtypeStruct((peers, send_rows, 128), F32),
        grid_spec=grid_spec,
        compiler_params=pltpu.CompilerParams(vmem_limit_bytes=50 << 20),
        name="land_backward",
    )(core, *x, *dlog, *hidden, *slope, w_out)


def other_core(values):
    return lax.ppermute(values, "core", [(0, 1), (1, 0)])


def local(
    covariates,
    w_in,
    b_in,
    w_out,
    b_out,
    owner,
    land_cell,
    row_taps,
    col_taps,
    rate,
    capacity,
    observed,
    surveyed,
):
    row_count = covariates.shape[0]
    tiles_y = lax.axis_size("y") * lax.axis_size("core")
    tiles_x = lax.axis_size("z") * lax.axis_size("x")
    devices = tiles_y * tiles_x
    slot_count = 2 * row_count // devices
    slots = devices * slot_count
    height, tile_width, species = observed.shape
    cell_count = height * tile_width
    core = lax.axis_index("core")
    theirs = other_core(covariates)
    intensity = forward(covariates, w_in, b_in, w_out, b_out)
    sent = intensity.astype(BF16)

    owner_rows = owner[:, 0]
    owner_hot = owner_rows[:, None] == jnp.arange(devices, dtype=jnp.int32)[None, :]
    row_ids = jnp.arange(row_count, dtype=jnp.int32)
    earlier = (row_ids[None, :] < row_ids[:, None]).astype(BF16)
    before = jnp.dot(earlier, owner_hot.astype(BF16), preferred_element_type=F32)
    slot_idx = jnp.sum(jnp.where(owner_hot, before, 0.0), axis=1).astype(jnp.int32)
    flat_slot = owner_rows * slot_count + slot_idx

    slot_ids = jnp.arange(slots, dtype=jnp.int32)
    pack = (flat_slot[None, :] == slot_ids[:, None]).astype(BF16)
    send_values = jnp.dot(pack, sent, preferred_element_type=F32).astype(BF16)
    slot_hot = slot_idx[:, None] == jnp.arange(slot_count, dtype=jnp.int32)[None, :]
    place_row = (land_cell // tile_width + 1).astype(F32)[:, None]
    place_col = (land_cell % tile_width).astype(F32)[:, None]
    places = jnp.concatenate(
        [jnp.where(slot_hot, place_row, 0.0), jnp.where(slot_hot, place_col, 0.0)], axis=1
    ).astype(BF16)
    table = lax.dot_general(
        owner_hot.astype(BF16), places, (((0,), (0,)), ((), ())), preferred_element_type=F32
    ).astype(BF16)
    table = jnp.pad(table[:, None, :], ((0, 0), (0, 7), (0, species - 2 * slot_count)))
    send = jnp.concatenate([send_values.reshape(devices, slot_count, species), table], axis=1)
    got = lax.all_to_all(send, ALL, split_axis=0, concat_axis=0, tiled=True)
    send, own = lax.optimization_barrier((send, covariates))
    own_gates = gates(core[None], own, w_in, b_in)
    got, own_gates = lax.optimization_barrier((got, own_gates))
    got_values = got[:, :slot_count].reshape(slots, species)
    got_row = got[:, slot_count, :slot_count].astype(jnp.int32)
    got_col = got[:, slot_count, slot_count : 2 * slot_count].astype(jnp.int32)
    cell_list = jnp.where(got_row > 0, (got_row - 1) * tile_width + got_col, -1).reshape(-1)
    cell_ids = jnp.arange(cell_count, dtype=jnp.int32)
    place = (cell_list[None, :] == cell_ids[:, None]).astype(BF16)
    start_field = jnp.dot(place, got_values, preferred_element_type=F32)

    code = jnp.where(surveyed[:, :, None] > 0, observed, -1).astype(BF16)
    send = jnp.concatenate(
        [
            start_field.astype(BF16).T.reshape(species, height, tile_width),
            code.reshape(cell_count, species).T.reshape(species, height, tile_width),
        ],
        axis=1,
    )
    traits = jnp.concatenate(
        [normalize(row_taps), normalize(col_taps), rate[:, None], capacity[:, None]], axis=1
    )
    traits = jnp.pad(traits, ((0, 0), (0, 32 - traits.shape[1])))
    traits = lax.dynamic_slice_in_dim(traits, lax.axis_index(ALL), 1, axis=0)
    scale = 1.0 / math.sqrt(row_count * devices)
    got = lax.all_to_all(send, ALL, 0, 0, tiled=True)
    send, theirs = lax.optimization_barrier((send, theirs))
    their_gates = gates(core[None], theirs, w_in, b_in)
    got, their_gates = lax.optimization_barrier((got, their_gates))
    density, grad_start = raster(traits, got, scale, tiles_y, tiles_x)
    grad_start = lax.all_to_all(grad_start, ALL, 0, 0, tiled=True).reshape(species, cell_count)

    take = (cell_list[:, None] == cell_ids[None, :]).astype(BF16)
    back_values = lax.dot_general(
        take, grad_start, (((1,), (1,)), ((), ())), preferred_element_type=F32
    ).astype(BF16)
    home_values = lax.all_to_all(
        back_values.reshape(devices, slot_count, species),
        ALL,
        split_axis=0,
        concat_axis=0,
        tiled=True,
    )
    home_values, density = lax.optimization_barrier((home_values, density))
    density = lax.all_to_all(density, ALL, 0, 0, tiled=True)
    unpack = (flat_slot[:, None] == slot_ids[None, :]).astype(BF16)
    returned = jnp.dot(unpack, home_values.reshape(slots, species), preferred_element_type=F32)
    dlog = (returned * intensity).astype(BF16)
    peers = devices // 2
    pieces = backward(
        core[None],
        (covariates, theirs),
        (dlog, other_core(dlog)),
        (own_gates[0], their_gates[0]),
        (own_gates[1], their_gates[1]),
        w_out,
        peers,
    )
    pieces, density = lax.optimization_barrier((pieces, density))
    density = density.reshape(species, cell_count).T.reshape(height, tile_width, species)
    pieces = lax.all_to_all(pieces, ("y", "z", "x"), 0, 0)
    pieces, density = lax.optimization_barrier((pieces, density))
    pieces = jnp.sum(pieces, axis=0)
    hid, cov = w_in.shape[1], w_in.shape[0]
    rows_in = cov // devices
    in_rows = 2 * rows_in * (hid // 2 // species)
    grad_w_out = pieces[in_rows:]
    halves = pieces[:in_rows].reshape(4, hid // 8 // species, 2, rows_in, species)
    mine = lax.dynamic_index_in_dim(halves, core, 2, keepdims=False)
    sent_over = other_core(lax.dynamic_index_in_dim(halves, 1 - core, 2, keepdims=False))
    first, second = jnp.where(core == 0, mine, sent_over), jnp.where(core == 0, sent_over, mine)
    grad_w_in = jnp.stack([first, second], axis=1)
    grad_w_in = grad_w_in.transpose(3, 0, 1, 2, 4).reshape(rows_in, hid)
    return (density, grad_w_in, grad_w_out)


def solution(mesh):
    tiles_y, tiles_x = mesh.devices.shape
    split = Mesh(mesh.devices.reshape(tiles_y // 2, 2, tiles_x // 4, 4), ALL)
    in_specs = (
        P(ALL, None),
        P(),
        P(),
        P(),
        P(),
        P(ALL, None),
        P(ALL),
        P(),
        P(),
        P(),
        P(),
        P(TY, TX, None),
        P(TY, TX),
    )
    out_specs = (P(TY, TX, None), P(ALL, None), P(ALL, None))
    return jax.shard_map(local, mesh=split, in_specs=in_specs, out_specs=out_specs, check_vma=False)
```

```python
import functools
import math

import jax
import jax.numpy as jnp
from jax import lax
from jax.experimental import pallas as pl
from jax.experimental.pallas import tpu as pltpu
from jax.sharding import Mesh
from jax.sharding import PartitionSpec as P

STEPS = 4
REACH = 4
CHUNK = 64
TY = ("y", "core")
TX = ("z", "x")
ALL = TY + TX
F32 = jnp.float32
BF16 = jnp.bfloat16


def normalize(taps):
    return taps / jnp.sum(taps, axis=1, keepdims=True)


def raster_body(scale, species_ref, got_ref, density_ref, grad_ref, cells, mids, codes):
    rows, across, lanes = codes.shape
    tall = grad_ref.shape[1]
    taps_y = [species_ref[0, k] for k in range(9)]
    taps_x = [species_ref[0, 9 + k] for k in range(9)]
    rate, capacity = species_ref[0, 18], species_ref[0, 19]
    for slot in range(2):
        cells[slot, 0:REACH] = jnp.zeros((REACH, across, lanes), F32)
        cells[slot, REACH + rows :] = jnp.zeros((REACH, across, lanes), F32)
    for band in range(rows // tall):
        at = band * tall
        tiles = slice(band * across, (band + 1) * across)
        start = jnp.swapaxes(got_ref[tiles, 0:tall, :].astype(F32), 0, 1)
        cells[0, REACH + at : REACH + at + tall] = 0.1 + start
        codes[at : at + tall] = jnp.swapaxes(got_ref[tiles, tall : 2 * tall, :].astype(F32), 0, 1)
    block = (CHUNK, across, lanes)
    lane = lax.broadcasted_iota(jnp.int32, block, 2)
    tile = lax.broadcasted_iota(jnp.int32, block, 1)
    from_right = (lane < REACH) & (tile < across - 1)
    from_left = (lane >= lanes - REACH) & (tile > 0)

    def spread(along_x):
        came = lax.broadcasted_iota(jnp.int32, (2 * lanes, lanes), 0)
        goes = lax.broadcasted_iota(jnp.int32, (2 * lanes, lanes), 1)
        beside = jnp.where(came < lanes + lanes // 2, came, came - 2 * lanes)
        tap = jnp.where(came < lanes, came, beside) - goes + REACH
        matrix = jnp.zeros((2 * lanes, lanes), F32)
        for k in range(9):
            matrix = jnp.where(tap == k, along_x[k], matrix)
        high = matrix.astype(BF16)
        return high, (matrix - high.astype(F32)).astype(BF16)

    def disperse(slot, at, along_y, along_x):
        total = None
        for k in range(9):
            part = along_y[k] * cells[slot, pl.ds(at + k, CHUNK)]
            total = part if total is None else total + part
        right = pltpu.roll(total, across - 1, axis=1)
        left = pltpu.roll(total, 1, axis=1)
        edge = jnp.where(from_right, right, jnp.where(from_left, left, 0.0))
        both = jnp.concatenate([total, edge], axis=2).reshape(CHUNK * across, 2 * lanes)
        high = both.astype(BF16)
        low = (both - high.astype(F32)).astype(BF16)
        result = jnp.dot(high, along_x[0], preferred_element_type=F32)
        result = result + jnp.dot(low, along_x[0], preferred_element_type=F32)
        result = result + jnp.dot(high, along_x[1], preferred_element_type=F32)
        return result.reshape(block)

    forth, back = spread(taps_x), spread(taps_x[::-1])

    def each_chunk(do):
        def step(chunk, carry):
            do(chunk * CHUNK)
            return carry

        lax.fori_loop(0, rows // CHUNK, step, 0)

    def forward_step(step, carry):
        slot = step % 2

        def do(at):
            mid = disperse(slot, at, taps_y, forth)
            mids[step, pl.ds(at, CHUNK)] = mid
            field = mid * (1.0 + rate) / (1.0 + mid * (rate / capacity))
            cells[1 - slot, pl.ds(REACH + at, CHUNK)] = field

        each_chunk(do)
        return carry

    lax.fori_loop(0, STEPS, forward_step, 0)
    last = STEPS % 2

    def grown(grad, step, at):
        denom = 1.0 + mids[step, pl.ds(at, CHUNK)] * (rate / capacity)
        return grad * (1.0 + rate) / (denom * denom)

    def loss(at):
        field = cells[last, pl.ds(REACH + at, CHUNK)]
        code = codes[pl.ds(at, CHUNK)]
        grad = jnp.where(code >= 0.0, (1.0 - code / field) * scale, 0.0)
        cells[1 - last, pl.ds(REACH + at, CHUNK)] = grown(grad, STEPS - 1, at)

    each_chunk(loss)
    for band in range(rows // tall):
        at = band * tall
        density_ref[band * across : (band + 1) * across] = jnp.swapaxes(
            cells[last, REACH + at : REACH + at + tall], 0, 1
        )

    def backward_step(step, carry):
        slot = (1 - last + step) % 2

        def do(at):
            grad = disperse(slot, at, taps_y[::-1], back)
            cells[1 - slot, pl.ds(REACH + at, CHUNK)] = grown(grad, STEPS - 2 - step, at)

        each_chunk(do)
        return carry

    lax.fori_loop(0, STEPS - 1, backward_step, 0)
    slot = (1 - last + STEPS - 1) % 2

    def final(at):
        codes[pl.ds(at, CHUNK)] = disperse(slot, at, taps_y[::-1], back)

    each_chunk(final)
    for band in range(rows // tall):
        at = band * tall
        grad_ref[band * across : (band + 1) * across] = jnp.swapaxes(
            codes[at : at + tall], 0, 1
        ).astype(BF16)


def raster(species, got, scale, tiles_y, tiles_x):
    tiles, two, lanes = got.shape
    tall = two // 2
    rows = tiles_y * tall

    def whole(shape):
        return pl.BlockSpec(shape, lambda: (0,) * len(shape))

    return pl.pallas_call(
        functools.partial(raster_body, scale),
        out_shape=[
            jax.ShapeDtypeStruct((tiles, tall, lanes), F32),
            jax.ShapeDtypeStruct((tiles, tall, lanes), BF16),
        ],
        in_specs=[pl.BlockSpec(memory_space=pltpu.SMEM), whole(got.shape)],
        out_specs=[whole((tiles, tall, lanes))] * 2,
        scratch_shapes=[
            pltpu.VMEM((2, rows + 2 * REACH, tiles_x, lanes), F32),
            pltpu.VMEM((STEPS, rows, tiles_x, lanes), F32),
            pltpu.VMEM((rows, tiles_x, lanes), F32),
        ],
        compiler_params=pltpu.CompilerParams(vmem_limit_bytes=48 << 20),
        name="raster_steps",
    )(species, got)


def forward_body(x_ref, w_in_ref, b_in_ref, w_out_ref, b_out_ref, intensity_ref):
    chunk = 512
    x = x_ref[...]
    log_rate = b_out_ref[...]
    for at in range(0, w_in_ref.shape[1], chunk):
        pre = jnp.dot(x, w_in_ref[:, at : at + chunk], preferred_element_type=F32)
        pre = pre + b_in_ref[:, at : at + chunk]
        hidden = (pre / (1.0 + jnp.exp(-pre))).astype(BF16)
        log_rate = log_rate + jnp.dot(
            hidden, w_out_ref[at : at + chunk, :], preferred_element_type=F32
        )
    intensity_ref[...] = jnp.exp(log_rate)


def forward(x, w_in, b_in, w_out, b_out, block=512):
    rows, cov = x.shape
    hid, species = w_out.shape

    def whole(shape):
        return pl.BlockSpec(shape, lambda i: (0, 0), pipeline_mode=pl.Buffered(1))

    return pl.pallas_call(
        forward_body,
        out_shape=jax.ShapeDtypeStruct((rows, species), F32),
        grid=(rows // block,),
        in_specs=[
            pl.BlockSpec((block, cov), lambda i: (i, 0)),
            whole((cov, hid)),
            whole((1, hid)),
            whole((hid, species)),
            whole((1, species)),
        ],
        out_specs=pl.BlockSpec((block, species), lambda i: (i, 0)),
        compiler_params=pltpu.CompilerParams(vmem_limit_bytes=40 << 20),
        name="land_forward",
    )(x, w_in, b_in[None, :], w_out, b_out[None, :])


def gates_body(core_ref, x_ref, w_in_ref, b_in_ref, hidden_ref, slope_ref):
    pre = jnp.dot(x_ref[...], w_in_ref[...], preferred_element_type=F32) + b_in_ref[...]
    gate = 1.0 / (1.0 + jnp.exp(-pre))
    scaled = pre * gate
    hidden_ref[...] = scaled.astype(BF16)
    slope_ref[...] = gate + scaled * (1.0 - gate)


def gates(core, x, w_in, b_in):
    n_y = 4
    rows, cov = x.shape
    hid = w_in.shape[1]
    width = hid // n_y // 2
    block = pl.BlockSpec((rows, width), lambda j, c: (0, j))
    return pl.pallas_call(
        gates_body,
        out_shape=[
            jax.ShapeDtypeStruct((rows, hid // 2), BF16),
            jax.ShapeDtypeStruct((rows, hid // 2), F32),
        ],
        grid_spec=pltpu.PrefetchScalarGridSpec(
            num_scalar_prefetch=1,
            grid=(n_y,),
            in_specs=[
                pl.BlockSpec((rows, cov), lambda j, c: (0, 0), pipeline_mode=pl.Buffered(1)),
                pl.BlockSpec((cov, width), lambda j, c: (0, 2 * j + c[0])),
                pl.BlockSpec((1, width), lambda j, c: (0, 2 * j + c[0])),
            ],
            out_specs=[block, block],
        ),
        compiler_params=pltpu.CompilerParams(vmem_limit_bytes=40 << 20),
        name="land_gates",
    )(core, x, w_in, b_in[None, :])


def backward_body(
    core_ref,
    x_own,
    x_other,
    dlog_own,
    dlog_other,
    hidden_own,
    hidden_other,
    slope_own,
    slope_other,
    w_out_ref,
    out_ref,
    in_acc,
    out_acc,
):
    j = pl.program_id(0)
    w_out = w_out_ref[...]

    def parts(x_ref, dlog_ref, hidden_ref, slope_ref):
        dlog = dlog_ref[...]
        dhidden = lax.dot_general(
            dlog, w_out, (((1,), (1,)), ((), ())), preferred_element_type=F32
        )
        dpre = (dhidden * slope_ref[...]).astype(BF16)
        rows = (((0,), (0,)), ((), ()))
        return (
            lax.dot_general(x_ref[...], dpre, rows, preferred_element_type=F32),
            lax.dot_general(hidden_ref[...], dlog, rows, preferred_element_type=F32),
        )

    in_acc[...], out_acc[...] = parts(x_own, dlog_own, hidden_own, slope_own)
    in_part, out_part = parts(x_other, dlog_other, hidden_other, slope_other)
    in_acc[...] += in_part
    out_acc[...] += out_part
    n_y = 4
    zx = out_ref.shape[0] // n_y
    tiles = in_acc.shape[1] // 128
    rows = in_acc.shape[0] // out_ref.shape[0] // 2
    units = out_acc.shape[0] // zx
    for y in range(n_y):
        for p in range(zx):
            for c in range(2):
                for k in range(tiles):
                    out_ref[
                        y * zx + p, pl.ds((j * tiles + k) * 2 * rows + c * rows, rows), :
                    ] = in_acc[
                        pl.ds((y * 2 * zx + c * zx + p) * rows, rows),
                        k * 128 : (k + 1) * 128,
                    ]
    base = 2 * rows * tiles * n_y
    for p in range(zx):
        out_ref[j * zx + p, base : base + units, :] = out_acc[p * units : (p + 1) * units, :]


def backward(core, x, dlog, hidden, slope, w_out, peers):
    n_y = 4
    rows, cov = x[0].shape
    hid, species = w_out.shape
    width = hid // n_y // 2
    send_rows = cov // peers * (hid // 2 // 128) + hid // 2 // peers

    def fixed(shape):
        return pl.BlockSpec(
            shape, lambda j, c: (0,) * len(shape), pipeline_mode=pl.Buffered(1)
        )

    grid_spec = pltpu.PrefetchScalarGridSpec(
        num_scalar_prefetch=1,
        grid=(n_y,),
        in_specs=[fixed((rows, cov))] * 2
        + [fixed((rows, species))] * 2
        + [pl.BlockSpec((rows, width), lambda j, c: (0, j))] * 4
        + [pl.BlockSpec((width, species), lambda j, c: (2 * j + c[0], 0))],
        out_specs=fixed((peers, send_rows, 128)),
        scratch_shapes=[pltpu.VMEM((cov, width), F32), pltpu.VMEM((width, species), F32)],
    )
    return pl.pallas_call(
        backward_body,
        out_shape=jax.ShapeDtypeStruct((peers, send_rows, 128), F32),
        grid_spec=grid_spec,
        compiler_params=pltpu.CompilerParams(vmem_limit_bytes=50 << 20),
        name="land_backward",
    )(core, *x, *dlog, *hidden, *slope, w_out)


def pick_body(wide, index_ref, table_ref, *refs):
    index = index_ref[...]
    out_ref = refs[-1]
    lanes = out_ref.shape[1]
    if wide:
        keys = table_ref.shape[1] // 2
        table = jnp.concatenate([table_ref[:, :keys], table_ref[:, keys:]], axis=0)
        dims = (((1,), (1,)), ((), ()))
    else:
        keys = table_ref.shape[0] // 2
        table = jnp.concatenate([table_ref[:keys, :], table_ref[keys:, :]], axis=1)
        dims = (((1,), (0,)), ((), ()))
    upper = index >= keys
    key = jnp.where(upper, index - keys, index)
    ids = lax.broadcasted_iota(jnp.int32, (index.shape[0], keys), 1)
    hot = jnp.where(ids == key, 1.0, 0.0).astype(BF16)
    both = lax.dot_general(hot, table, dims, preferred_element_type=F32)
    picked = jnp.where(upper, both[:, lanes:], both[:, :lanes])
    if len(refs) > 1:
        picked = picked * refs[0][...]
    out_ref[...] = picked.astype(BF16)


def pick(index, table, factors=None, wide=False, block=512):
    rows = index.shape[0]
    lanes = table.shape[0] if wide else table.shape[1]
    block_spec = pl.BlockSpec((block, lanes), lambda i: (i, 0))
    more = () if factors is None else (factors,)
    return pl.pallas_call(
        functools.partial(pick_body, wide),
        out_shape=jax.ShapeDtypeStruct((rows, lanes), BF16),
        grid=(rows // block,),
        in_specs=[
            pl.BlockSpec((block, 1), lambda i: (i, 0)),
            pl.BlockSpec(table.shape, lambda i: (0, 0), pipeline_mode=pl.Buffered(1)),
        ]
        + [block_spec] * len(more),
        out_specs=block_spec,
        compiler_params=pltpu.CompilerParams(vmem_limit_bytes=40 << 20),
        name="pick_rows",
    )(index[:, None], table, *more)


def other_core(values):
    return lax.ppermute(values, "core", [(0, 1), (1, 0)])


def local(
    covariates,
    w_in,
    b_in,
    w_out,
    b_out,
    owner,
    land_cell,
    row_taps,
    col_taps,
    rate,
    capacity,
    observed,
    surveyed,
):
    row_count = covariates.shape[0]
    tiles_y = lax.axis_size("y") * lax.axis_size("core")
    tiles_x = lax.axis_size("z") * lax.axis_size("x")
    devices = tiles_y * tiles_x
    slot_count = 2 * row_count // devices
    slots = devices * slot_count
    height, tile_width, species = observed.shape
    cell_count = height * tile_width
    core = lax.axis_index("core")
    theirs = other_core(covariates)
    intensity = forward(covariates, w_in, b_in, w_out, b_out)

    owner_rows = owner[:, 0]
    owner_hot = owner_rows[:, None] == jnp.arange(devices, dtype=jnp.int32)[None, :]
    row_ids = jnp.arange(row_count, dtype=jnp.int32)
    earlier = (row_ids[None, :] < row_ids[:, None]).astype(BF16)
    before = jnp.dot(earlier, owner_hot.astype(BF16), preferred_element_type=F32)
    slot_idx = jnp.sum(jnp.where(owner_hot, before, 0.0), axis=1).astype(jnp.int32)
    flat_slot = owner_rows * slot_count + slot_idx

    upper = flat_slot >= slots // 2
    slot_ids = jnp.arange(slots // 2, dtype=jnp.int32)
    slot_key = jnp.where(upper, flat_slot - slots // 2, flat_slot)
    pack = (slot_key[None, :] == slot_ids[:, None]).astype(BF16)
    halves = jnp.concatenate(
        [jnp.where(upper[:, None], 0.0, intensity), jnp.where(upper[:, None], intensity, 0.0)],
        axis=1,
    ).astype(BF16)
    packed = jnp.dot(pack, halves, preferred_element_type=F32).astype(BF16)
    send_values = jnp.concatenate([packed[:, :species], packed[:, species:]])
    slot_hot = jnp.arange(slot_count, dtype=jnp.int32)[:, None] == slot_idx[None, :]
    place_row = (land_cell // tile_width + 1).astype(F32)[None, :]
    place_col = (land_cell % tile_width).astype(F32)[None, :]
    places = jnp.concatenate(
        [jnp.where(slot_hot, place_row, 0.0), jnp.where(slot_hot, place_col, 0.0)], axis=0
    ).astype(BF16)
    table = jnp.dot(places, owner_hot.astype(BF16), preferred_element_type=F32).astype(BF16).T
    table = jnp.pad(table[:, None, :], ((0, 0), (0, 7), (0, species - 2 * slot_count)))
    send = jnp.concatenate([send_values.reshape(devices, slot_count, species), table], axis=1)
    got = lax.all_to_all(send, ALL, split_axis=0, concat_axis=0, tiled=True)
    send, own = lax.optimization_barrier((send, covariates))
    own_gates = gates(core[None], own, w_in, b_in)
    got, own_gates = lax.optimization_barrier((got, own_gates))
    got_values = got[:, :slot_count].reshape(slots, species)
    got_row = got[:, slot_count, :slot_count].astype(jnp.int32)
    got_col = got[:, slot_count, slot_count : 2 * slot_count].astype(jnp.int32)
    cell_list = jnp.where(got_row > 0, (got_row - 1) * tile_width + got_col, -1).reshape(-1)
    cell_ids = jnp.arange(cell_count, dtype=jnp.int32)
    place = (cell_list[None, :] == cell_ids[:, None]).astype(BF16)
    start_field = jnp.dot(place, got_values, preferred_element_type=F32)

    code = jnp.where(surveyed[:, :, None] > 0, observed, -1).astype(BF16)
    send = jnp.concatenate(
        [
            start_field.astype(BF16).T.reshape(species, height, tile_width),
            code.reshape(cell_count, species).T.reshape(species, height, tile_width),
        ],
        axis=1,
    )
    traits = jnp.concatenate(
        [normalize(row_taps), normalize(col_taps), rate[:, None], capacity[:, None]], axis=1
    )
    traits = jnp.pad(traits, ((0, 0), (0, 32 - traits.shape[1])))
    traits = lax.dynamic_slice_in_dim(traits, lax.axis_index(ALL), 1, axis=0)
    scale = 1.0 / math.sqrt(row_count * devices)
    got = lax.all_to_all(send, ALL, 0, 0, tiled=True)
    send, theirs = lax.optimization_barrier((send, theirs))
    their_gates = gates(core[None], theirs, w_in, b_in)
    got, their_gates = lax.optimization_barrier((got, their_gates))
    density, grad_start = raster(traits, got, scale, tiles_y, tiles_x)
    grad_start = lax.all_to_all(grad_start, ALL, 0, 0, tiled=True).reshape(species, cell_count)

    back_values = pick(cell_list, grad_start, wide=True)
    home_values = lax.all_to_all(
        back_values.reshape(devices, slot_count, species),
        ALL,
        split_axis=0,
        concat_axis=0,
        tiled=True,
    )
    home_values, density = lax.optimization_barrier((home_values, density))
    density = lax.all_to_all(density, ALL, 0, 0, tiled=True)
    dlog = pick(flat_slot, home_values.reshape(slots, species), intensity)
    peers = devices // 2
    pieces = backward(
        core[None],
        (covariates, theirs),
        (dlog, other_core(dlog)),
        (own_gates[0], their_gates[0]),
        (own_gates[1], their_gates[1]),
        w_out,
        peers,
    )
    pieces, density = lax.optimization_barrier((pieces, density))
    density = density.reshape(species, cell_count).T.reshape(height, tile_width, species)
    pieces = lax.all_to_all(pieces, ("y", "z", "x"), 0, 0)
    pieces, density = lax.optimization_barrier((pieces, density))
    pieces = jnp.sum(pieces, axis=0)
    hid, cov = w_in.shape[1], w_in.shape[0]
    rows_in = cov // devices
    in_rows = 2 * rows_in * (hid // 2 // species)
    grad_w_out = pieces[in_rows:]
    halves = pieces[:in_rows].reshape(4, hid // 8 // species, 2, rows_in, species)
    mine = lax.dynamic_index_in_dim(halves, core, 2, keepdims=False)
    sent_over = other_core(lax.dynamic_index_in_dim(halves, 1 - core, 2, keepdims=False))
    first, second = jnp.where(core == 0, mine, sent_over), jnp.where(core == 0, sent_over, mine)
    grad_w_in = jnp.stack([first, second], axis=1)
    grad_w_in = grad_w_in.transpose(3, 0, 1, 2, 4).reshape(rows_in, hid)
    return (density, grad_w_in, grad_w_out)


def solution(mesh):
    tiles_y, tiles_x = mesh.devices.shape
    split = Mesh(mesh.devices.reshape(tiles_y // 2, 2, tiles_x // 4, 4), ALL)
    in_specs = (
        P(ALL, None),
        P(),
        P(),
        P(),
        P(),
        P(ALL, None),
        P(ALL),
        P(),
        P(),
        P(),
        P(),
        P(TY, TX, None),
        P(TY, TX),
    )
    out_specs = (P(TY, TX, None), P(ALL, None), P(ALL, None))
    return jax.shard_map(local, mesh=split, in_specs=in_specs, out_specs=out_specs, check_vma=False)
```

```python
import functools
import math

import jax
import jax.numpy as jnp
from jax import lax
from jax.experimental import pallas as pl
from jax.experimental.pallas import tpu as pltpu
from jax.sharding import Mesh
from jax.sharding import PartitionSpec as P

STEPS = 4
REACH = 4
CHUNK = 64
TY = ("y", "core")
TX = ("z", "x")
ALL = TY + TX
F32 = jnp.float32
BF16 = jnp.bfloat16


def normalize(taps):
    return taps / jnp.sum(taps, axis=1, keepdims=True)


def raster_body(scale, species_ref, got_ref, density_ref, grad_ref, cells, mids, codes):
    rows, across, lanes = codes.shape
    tall = grad_ref.shape[1]
    taps_y = [species_ref[0, k] for k in range(9)]
    taps_x = [species_ref[0, 9 + k] for k in range(9)]
    rate, capacity = species_ref[0, 18], species_ref[0, 19]
    for slot in range(2):
        cells[slot, 0:REACH] = jnp.zeros((REACH, across, lanes), F32)
        cells[slot, REACH + rows :] = jnp.zeros((REACH, across, lanes), F32)
    for band in range(rows // tall):
        at = band * tall
        tiles = slice(band * across, (band + 1) * across)
        start = jnp.swapaxes(got_ref[tiles, 0:tall, :].astype(F32), 0, 1)
        cells[0, REACH + at : REACH + at + tall] = 0.1 + start
        codes[at : at + tall] = jnp.swapaxes(got_ref[tiles, tall : 2 * tall, :].astype(F32), 0, 1)
    block = (CHUNK, across, lanes)
    lane = lax.broadcasted_iota(jnp.int32, block, 2)
    tile = lax.broadcasted_iota(jnp.int32, block, 1)
    from_right = (lane < REACH) & (tile < across - 1)
    from_left = (lane >= lanes - REACH) & (tile > 0)

    def spread(along_x):
        came = lax.broadcasted_iota(jnp.int32, (2 * lanes, lanes), 0)
        goes = lax.broadcasted_iota(jnp.int32, (2 * lanes, lanes), 1)
        beside = jnp.where(came < lanes + lanes // 2, came, came - 2 * lanes)
        tap = jnp.where(came < lanes, came, beside) - goes + REACH
        matrix = jnp.zeros((2 * lanes, lanes), F32)
        for k in range(9):
            matrix = jnp.where(tap == k, along_x[k], matrix)
        high = matrix.astype(BF16)
        return high, (matrix - high.astype(F32)).astype(BF16)

    def disperse(slot, at, along_y, along_x):
        total = None
        for k in range(9):
            part = along_y[k] * cells[slot, pl.ds(at + k, CHUNK)]
            total = part if total is None else total + part
        right = pltpu.roll(total, across - 1, axis=1)
        left = pltpu.roll(total, 1, axis=1)
        edge = jnp.where(from_right, right, jnp.where(from_left, left, 0.0))
        both = jnp.concatenate([total, edge], axis=2).reshape(CHUNK * across, 2 * lanes)
        high = both.astype(BF16)
        low = (both - high.astype(F32)).astype(BF16)
        result = jnp.dot(high, along_x[0], preferred_element_type=F32)
        result = result + jnp.dot(low, along_x[0], preferred_element_type=F32)
        result = result + jnp.dot(high, along_x[1], preferred_element_type=F32)
        return result.reshape(block)

    forth, back = spread(taps_x), spread(taps_x[::-1])

    def each_chunk(do):
        def step(chunk, carry):
            do(chunk * CHUNK)
            return carry

        lax.fori_loop(0, rows // CHUNK, step, 0)

    def forward_step(step, carry):
        slot = step % 2

        def do(at):
            mid = disperse(slot, at, taps_y, forth)
            mids[step, pl.ds(at, CHUNK)] = mid
            field = mid * (1.0 + rate) / (1.0 + mid * (rate / capacity))
            cells[1 - slot, pl.ds(REACH + at, CHUNK)] = field

        each_chunk(do)
        return carry

    lax.fori_loop(0, STEPS, forward_step, 0)
    last = STEPS % 2

    def grown(grad, step, at):
        denom = 1.0 + mids[step, pl.ds(at, CHUNK)] * (rate / capacity)
        return grad * (1.0 + rate) / (denom * denom)

    def loss(at):
        field = cells[last, pl.ds(REACH + at, CHUNK)]
        code = codes[pl.ds(at, CHUNK)]
        grad = jnp.where(code >= 0.0, (1.0 - code / field) * scale, 0.0)
        cells[1 - last, pl.ds(REACH + at, CHUNK)] = grown(grad, STEPS - 1, at)

    each_chunk(loss)
    for band in range(rows // tall):
        at = band * tall
        density_ref[band * across : (band + 1) * across] = jnp.swapaxes(
            cells[last, REACH + at : REACH + at + tall], 0, 1
        )

    def backward_step(step, carry):
        slot = (1 - last + step) % 2

        def do(at):
            grad = disperse(slot, at, taps_y[::-1], back)
            cells[1 - slot, pl.ds(REACH + at, CHUNK)] = grown(grad, STEPS - 2 - step, at)

        each_chunk(do)
        return carry

    lax.fori_loop(0, STEPS - 1, backward_step, 0)
    slot = (1 - last + STEPS - 1) % 2

    def final(at):
        codes[pl.ds(at, CHUNK)] = disperse(slot, at, taps_y[::-1], back)

    each_chunk(final)
    for band in range(rows // tall):
        at = band * tall
        grad_ref[band * across : (band + 1) * across] = jnp.swapaxes(
            codes[at : at + tall], 0, 1
        ).astype(BF16)


def raster(species, got, scale, tiles_y, tiles_x):
    tiles, two, lanes = got.shape
    tall = two // 2
    rows = tiles_y * tall

    def whole(shape):
        return pl.BlockSpec(shape, lambda: (0,) * len(shape))

    return pl.pallas_call(
        functools.partial(raster_body, scale),
        out_shape=[
            jax.ShapeDtypeStruct((tiles, tall, lanes), F32),
            jax.ShapeDtypeStruct((tiles, tall, lanes), BF16),
        ],
        in_specs=[pl.BlockSpec(memory_space=pltpu.SMEM), whole(got.shape)],
        out_specs=[whole((tiles, tall, lanes))] * 2,
        scratch_shapes=[
            pltpu.VMEM((2, rows + 2 * REACH, tiles_x, lanes), F32),
            pltpu.VMEM((STEPS, rows, tiles_x, lanes), F32),
            pltpu.VMEM((rows, tiles_x, lanes), F32),
        ],
        compiler_params=pltpu.CompilerParams(vmem_limit_bytes=48 << 20),
        name="raster_steps",
    )(species, got)


def forward_body(x_ref, w_in_ref, b_in_ref, w_out_ref, b_out_ref, intensity_ref):
    chunk = 512
    x = x_ref[...]
    log_rate = b_out_ref[...]
    for at in range(0, w_in_ref.shape[1], chunk):
        pre = jnp.dot(x, w_in_ref[:, at : at + chunk], preferred_element_type=F32)
        pre = pre + b_in_ref[:, at : at + chunk]
        hidden = (pre / (1.0 + jnp.exp(-pre))).astype(BF16)
        log_rate = log_rate + jnp.dot(
            hidden, w_out_ref[at : at + chunk, :], preferred_element_type=F32
        )
    intensity_ref[...] = jnp.exp(log_rate)


def forward(x, w_in, b_in, w_out, b_out, block=512):
    rows, cov = x.shape
    hid, species = w_out.shape

    def whole(shape):
        return pl.BlockSpec(shape, lambda i: (0, 0), pipeline_mode=pl.Buffered(1))

    return pl.pallas_call(
        forward_body,
        out_shape=jax.ShapeDtypeStruct((rows, species), F32),
        grid=(rows // block,),
        in_specs=[
            pl.BlockSpec((block, cov), lambda i: (i, 0)),
            whole((cov, hid)),
            whole((1, hid)),
            whole((hid, species)),
            whole((1, species)),
        ],
        out_specs=pl.BlockSpec((block, species), lambda i: (i, 0)),
        compiler_params=pltpu.CompilerParams(vmem_limit_bytes=40 << 20),
        name="land_forward",
    )(x, w_in, b_in[None, :], w_out, b_out[None, :])


def gates_body(core_ref, x_ref, w_in_ref, b_in_ref, hidden_ref, slope_ref):
    pre = jnp.dot(x_ref[...], w_in_ref[...], preferred_element_type=F32) + b_in_ref[...]
    gate = 1.0 / (1.0 + jnp.exp(-pre))
    scaled = pre * gate
    hidden_ref[...] = scaled.astype(BF16)
    slope_ref[...] = gate + scaled * (1.0 - gate)


def gates(core, x, w_in, b_in):
    n_y = 4
    rows, cov = x.shape
    hid = w_in.shape[1]
    width = hid // n_y // 2
    block = pl.BlockSpec((rows, width), lambda j, c: (0, j))
    return pl.pallas_call(
        gates_body,
        out_shape=[
            jax.ShapeDtypeStruct((rows, hid // 2), BF16),
            jax.ShapeDtypeStruct((rows, hid // 2), F32),
        ],
        grid_spec=pltpu.PrefetchScalarGridSpec(
            num_scalar_prefetch=1,
            grid=(n_y,),
            in_specs=[
                pl.BlockSpec((rows, cov), lambda j, c: (0, 0), pipeline_mode=pl.Buffered(1)),
                pl.BlockSpec((cov, width), lambda j, c: (0, 2 * j + c[0])),
                pl.BlockSpec((1, width), lambda j, c: (0, 2 * j + c[0])),
            ],
            out_specs=[block, block],
        ),
        compiler_params=pltpu.CompilerParams(vmem_limit_bytes=40 << 20),
        name="land_gates",
    )(core, x, w_in, b_in[None, :])


def backward_body(
    core_ref,
    x_own,
    x_other,
    dlog_own,
    dlog_other,
    hidden_own,
    hidden_other,
    slope_own,
    slope_other,
    w_out_ref,
    out_ref,
    in_acc,
    out_acc,
):
    j = pl.program_id(0)
    w_out = w_out_ref[...]

    def parts(x_ref, dlog_ref, hidden_ref, slope_ref):
        dlog = dlog_ref[...]
        dhidden = lax.dot_general(
            dlog, w_out, (((1,), (1,)), ((), ())), preferred_element_type=F32
        )
        dpre = (dhidden * slope_ref[...]).astype(BF16)
        rows = (((0,), (0,)), ((), ()))
        return (
            lax.dot_general(x_ref[...], dpre, rows, preferred_element_type=F32),
            lax.dot_general(hidden_ref[...], dlog, rows, preferred_element_type=F32),
        )

    in_acc[...], out_acc[...] = parts(x_own, dlog_own, hidden_own, slope_own)
    in_part, out_part = parts(x_other, dlog_other, hidden_other, slope_other)
    in_acc[...] += in_part
    out_acc[...] += out_part
    n_y = 4
    zx = out_ref.shape[0] // n_y
    tiles = in_acc.shape[1] // 128
    rows = in_acc.shape[0] // out_ref.shape[0] // 2
    units = out_acc.shape[0] // zx
    for y in range(n_y):
        for p in range(zx):
            for c in range(2):
                for k in range(tiles):
                    out_ref[
                        y * zx + p, pl.ds((j * tiles + k) * 2 * rows + c * rows, rows), :
                    ] = in_acc[
                        pl.ds((y * 2 * zx + c * zx + p) * rows, rows),
                        k * 128 : (k + 1) * 128,
                    ]
    base = 2 * rows * tiles * n_y
    for p in range(zx):
        out_ref[j * zx + p, base : base + units, :] = out_acc[p * units : (p + 1) * units, :]


def backward(core, x, dlog, hidden, slope, w_out, peers):
    n_y = 4
    rows, cov = x[0].shape
    hid, species = w_out.shape
    width = hid // n_y // 2
    send_rows = cov // peers * (hid // 2 // 128) + hid // 2 // peers

    def fixed(shape):
        return pl.BlockSpec(
            shape, lambda j, c: (0,) * len(shape), pipeline_mode=pl.Buffered(1)
        )

    grid_spec = pltpu.PrefetchScalarGridSpec(
        num_scalar_prefetch=1,
        grid=(n_y,),
        in_specs=[fixed((rows, cov))] * 2
        + [fixed((rows, species))] * 2
        + [pl.BlockSpec((rows, width), lambda j, c: (0, j))] * 4
        + [pl.BlockSpec((width, species), lambda j, c: (2 * j + c[0], 0))],
        out_specs=fixed((peers, send_rows, 128)),
        scratch_shapes=[pltpu.VMEM((cov, width), F32), pltpu.VMEM((width, species), F32)],
    )
    return pl.pallas_call(
        backward_body,
        out_shape=jax.ShapeDtypeStruct((peers, send_rows, 128), F32),
        grid_spec=grid_spec,
        compiler_params=pltpu.CompilerParams(vmem_limit_bytes=50 << 20),
        name="land_backward",
    )(core, *x, *dlog, *hidden, *slope, w_out)


def place_body(slot_count, got_ref, code_ref, out_ref, total):
    sources, _, species = got_ref.shape
    tall, wide = code_ref.shape[1:]
    half = tall // 2
    keys = half * wide
    group = 4
    values = jnp.swapaxes(got_ref[:, :slot_count, :].astype(F32), 0, 1).astype(BF16)
    spots = got_ref[:, slot_count : slot_count + 8, :].astype(F32)[:, 0, :]
    along = spots.T
    ids = lax.broadcasted_iota(jnp.int32, (keys, sources), 0)
    for first in range(0, slot_count, group):
        hots, rows = [], []
        for slot in range(first, first + group):
            row = along[slot : slot + 1, :].astype(jnp.int32) - 1
            col = along[slot_count + slot : slot_count + slot + 1, :].astype(jnp.int32)
            cell = row * wide + col
            key = jnp.where(row >= half, cell - keys, cell)
            hots.append(jnp.where(ids == key, 1.0, 0.0).astype(BF16))
            upper = spots[:, slot : slot + 1] > half
            value = values[slot].astype(F32)
            rows.append(
                jnp.concatenate(
                    [jnp.where(upper, 0.0, value), jnp.where(upper, value, 0.0)], axis=1
                ).astype(BF16)
            )
        part = jnp.dot(
            jnp.concatenate(hots, axis=1),
            jnp.concatenate(rows, axis=0),
            preferred_element_type=F32,
        )
        if first == 0:
            total[...] = part
        else:
            total[...] += part
    lines = [
        total[
            r % half * wide : (r % half + 1) * wide,
            r // half * species : (r // half + 1) * species,
        ].T
        for r in range(tall)
    ]
    out_ref[:, :tall, :] = jnp.swapaxes(jnp.stack(lines), 0, 1).astype(BF16)
    out_ref[:, tall:, :] = code_ref[...]


def place(got, code, slot_count):
    _, tall, wide = code.shape
    species = got.shape[2]

    def whole(shape):
        return pl.BlockSpec(shape, lambda: (0,) * len(shape))

    return pl.pallas_call(
        functools.partial(place_body, slot_count),
        out_shape=jax.ShapeDtypeStruct((species, 2 * tall, wide), BF16),
        in_specs=[whole(got.shape), whole(code.shape)],
        out_specs=whole((species, 2 * tall, wide)),
        scratch_shapes=[pltpu.VMEM((tall * wide // 2, 2 * species), F32)],
        compiler_params=pltpu.CompilerParams(vmem_limit_bytes=40 << 20),
        name="place_cells",
    )(got, code)


def pick_body(wide, index_ref, table_ref, *refs):
    out_ref = refs[-1]
    rows, lanes = out_ref.shape
    index = index_ref[...]
    if index.shape[1] != 1:
        index = jnp.broadcast_to(index, (8, rows)).T[:, :1]
    if wide:
        keys = table_ref.shape[1] // 2
        table = jnp.concatenate([table_ref[:, :keys], table_ref[:, keys:]], axis=0)
        dims = (((1,), (1,)), ((), ()))
    else:
        keys = table_ref.shape[0] // 2
        table = jnp.concatenate([table_ref[:keys, :], table_ref[keys:, :]], axis=1)
        dims = (((1,), (0,)), ((), ()))
    upper = index >= keys
    key = jnp.where(upper, index - keys, index)
    ids = lax.broadcasted_iota(jnp.int32, (index.shape[0], keys), 1)
    hot = jnp.where(ids == key, 1.0, 0.0).astype(BF16)
    both = lax.dot_general(hot, table, dims, preferred_element_type=F32)
    picked = jnp.where(upper, both[:, lanes:], both[:, :lanes])
    if len(refs) > 1:
        picked = picked * refs[0][...]
    out_ref[...] = picked.astype(BF16)


def pick(index, table, factors=None, wide=False, block=512):
    rows = index.size
    column = index.shape[1] == 1
    lanes = table.shape[0] if wide else table.shape[1]
    block_spec = pl.BlockSpec((block, lanes), lambda i: (i, 0))
    more = () if factors is None else (factors,)
    return pl.pallas_call(
        functools.partial(pick_body, wide),
        out_shape=jax.ShapeDtypeStruct((rows, lanes), BF16),
        grid=(rows // block,),
        in_specs=[
            pl.BlockSpec((block, 1), lambda i: (i, 0))
            if column
            else pl.BlockSpec((1, block), lambda i: (0, i)),
            pl.BlockSpec(table.shape, lambda i: (0, 0), pipeline_mode=pl.Buffered(1)),
        ]
        + [block_spec] * len(more),
        out_specs=block_spec,
        compiler_params=pltpu.CompilerParams(vmem_limit_bytes=40 << 20),
        name="pick_rows",
    )(index, table, *more)


def other_core(values):
    return lax.ppermute(values, "core", [(0, 1), (1, 0)])


def local(
    covariates,
    w_in,
    b_in,
    w_out,
    b_out,
    owner,
    land_cell,
    row_taps,
    col_taps,
    rate,
    capacity,
    observed,
    surveyed,
):
    row_count = covariates.shape[0]
    tiles_y = lax.axis_size("y") * lax.axis_size("core")
    tiles_x = lax.axis_size("z") * lax.axis_size("x")
    devices = tiles_y * tiles_x
    slot_count = 2 * row_count // devices
    slots = devices * slot_count
    height, tile_width, species = observed.shape
    cell_count = height * tile_width
    core = lax.axis_index("core")
    theirs = other_core(covariates)
    intensity = forward(covariates, w_in, b_in, w_out, b_out)

    owner_rows = owner[:, 0]
    owner_hot = owner_rows[:, None] == jnp.arange(devices, dtype=jnp.int32)[None, :]
    row_ids = jnp.arange(row_count, dtype=jnp.int32)
    earlier = (row_ids[None, :] < row_ids[:, None]).astype(BF16)
    before = jnp.dot(earlier, owner_hot.astype(BF16), preferred_element_type=F32)
    slot_idx = jnp.sum(jnp.where(owner_hot, before, 0.0), axis=1).astype(jnp.int32)
    flat_slot = owner_rows * slot_count + slot_idx

    upper = flat_slot >= slots // 2
    slot_ids = jnp.arange(slots // 2, dtype=jnp.int32)
    slot_key = jnp.where(upper, flat_slot - slots // 2, flat_slot)
    pack = (slot_key[None, :] == slot_ids[:, None]).astype(BF16)
    halves = jnp.concatenate(
        [jnp.where(upper[:, None], 0.0, intensity), jnp.where(upper[:, None], intensity, 0.0)],
        axis=1,
    ).astype(BF16)
    packed = jnp.dot(pack, halves, preferred_element_type=F32).astype(BF16)
    send_values = jnp.concatenate([packed[:, :species], packed[:, species:]])
    slot_hot = jnp.arange(slot_count, dtype=jnp.int32)[:, None] == slot_idx[None, :]
    place_row = (land_cell // tile_width + 1).astype(F32)[None, :]
    place_col = (land_cell % tile_width).astype(F32)[None, :]
    places = jnp.concatenate(
        [jnp.where(slot_hot, place_row, 0.0), jnp.where(slot_hot, place_col, 0.0)], axis=0
    ).astype(BF16)
    table = jnp.dot(places, owner_hot.astype(BF16), preferred_element_type=F32).astype(BF16).T
    table = jnp.pad(table[:, None, :], ((0, 0), (0, 7), (0, species - 2 * slot_count)))
    send = jnp.concatenate([send_values.reshape(devices, slot_count, species), table], axis=1)
    got = lax.all_to_all(send, ALL, split_axis=0, concat_axis=0, tiled=True)
    send, own = lax.optimization_barrier((send, covariates))
    own_gates = gates(core[None], own, w_in, b_in)
    got, own_gates = lax.optimization_barrier((got, own_gates))
    got_row = got[:, slot_count, :slot_count].astype(jnp.int32)
    got_col = got[:, slot_count, slot_count : 2 * slot_count].astype(jnp.int32)
    cell_list = jnp.where(got_row > 0, (got_row - 1) * tile_width + got_col, -1).reshape(-1)

    code = jnp.where(surveyed[:, :, None] > 0, observed, -1).astype(BF16)
    code = code.reshape(cell_count, species).T.reshape(species, height, tile_width)
    send = place(got, code, slot_count)
    traits = jnp.concatenate(
        [normalize(row_taps), normalize(col_taps), rate[:, None], capacity[:, None]], axis=1
    )
    traits = jnp.pad(traits, ((0, 0), (0, 32 - traits.shape[1])))
    traits = lax.dynamic_slice_in_dim(traits, lax.axis_index(ALL), 1, axis=0)
    scale = 1.0 / math.sqrt(row_count * devices)
    got = lax.all_to_all(send, ALL, 0, 0, tiled=True)
    send, theirs = lax.optimization_barrier((send, theirs))
    their_gates = gates(core[None], theirs, w_in, b_in)
    got, their_gates = lax.optimization_barrier((got, their_gates))
    density, grad_start = raster(traits, got, scale, tiles_y, tiles_x)
    grad_start = lax.all_to_all(grad_start, ALL, 0, 0, tiled=True).reshape(species, cell_count)

    back_values = pick(cell_list[:, None], grad_start, wide=True)
    home_values = lax.all_to_all(
        back_values.reshape(devices, slot_count, species),
        ALL,
        split_axis=0,
        concat_axis=0,
        tiled=True,
    )
    home_values, density = lax.optimization_barrier((home_values, density))
    density = lax.all_to_all(density, ALL, 0, 0, tiled=True)
    dlog = pick(flat_slot[None, :], home_values.reshape(slots, species), intensity)
    peers = devices // 2
    pieces = backward(
        core[None],
        (covariates, theirs),
        (dlog, other_core(dlog)),
        (own_gates[0], their_gates[0]),
        (own_gates[1], their_gates[1]),
        w_out,
        peers,
    )
    pieces, density = lax.optimization_barrier((pieces, density))
    density = density.reshape(species, cell_count).T.reshape(height, tile_width, species)
    pieces = lax.all_to_all(pieces, ("y", "z", "x"), 0, 0)
    pieces, density = lax.optimization_barrier((pieces, density))
    pieces = jnp.sum(pieces, axis=0)
    hid, cov = w_in.shape[1], w_in.shape[0]
    rows_in = cov // devices
    in_rows = 2 * rows_in * (hid // 2 // species)
    grad_w_out = pieces[in_rows:]
    halves = pieces[:in_rows].reshape(4, hid // 8 // species, 2, rows_in, species)
    mine = lax.dynamic_index_in_dim(halves, core, 2, keepdims=False)
    sent_over = other_core(lax.dynamic_index_in_dim(halves, 1 - core, 2, keepdims=False))
    first, second = jnp.where(core == 0, mine, sent_over), jnp.where(core == 0, sent_over, mine)
    grad_w_in = jnp.stack([first, second], axis=1)
    grad_w_in = grad_w_in.transpose(3, 0, 1, 2, 4).reshape(rows_in, hid)
    return (density, grad_w_in, grad_w_out)


def solution(mesh):
    tiles_y, tiles_x = mesh.devices.shape
    split = Mesh(mesh.devices.reshape(tiles_y // 2, 2, tiles_x // 4, 4), ALL)
    in_specs = (
        P(ALL, None),
        P(),
        P(),
        P(),
        P(),
        P(ALL, None),
        P(ALL),
        P(),
        P(),
        P(),
        P(),
        P(TY, TX, None),
        P(TY, TX),
    )
    out_specs = (P(TY, TX, None), P(ALL, None), P(ALL, None))
    return jax.shard_map(local, mesh=split, in_specs=in_specs, out_specs=out_specs, check_vma=False)
```

```python
import functools
import math

import jax
import jax.numpy as jnp
from jax import lax
from jax.experimental import pallas as pl
from jax.experimental.pallas import tpu as pltpu
from jax.sharding import Mesh
from jax.sharding import PartitionSpec as P

STEPS = 4
REACH = 4
CHUNK = 64
TY = ("y", "core")
TX = ("z", "x")
ALL = TY + TX
F32 = jnp.float32
BF16 = jnp.bfloat16


def normalize(taps):
    return taps / jnp.sum(taps, axis=1, keepdims=True)


def raster_body(scale, species_ref, got_ref, density_ref, grad_ref, cells, mids, codes):
    rows, across, lanes = codes.shape
    tall = grad_ref.shape[1]
    taps_y = [species_ref[0, k] for k in range(9)]
    taps_x = [species_ref[0, 9 + k] for k in range(9)]
    rate, capacity = species_ref[0, 18], species_ref[0, 19]
    for slot in range(2):
        cells[slot, 0:REACH] = jnp.zeros((REACH, across, lanes), F32)
        cells[slot, REACH + rows :] = jnp.zeros((REACH, across, lanes), F32)
    for band in range(rows // tall):
        at = band * tall
        tiles = slice(band * across, (band + 1) * across)
        start = jnp.swapaxes(got_ref[tiles, 0:tall, :].astype(F32), 0, 1)
        cells[0, REACH + at : REACH + at + tall] = 0.1 + start
        codes[at : at + tall] = jnp.swapaxes(got_ref[tiles, tall : 2 * tall, :].astype(F32), 0, 1)
    block = (CHUNK, across, lanes)
    lane = lax.broadcasted_iota(jnp.int32, block, 2)
    tile = lax.broadcasted_iota(jnp.int32, block, 1)
    from_right = (lane < REACH) & (tile < across - 1)
    from_left = (lane >= lanes - REACH) & (tile > 0)

    def spread(along_x):
        came = lax.broadcasted_iota(jnp.int32, (2 * lanes, lanes), 0)
        goes = lax.broadcasted_iota(jnp.int32, (2 * lanes, lanes), 1)
        beside = jnp.where(came < lanes + lanes // 2, came, came - 2 * lanes)
        tap = jnp.where(came < lanes, came, beside) - goes + REACH
        matrix = jnp.zeros((2 * lanes, lanes), F32)
        for k in range(9):
            matrix = jnp.where(tap == k, along_x[k], matrix)
        high = matrix.astype(BF16)
        return high, (matrix - high.astype(F32)).astype(BF16)

    def disperse(slot, at, along_y, along_x):
        total = None
        for k in range(9):
            part = along_y[k] * cells[slot, pl.ds(at + k, CHUNK)]
            total = part if total is None else total + part
        right = pltpu.roll(total, across - 1, axis=1)
        left = pltpu.roll(total, 1, axis=1)
        edge = jnp.where(from_right, right, jnp.where(from_left, left, 0.0))
        both = jnp.concatenate([total, edge], axis=2).reshape(CHUNK * across, 2 * lanes)
        high = both.astype(BF16)
        low = (both - high.astype(F32)).astype(BF16)
        result = jnp.dot(high, along_x[0], preferred_element_type=F32)
        result = result + jnp.dot(low, along_x[0], preferred_element_type=F32)
        result = result + jnp.dot(high, along_x[1], preferred_element_type=F32)
        return result.reshape(block)

    forth, back = spread(taps_x), spread(taps_x[::-1])

    def each_chunk(do):
        def step(chunk, carry):
            do(chunk * CHUNK)
            return carry

        lax.fori_loop(0, rows // CHUNK, step, 0)

    def forward_step(step, carry):
        slot = step % 2

        def do(at):
            mid = disperse(slot, at, taps_y, forth)
            mids[step, pl.ds(at, CHUNK)] = mid
            field = mid * (1.0 + rate) / (1.0 + mid * (rate / capacity))
            cells[1 - slot, pl.ds(REACH + at, CHUNK)] = field

        each_chunk(do)
        return carry

    lax.fori_loop(0, STEPS, forward_step, 0)
    last = STEPS % 2

    def grown(grad, step, at):
        denom = 1.0 + mids[step, pl.ds(at, CHUNK)] * (rate / capacity)
        return grad * (1.0 + rate) / (denom * denom)

    def loss(at):
        field = cells[last, pl.ds(REACH + at, CHUNK)]
        code = codes[pl.ds(at, CHUNK)]
        grad = jnp.where(code >= 0.0, (1.0 - code / field) * scale, 0.0)
        cells[1 - last, pl.ds(REACH + at, CHUNK)] = grown(grad, STEPS - 1, at)

    each_chunk(loss)
    for band in range(rows // tall):
        at = band * tall
        density_ref[band * across : (band + 1) * across] = jnp.swapaxes(
            cells[last, REACH + at : REACH + at + tall], 0, 1
        )

    def backward_step(step, carry):
        slot = (1 - last + step) % 2

        def do(at):
            grad = disperse(slot, at, taps_y[::-1], back)
            cells[1 - slot, pl.ds(REACH + at, CHUNK)] = grown(grad, STEPS - 2 - step, at)

        each_chunk(do)
        return carry

    lax.fori_loop(0, STEPS - 1, backward_step, 0)
    slot = (1 - last + STEPS - 1) % 2

    def final(at):
        codes[pl.ds(at, CHUNK)] = disperse(slot, at, taps_y[::-1], back)

    each_chunk(final)
    for band in range(rows // tall):
        at = band * tall
        grad_ref[band * across : (band + 1) * across] = jnp.swapaxes(
            codes[at : at + tall], 0, 1
        ).astype(BF16)


def raster(species, got, scale, tiles_y, tiles_x):
    tiles, two, lanes = got.shape
    tall = two // 2
    rows = tiles_y * tall

    def whole(shape):
        return pl.BlockSpec(shape, lambda: (0,) * len(shape))

    return pl.pallas_call(
        functools.partial(raster_body, scale),
        out_shape=[
            jax.ShapeDtypeStruct((tiles, tall, lanes), F32),
            jax.ShapeDtypeStruct((tiles, tall, lanes), BF16),
        ],
        in_specs=[pl.BlockSpec(memory_space=pltpu.SMEM), whole(got.shape)],
        out_specs=[whole((tiles, tall, lanes))] * 2,
        scratch_shapes=[
            pltpu.VMEM((2, rows + 2 * REACH, tiles_x, lanes), F32),
            pltpu.VMEM((STEPS, rows, tiles_x, lanes), F32),
            pltpu.VMEM((rows, tiles_x, lanes), F32),
        ],
        compiler_params=pltpu.CompilerParams(vmem_limit_bytes=48 << 20),
        name="raster_steps",
    )(species, got)


def forward_body(x_ref, w_in_ref, b_in_ref, w_out_ref, b_out_ref, intensity_ref):
    chunk = 512
    x = x_ref[...]
    log_rate = b_out_ref[...]
    for at in range(0, w_in_ref.shape[1], chunk):
        pre = jnp.dot(x, w_in_ref[:, at : at + chunk], preferred_element_type=F32)
        pre = pre + b_in_ref[:, at : at + chunk]
        hidden = (pre / (1.0 + jnp.exp(-pre))).astype(BF16)
        log_rate = log_rate + jnp.dot(
            hidden, w_out_ref[at : at + chunk, :], preferred_element_type=F32
        )
    intensity_ref[...] = jnp.exp(log_rate)


def forward(x, w_in, b_in, w_out, b_out, block=512):
    rows, cov = x.shape
    hid, species = w_out.shape

    def whole(shape):
        return pl.BlockSpec(shape, lambda i: (0, 0), pipeline_mode=pl.Buffered(1))

    return pl.pallas_call(
        forward_body,
        out_shape=jax.ShapeDtypeStruct((rows, species), F32),
        grid=(rows // block,),
        in_specs=[
            pl.BlockSpec((block, cov), lambda i: (i, 0)),
            whole((cov, hid)),
            whole((1, hid)),
            whole((hid, species)),
            whole((1, species)),
        ],
        out_specs=pl.BlockSpec((block, species), lambda i: (i, 0)),
        compiler_params=pltpu.CompilerParams(vmem_limit_bytes=40 << 20),
        name="land_forward",
    )(x, w_in, b_in[None, :], w_out, b_out[None, :])


def gates_body(core_ref, x_ref, w_in_ref, b_in_ref, hidden_ref, slope_ref):
    pre = jnp.dot(x_ref[...], w_in_ref[...], preferred_element_type=F32) + b_in_ref[...]
    gate = 1.0 / (1.0 + jnp.exp(-pre))
    scaled = pre * gate
    hidden_ref[...] = scaled.astype(BF16)
    slope_ref[...] = gate + scaled * (1.0 - gate)


def gates(core, x, w_in, b_in):
    n_y = 4
    rows, cov = x.shape
    hid = w_in.shape[1]
    width = hid // n_y // 2
    block = pl.BlockSpec((rows, width), lambda j, c: (0, j))
    return pl.pallas_call(
        gates_body,
        out_shape=[
            jax.ShapeDtypeStruct((rows, hid // 2), BF16),
            jax.ShapeDtypeStruct((rows, hid // 2), F32),
        ],
        grid_spec=pltpu.PrefetchScalarGridSpec(
            num_scalar_prefetch=1,
            grid=(n_y,),
            in_specs=[
                pl.BlockSpec((rows, cov), lambda j, c: (0, 0), pipeline_mode=pl.Buffered(1)),
                pl.BlockSpec((cov, width), lambda j, c: (0, 2 * j + c[0])),
                pl.BlockSpec((1, width), lambda j, c: (0, 2 * j + c[0])),
            ],
            out_specs=[block, block],
        ),
        compiler_params=pltpu.CompilerParams(vmem_limit_bytes=40 << 20),
        name="land_gates",
    )(core, x, w_in, b_in[None, :])


def backward_body(
    core_ref,
    x_own,
    x_other,
    dlog_own,
    dlog_other,
    hidden_own,
    hidden_other,
    slope_own,
    slope_other,
    w_out_ref,
    out_ref,
    in_acc,
    out_acc,
):
    j = pl.program_id(0)
    w_out = w_out_ref[...]

    def parts(x_ref, dlog_ref, hidden_ref, slope_ref):
        dlog = dlog_ref[...]
        dhidden = lax.dot_general(
            dlog, w_out, (((1,), (1,)), ((), ())), preferred_element_type=F32
        )
        dpre = (dhidden * slope_ref[...]).astype(BF16)
        rows = (((0,), (0,)), ((), ()))
        return (
            lax.dot_general(x_ref[...], dpre, rows, preferred_element_type=F32),
            lax.dot_general(hidden_ref[...], dlog, rows, preferred_element_type=F32),
        )

    in_acc[...], out_acc[...] = parts(x_own, dlog_own, hidden_own, slope_own)
    in_part, out_part = parts(x_other, dlog_other, hidden_other, slope_other)
    in_acc[...] += in_part
    out_acc[...] += out_part
    n_y = 4
    zx = out_ref.shape[0] // n_y
    tiles = in_acc.shape[1] // 128
    rows = in_acc.shape[0] // out_ref.shape[0] // 2
    units = out_acc.shape[0] // zx
    for y in range(n_y):
        for p in range(zx):
            for c in range(2):
                for k in range(tiles):
                    out_ref[
                        y * zx + p, pl.ds((j * tiles + k) * 2 * rows + c * rows, rows), :
                    ] = in_acc[
                        pl.ds((y * 2 * zx + c * zx + p) * rows, rows),
                        k * 128 : (k + 1) * 128,
                    ]
    base = 2 * rows * tiles * n_y
    for p in range(zx):
        out_ref[j * zx + p, base : base + units, :] = out_acc[p * units : (p + 1) * units, :]


def backward(core, x, dlog, hidden, slope, w_out, peers):
    n_y = 4
    rows, cov = x[0].shape
    hid, species = w_out.shape
    width = hid // n_y // 2
    send_rows = cov // peers * (hid // 2 // 128) + hid // 2 // peers

    def fixed(shape):
        return pl.BlockSpec(
            shape, lambda j, c: (0,) * len(shape), pipeline_mode=pl.Buffered(1)
        )

    grid_spec = pltpu.PrefetchScalarGridSpec(
        num_scalar_prefetch=1,
        grid=(n_y,),
        in_specs=[fixed((rows, cov))] * 2
        + [fixed((rows, species))] * 2
        + [pl.BlockSpec((rows, width), lambda j, c: (0, j))] * 4
        + [pl.BlockSpec((width, species), lambda j, c: (2 * j + c[0], 0))],
        out_specs=fixed((peers, send_rows, 128)),
        scratch_shapes=[pltpu.VMEM((cov, width), F32), pltpu.VMEM((width, species), F32)],
    )
    return pl.pallas_call(
        backward_body,
        out_shape=jax.ShapeDtypeStruct((peers, send_rows, 128), F32),
        grid_spec=grid_spec,
        compiler_params=pltpu.CompilerParams(vmem_limit_bytes=50 << 20),
        name="land_backward",
    )(core, *x, *dlog, *hidden, *slope, w_out)


def pack_body(wide, owner_ref, cell_ref, intensity_ref, send_ref, slot_ref):
    devices, tall, species = send_ref.shape
    slot_count = tall - 8
    rows = intensity_ref.shape[0]
    half = devices * slot_count // 2
    block = 256
    owner = owner_ref[...]
    hot = jnp.where(lax.broadcasted_iota(jnp.int32, (devices, rows), 0) == owner, 1.0, 0.0)
    first = lax.broadcasted_iota(jnp.int32, (block, block), 0)
    second = lax.broadcasted_iota(jnp.int32, (block, block), 1)
    earlier = jnp.where(first < second, 1.0, 0.0).astype(BF16)
    count = jnp.zeros((devices, 1), F32)
    parts = []
    for at in range(0, rows, block):
        here = hot[:, at : at + block]
        before = jnp.dot(here.astype(BF16), earlier, preferred_element_type=F32) + count
        parts.append(jnp.sum(before * here, axis=0, keepdims=True))
        count = count + jnp.sum(here, axis=1, keepdims=True)
    slot = jnp.concatenate(parts, axis=1).astype(jnp.int32)
    flat = owner * slot_count + slot
    slot_ref[...] = flat

    cell = cell_ref[...].astype(F32)
    row = jnp.floor(cell / wide)
    col = cell - row * wide
    taken = lax.broadcasted_iota(jnp.int32, (slot_count, rows), 0) == slot
    places = jnp.concatenate(
        [jnp.where(taken, row + 1.0, 0.0), jnp.where(taken, col, 0.0)], axis=0
    ).astype(BF16)
    table = lax.dot_general(
        places, hot.astype(BF16), (((1,), (1,)), ((), ())), preferred_element_type=F32
    ).T
    table = jnp.concatenate([table, jnp.zeros((devices, species - 2 * slot_count), F32)], axis=1)
    line = lax.broadcasted_iota(jnp.int32, (devices, 8, species), 1)
    send_ref[:, slot_count:, :] = jnp.where(line == 0, table[:, None, :], 0.0).astype(BF16)

    key = jnp.where(flat >= half, flat - half, flat)
    upper = jnp.broadcast_to(flat, (8, rows)).T[:, :1] >= half
    value = intensity_ref[...]
    value = jnp.concatenate(
        [jnp.where(upper, 0.0, value), jnp.where(upper, value, 0.0)], axis=1
    ).astype(BF16)
    step = 16 * slot_count
    ids = lax.broadcasted_iota(jnp.int32, (step, rows), 0)
    for at in range(0, half, step):
        pick = jnp.where(ids == key - at, 1.0, 0.0).astype(BF16)
        out = jnp.dot(pick, value, preferred_element_type=F32)
        for side in range(2):
            to = (side * half + at) // slot_count
            send_ref[to : to + 16, :slot_count, :] = (
                out[:, side * species : (side + 1) * species]
                .reshape(16, slot_count, species)
                .astype(BF16)
            )


def pack(owner, cell, intensity, devices, slot_count, wide):
    rows, species = intensity.shape

    def whole(shape):
        return pl.BlockSpec(shape, lambda: (0,) * len(shape))

    return pl.pallas_call(
        functools.partial(pack_body, wide),
        out_shape=[
            jax.ShapeDtypeStruct((devices, slot_count + 8, species), BF16),
            jax.ShapeDtypeStruct((1, rows), jnp.int32),
        ],
        in_specs=[whole((1, rows)), whole((1, rows)), whole((rows, species))],
        out_specs=[whole((devices, slot_count + 8, species)), whole((1, rows))],
        compiler_params=pltpu.CompilerParams(vmem_limit_bytes=48 << 20),
        name="pack_cells",
    )(owner, cell, intensity)


def place_body(slot_count, got_ref, code_ref, out_ref, total):
    sources, _, species = got_ref.shape
    tall, wide = code_ref.shape[1:]
    half = tall // 2
    keys = half * wide
    group = 4
    values = jnp.swapaxes(got_ref[:, :slot_count, :].astype(F32), 0, 1).astype(BF16)
    spots = got_ref[:, slot_count : slot_count + 8, :].astype(F32)[:, 0, :]
    along = spots.T
    ids = lax.broadcasted_iota(jnp.int32, (keys, sources), 0)
    for first in range(0, slot_count, group):
        hots, rows = [], []
        for slot in range(first, first + group):
            row = along[slot : slot + 1, :].astype(jnp.int32) - 1
            col = along[slot_count + slot : slot_count + slot + 1, :].astype(jnp.int32)
            cell = row * wide + col
            key = jnp.where(row >= half, cell - keys, cell)
            hots.append(jnp.where(ids == key, 1.0, 0.0).astype(BF16))
            upper = spots[:, slot : slot + 1] > half
            value = values[slot].astype(F32)
            rows.append(
                jnp.concatenate(
                    [jnp.where(upper, 0.0, value), jnp.where(upper, value, 0.0)], axis=1
                ).astype(BF16)
            )
        part = jnp.dot(
            jnp.concatenate(hots, axis=1),
            jnp.concatenate(rows, axis=0),
            preferred_element_type=F32,
        )
        if first == 0:
            total[...] = part
        else:
            total[...] += part
    lines = [
        total[
            r % half * wide : (r % half + 1) * wide,
            r // half * species : (r // half + 1) * species,
        ].T
        for r in range(tall)
    ]
    out_ref[:, :tall, :] = jnp.swapaxes(jnp.stack(lines), 0, 1).astype(BF16)
    out_ref[:, tall:, :] = code_ref[...]


def place(got, code, slot_count):
    _, tall, wide = code.shape
    species = got.shape[2]

    def whole(shape):
        return pl.BlockSpec(shape, lambda: (0,) * len(shape))

    return pl.pallas_call(
        functools.partial(place_body, slot_count),
        out_shape=jax.ShapeDtypeStruct((species, 2 * tall, wide), BF16),
        in_specs=[whole(got.shape), whole(code.shape)],
        out_specs=whole((species, 2 * tall, wide)),
        scratch_shapes=[pltpu.VMEM((tall * wide // 2, 2 * species), F32)],
        compiler_params=pltpu.CompilerParams(vmem_limit_bytes=40 << 20),
        name="place_cells",
    )(got, code)


def pick_body(wide, index_ref, table_ref, *refs):
    out_ref = refs[-1]
    rows, lanes = out_ref.shape
    index = index_ref[...]
    if index.shape[1] != 1:
        index = jnp.broadcast_to(index, (8, rows)).T[:, :1]
    if wide:
        keys = table_ref.shape[1] // 2
        table = jnp.concatenate([table_ref[:, :keys], table_ref[:, keys:]], axis=0)
        dims = (((1,), (1,)), ((), ()))
    else:
        keys = table_ref.shape[0] // 2
        table = jnp.concatenate([table_ref[:keys, :], table_ref[keys:, :]], axis=1)
        dims = (((1,), (0,)), ((), ()))
    upper = index >= keys
    key = jnp.where(upper, index - keys, index)
    ids = lax.broadcasted_iota(jnp.int32, (index.shape[0], keys), 1)
    hot = jnp.where(ids == key, 1.0, 0.0).astype(BF16)
    both = lax.dot_general(hot, table, dims, preferred_element_type=F32)
    picked = jnp.where(upper, both[:, lanes:], both[:, :lanes])
    if len(refs) > 1:
        picked = picked * refs[0][...]
    out_ref[...] = picked.astype(BF16)


def pick(index, table, factors=None, wide=False, block=512):
    rows = index.size
    column = index.shape[1] == 1
    lanes = table.shape[0] if wide else table.shape[1]
    block_spec = pl.BlockSpec((block, lanes), lambda i: (i, 0))
    more = () if factors is None else (factors,)
    return pl.pallas_call(
        functools.partial(pick_body, wide),
        out_shape=jax.ShapeDtypeStruct((rows, lanes), BF16),
        grid=(rows // block,),
        in_specs=[
            pl.BlockSpec((block, 1), lambda i: (i, 0))
            if column
            else pl.BlockSpec((1, block), lambda i: (0, i)),
            pl.BlockSpec(table.shape, lambda i: (0, 0), pipeline_mode=pl.Buffered(1)),
        ]
        + [block_spec] * len(more),
        out_specs=block_spec,
        compiler_params=pltpu.CompilerParams(vmem_limit_bytes=40 << 20),
        name="pick_rows",
    )(index, table, *more)


def other_core(values):
    return lax.ppermute(values, "core", [(0, 1), (1, 0)])


def local(
    covariates,
    w_in,
    b_in,
    w_out,
    b_out,
    owner,
    land_cell,
    row_taps,
    col_taps,
    rate,
    capacity,
    observed,
    surveyed,
):
    row_count = covariates.shape[0]
    tiles_y = lax.axis_size("y") * lax.axis_size("core")
    tiles_x = lax.axis_size("z") * lax.axis_size("x")
    devices = tiles_y * tiles_x
    slot_count = 2 * row_count // devices
    slots = devices * slot_count
    height, tile_width, species = observed.shape
    cell_count = height * tile_width
    core = lax.axis_index("core")
    theirs = other_core(covariates)
    intensity = forward(covariates, w_in, b_in, w_out, b_out)

    send, flat_slot = pack(
        owner.reshape(1, row_count),
        land_cell.reshape(1, row_count),
        intensity,
        devices,
        slot_count,
        tile_width,
    )
    got = lax.all_to_all(send, ALL, split_axis=0, concat_axis=0, tiled=True)
    send, own = lax.optimization_barrier((send, covariates))
    own_gates = gates(core[None], own, w_in, b_in)
    got, own_gates = lax.optimization_barrier((got, own_gates))
    got_row = got[:, slot_count, :slot_count].astype(jnp.int32)
    got_col = got[:, slot_count, slot_count : 2 * slot_count].astype(jnp.int32)
    cell_list = jnp.where(got_row > 0, (got_row - 1) * tile_width + got_col, -1).reshape(-1)

    code = jnp.where(surveyed[:, :, None] > 0, observed, -1).astype(BF16)
    code = code.reshape(cell_count, species).T.reshape(species, height, tile_width)
    send = place(got, code, slot_count)
    traits = jnp.concatenate(
        [normalize(row_taps), normalize(col_taps), rate[:, None], capacity[:, None]], axis=1
    )
    traits = jnp.pad(traits, ((0, 0), (0, 32 - traits.shape[1])))
    traits = lax.dynamic_slice_in_dim(traits, lax.axis_index(ALL), 1, axis=0)
    scale = 1.0 / math.sqrt(row_count * devices)
    got = lax.all_to_all(send, ALL, 0, 0, tiled=True)
    send, theirs = lax.optimization_barrier((send, theirs))
    their_gates = gates(core[None], theirs, w_in, b_in)
    got, their_gates = lax.optimization_barrier((got, their_gates))
    density, grad_start = raster(traits, got, scale, tiles_y, tiles_x)
    grad_start = lax.all_to_all(grad_start, ALL, 0, 0, tiled=True).reshape(species, cell_count)

    back_values = pick(cell_list[:, None], grad_start, wide=True)
    home_values = lax.all_to_all(
        back_values.reshape(devices, slot_count, species),
        ALL,
        split_axis=0,
        concat_axis=0,
        tiled=True,
    )
    home_values, density = lax.optimization_barrier((home_values, density))
    density = lax.all_to_all(density, ALL, 0, 0, tiled=True)
    dlog = pick(flat_slot, home_values.reshape(slots, species), intensity)
    peers = devices // 2
    pieces = backward(
        core[None],
        (covariates, theirs),
        (dlog, other_core(dlog)),
        (own_gates[0], their_gates[0]),
        (own_gates[1], their_gates[1]),
        w_out,
        peers,
    )
    pieces, density = lax.optimization_barrier((pieces, density))
    density = density.reshape(species, cell_count).T.reshape(height, tile_width, species)
    pieces = lax.all_to_all(pieces, ("y", "z", "x"), 0, 0)
    pieces, density = lax.optimization_barrier((pieces, density))
    pieces = jnp.sum(pieces, axis=0)
    hid, cov = w_in.shape[1], w_in.shape[0]
    rows_in = cov // devices
    in_rows = 2 * rows_in * (hid // 2 // species)
    grad_w_out = pieces[in_rows:]
    halves = pieces[:in_rows].reshape(4, hid // 8 // species, 2, rows_in, species)
    mine = lax.dynamic_index_in_dim(halves, core, 2, keepdims=False)
    sent_over = other_core(lax.dynamic_index_in_dim(halves, 1 - core, 2, keepdims=False))
    first, second = jnp.where(core == 0, mine, sent_over), jnp.where(core == 0, sent_over, mine)
    grad_w_in = jnp.stack([first, second], axis=1)
    grad_w_in = grad_w_in.transpose(3, 0, 1, 2, 4).reshape(rows_in, hid)
    return (density, grad_w_in, grad_w_out)


def solution(mesh):
    tiles_y, tiles_x = mesh.devices.shape
    split = Mesh(mesh.devices.reshape(tiles_y // 2, 2, tiles_x // 4, 4), ALL)
    in_specs = (
        P(ALL, None),
        P(),
        P(),
        P(),
        P(),
        P(ALL, None),
        P(ALL),
        P(),
        P(),
        P(),
        P(),
        P(TY, TX, None),
        P(TY, TX),
    )
    out_specs = (P(TY, TX, None), P(ALL, None), P(ALL, None))
    return jax.shard_map(local, mesh=split, in_specs=in_specs, out_specs=out_specs, check_vma=False)
```

```python
import functools
import math

import jax
import jax.numpy as jnp
from jax import lax
from jax.experimental import pallas as pl
from jax.experimental.pallas import tpu as pltpu
from jax.sharding import Mesh
from jax.sharding import PartitionSpec as P

STEPS = 4
REACH = 4
CHUNK = 64
TY = ("y", "core")
TX = ("z", "x")
ALL = TY + TX
F32 = jnp.float32
BF16 = jnp.bfloat16


def normalize(taps):
    return taps / jnp.sum(taps, axis=1, keepdims=True)


def raster_body(scale, species_ref, got_ref, density_ref, grad_ref, cells, mids, codes):
    rows, across, lanes = codes.shape
    tall = grad_ref.shape[1]
    taps_y = [species_ref[0, k] for k in range(9)]
    taps_x = [species_ref[0, 9 + k] for k in range(9)]
    rate, capacity = species_ref[0, 18], species_ref[0, 19]
    for slot in range(2):
        cells[slot, 0:REACH] = jnp.zeros((REACH, across, lanes), F32)
        cells[slot, REACH + rows :] = jnp.zeros((REACH, across, lanes), F32)
    for band in range(rows // tall):
        at = band * tall
        tiles = slice(band * across, (band + 1) * across)
        start = jnp.swapaxes(got_ref[tiles, 0:tall, :].astype(F32), 0, 1)
        cells[0, REACH + at : REACH + at + tall] = 0.1 + start
        codes[at : at + tall] = jnp.swapaxes(got_ref[tiles, tall : 2 * tall, :].astype(F32), 0, 1)
    block = (CHUNK, across, lanes)
    lane = lax.broadcasted_iota(jnp.int32, block, 2)
    tile = lax.broadcasted_iota(jnp.int32, block, 1)
    from_right = (lane < REACH) & (tile < across - 1)
    from_left = (lane >= lanes - REACH) & (tile > 0)

    def spread(along_x):
        came = lax.broadcasted_iota(jnp.int32, (2 * lanes, lanes), 0)
        goes = lax.broadcasted_iota(jnp.int32, (2 * lanes, lanes), 1)
        beside = jnp.where(came < lanes + lanes // 2, came, came - 2 * lanes)
        tap = jnp.where(came < lanes, came, beside) - goes + REACH
        matrix = jnp.zeros((2 * lanes, lanes), F32)
        for k in range(9):
            matrix = jnp.where(tap == k, along_x[k], matrix)
        high = matrix.astype(BF16)
        return high, (matrix - high.astype(F32)).astype(BF16)

    def disperse(slot, at, along_y, along_x):
        total = None
        for k in range(9):
            part = along_y[k] * cells[slot, pl.ds(at + k, CHUNK)]
            total = part if total is None else total + part
        right = pltpu.roll(total, across - 1, axis=1)
        left = pltpu.roll(total, 1, axis=1)
        edge = jnp.where(from_right, right, jnp.where(from_left, left, 0.0))
        both = jnp.concatenate([total, edge], axis=2).reshape(CHUNK * across, 2 * lanes)
        high = both.astype(BF16)
        low = (both - high.astype(F32)).astype(BF16)
        result = jnp.dot(high, along_x[0], preferred_element_type=F32)
        result = result + jnp.dot(low, along_x[0], preferred_element_type=F32)
        result = result + jnp.dot(high, along_x[1], preferred_element_type=F32)
        return result.reshape(block)

    forth, back = spread(taps_x), spread(taps_x[::-1])

    def each_chunk(do):
        def step(chunk, carry):
            do(chunk * CHUNK)
            return carry

        lax.fori_loop(0, rows // CHUNK, step, 0)

    def forward_step(step, carry):
        slot = step % 2

        def do(at):
            mid = disperse(slot, at, taps_y, forth)
            mids[step, pl.ds(at, CHUNK)] = mid
            field = mid * (1.0 + rate) / (1.0 + mid * (rate / capacity))
            cells[1 - slot, pl.ds(REACH + at, CHUNK)] = field

        each_chunk(do)
        return carry

    lax.fori_loop(0, STEPS, forward_step, 0)
    last = STEPS % 2

    def grown(grad, step, at):
        denom = 1.0 + mids[step, pl.ds(at, CHUNK)] * (rate / capacity)
        return grad * (1.0 + rate) / (denom * denom)

    def loss(at):
        field = cells[last, pl.ds(REACH + at, CHUNK)]
        code = codes[pl.ds(at, CHUNK)]
        grad = jnp.where(code >= 0.0, (1.0 - code / field) * scale, 0.0)
        cells[1 - last, pl.ds(REACH + at, CHUNK)] = grown(grad, STEPS - 1, at)

    each_chunk(loss)
    for band in range(rows // tall):
        at = band * tall
        density_ref[band * across : (band + 1) * across] = jnp.swapaxes(
            cells[last, REACH + at : REACH + at + tall], 0, 1
        )

    def backward_step(step, carry):
        slot = (1 - last + step) % 2

        def do(at):
            grad = disperse(slot, at, taps_y[::-1], back)
            cells[1 - slot, pl.ds(REACH + at, CHUNK)] = grown(grad, STEPS - 2 - step, at)

        each_chunk(do)
        return carry

    lax.fori_loop(0, STEPS - 1, backward_step, 0)
    slot = (1 - last + STEPS - 1) % 2

    def final(at):
        codes[pl.ds(at, CHUNK)] = disperse(slot, at, taps_y[::-1], back)

    each_chunk(final)
    for band in range(rows // tall):
        at = band * tall
        grad_ref[band * across : (band + 1) * across] = jnp.swapaxes(
            codes[at : at + tall], 0, 1
        ).astype(BF16)


def raster(species, got, scale, tiles_y, tiles_x):
    tiles, two, lanes = got.shape
    tall = two // 2
    rows = tiles_y * tall

    def whole(shape):
        return pl.BlockSpec(shape, lambda: (0,) * len(shape))

    return pl.pallas_call(
        functools.partial(raster_body, scale),
        out_shape=[
            pltpu.HBM((tiles, tall, lanes), F32),
            pltpu.HBM((tiles, tall, lanes), BF16),
        ],
        in_specs=[pl.BlockSpec(memory_space=pltpu.SMEM), whole(got.shape)],
        out_specs=[whole((tiles, tall, lanes))] * 2,
        scratch_shapes=[
            pltpu.VMEM((2, rows + 2 * REACH, tiles_x, lanes), F32),
            pltpu.VMEM((STEPS, rows, tiles_x, lanes), F32),
            pltpu.VMEM((rows, tiles_x, lanes), F32),
        ],
        compiler_params=pltpu.CompilerParams(vmem_limit_bytes=48 << 20),
        name="raster_steps",
    )(species, got)


def forward_body(x_ref, w_in_ref, b_in_ref, w_out_ref, b_out_ref, intensity_ref):
    chunk = 512
    x = x_ref[...]
    log_rate = b_out_ref[...]
    for at in range(0, w_in_ref.shape[1], chunk):
        pre = jnp.dot(x, w_in_ref[:, at : at + chunk], preferred_element_type=F32)
        pre = pre + b_in_ref[:, at : at + chunk]
        hidden = (pre / (1.0 + jnp.exp(-pre))).astype(BF16)
        log_rate = log_rate + jnp.dot(
            hidden, w_out_ref[at : at + chunk, :], preferred_element_type=F32
        )
    intensity_ref[...] = jnp.exp(log_rate)


def forward(x, w_in, b_in, w_out, b_out, block=512):
    rows, cov = x.shape
    hid, species = w_out.shape

    def whole(shape):
        return pl.BlockSpec(shape, lambda i: (0, 0), pipeline_mode=pl.Buffered(1))

    return pl.pallas_call(
        forward_body,
        out_shape=jax.ShapeDtypeStruct((rows, species), F32),
        grid=(rows // block,),
        in_specs=[
            pl.BlockSpec((block, cov), lambda i: (i, 0)),
            whole((cov, hid)),
            whole((1, hid)),
            whole((hid, species)),
            whole((1, species)),
        ],
        out_specs=pl.BlockSpec((block, species), lambda i: (i, 0)),
        compiler_params=pltpu.CompilerParams(vmem_limit_bytes=40 << 20),
        name="land_forward",
    )(*in_hbm(x, w_in), b_in[None, :], *in_hbm(w_out), b_out[None, :])


def gates_body(core_ref, x_ref, w_in_ref, b_in_ref, hidden_ref, slope_ref):
    pre = jnp.dot(x_ref[...], w_in_ref[...], preferred_element_type=F32) + b_in_ref[...]
    gate = 1.0 / (1.0 + jnp.exp(-pre))
    scaled = pre * gate
    hidden_ref[...] = scaled.astype(BF16)
    slope_ref[...] = gate + scaled * (1.0 - gate)


def gates(core, x, w_in, b_in):
    n_y = 4
    rows, cov = x.shape
    hid = w_in.shape[1]
    width = hid // n_y // 2
    block = pl.BlockSpec((rows, width), lambda j, c: (0, j))
    return pl.pallas_call(
        gates_body,
        out_shape=[
            pltpu.HBM((rows, hid // 2), BF16),
            pltpu.HBM((rows, hid // 2), F32),
        ],
        grid_spec=pltpu.PrefetchScalarGridSpec(
            num_scalar_prefetch=1,
            grid=(n_y,),
            in_specs=[
                pl.BlockSpec((rows, cov), lambda j, c: (0, 0), pipeline_mode=pl.Buffered(1)),
                pl.BlockSpec((cov, width), lambda j, c: (0, 2 * j + c[0])),
                pl.BlockSpec((1, width), lambda j, c: (0, 2 * j + c[0])),
            ],
            out_specs=[block, block],
        ),
        compiler_params=pltpu.CompilerParams(vmem_limit_bytes=40 << 20),
        name="land_gates",
    )(core, *in_hbm(x, w_in), b_in[None, :])


def backward_body(
    core_ref,
    x_own,
    x_other,
    dlog_own,
    dlog_other,
    hidden_own,
    hidden_other,
    slope_own,
    slope_other,
    w_out_ref,
    out_ref,
    in_acc,
    out_acc,
):
    j = pl.program_id(0)
    w_out = w_out_ref[...]

    def parts(x_ref, dlog_ref, hidden_ref, slope_ref):
        dlog = dlog_ref[...]
        dhidden = lax.dot_general(
            dlog, w_out, (((1,), (1,)), ((), ())), preferred_element_type=F32
        )
        dpre = (dhidden * slope_ref[...]).astype(BF16)
        rows = (((0,), (0,)), ((), ()))
        return (
            lax.dot_general(x_ref[...], dpre, rows, preferred_element_type=F32),
            lax.dot_general(hidden_ref[...], dlog, rows, preferred_element_type=F32),
        )

    in_acc[...], out_acc[...] = parts(x_own, dlog_own, hidden_own, slope_own)
    in_part, out_part = parts(x_other, dlog_other, hidden_other, slope_other)
    in_acc[...] += in_part
    out_acc[...] += out_part
    n_y = 4
    zx = out_ref.shape[0] // n_y
    tiles = in_acc.shape[1] // 128
    rows = in_acc.shape[0] // out_ref.shape[0] // 2
    units = out_acc.shape[0] // zx
    for y in range(n_y):
        for p in range(zx):
            for c in range(2):
                for k in range(tiles):
                    out_ref[
                        y * zx + p, pl.ds((j * tiles + k) * 2 * rows + c * rows, rows), :
                    ] = in_acc[
                        pl.ds((y * 2 * zx + c * zx + p) * rows, rows),
                        k * 128 : (k + 1) * 128,
                    ]
    base = 2 * rows * tiles * n_y
    for p in range(zx):
        out_ref[j * zx + p, base : base + units, :] = out_acc[p * units : (p + 1) * units, :]


def backward(core, x, dlog, hidden, slope, w_out, peers):
    n_y = 4
    rows, cov = x[0].shape
    hid, species = w_out.shape
    width = hid // n_y // 2
    send_rows = cov // peers * (hid // 2 // 128) + hid // 2 // peers

    def fixed(shape):
        return pl.BlockSpec(
            shape, lambda j, c: (0,) * len(shape), pipeline_mode=pl.Buffered(1)
        )

    grid_spec = pltpu.PrefetchScalarGridSpec(
        num_scalar_prefetch=1,
        grid=(n_y,),
        in_specs=[fixed((rows, cov))] * 2
        + [fixed((rows, species))] * 2
        + [pl.BlockSpec((rows, width), lambda j, c: (0, j))] * 4
        + [pl.BlockSpec((width, species), lambda j, c: (2 * j + c[0], 0))],
        out_specs=fixed((peers, send_rows, 128)),
        scratch_shapes=[pltpu.VMEM((cov, width), F32), pltpu.VMEM((width, species), F32)],
    )
    return pl.pallas_call(
        backward_body,
        out_shape=jax.ShapeDtypeStruct((peers, send_rows, 128), F32),
        grid_spec=grid_spec,
        compiler_params=pltpu.CompilerParams(vmem_limit_bytes=50 << 20),
        name="land_backward",
    )(core, *x, *dlog, *hidden, *slope, w_out)


def in_hbm(*arrays):
    return tuple(pltpu.with_memory_space_constraint(array, pltpu.HBM) for array in arrays)


def pack_body(wide, owner_ref, cell_ref, intensity_ref, send_ref, slot_ref):
    devices, tall, species = send_ref.shape
    slot_count = tall - 8
    rows = intensity_ref.shape[0]
    half = devices * slot_count // 2
    block = 256
    owner = owner_ref[...]
    hot = jnp.where(lax.broadcasted_iota(jnp.int32, (devices, rows), 0) == owner, 1.0, 0.0)
    first = lax.broadcasted_iota(jnp.int32, (block, block), 0)
    second = lax.broadcasted_iota(jnp.int32, (block, block), 1)
    earlier = jnp.where(first < second, 1.0, 0.0).astype(BF16)
    count = jnp.zeros((devices, 1), F32)
    parts = []
    for at in range(0, rows, block):
        here = hot[:, at : at + block]
        before = jnp.dot(here.astype(BF16), earlier, preferred_element_type=F32) + count
        parts.append(jnp.sum(before * here, axis=0, keepdims=True))
        count = count + jnp.sum(here, axis=1, keepdims=True)
    slot = jnp.concatenate(parts, axis=1).astype(jnp.int32)
    flat = owner * slot_count + slot
    slot_ref[...] = flat

    cell = cell_ref[...].astype(F32)
    row = jnp.floor(cell / wide)
    col = cell - row * wide
    taken = lax.broadcasted_iota(jnp.int32, (slot_count, rows), 0) == slot
    places = jnp.concatenate(
        [jnp.where(taken, row + 1.0, 0.0), jnp.where(taken, col, 0.0)], axis=0
    ).astype(BF16)
    table = lax.dot_general(
        places, hot.astype(BF16), (((1,), (1,)), ((), ())), preferred_element_type=F32
    ).T
    table = jnp.concatenate([table, jnp.zeros((devices, species - 2 * slot_count), F32)], axis=1)
    line = lax.broadcasted_iota(jnp.int32, (devices, 8, species), 1)
    send_ref[:, slot_count:, :] = jnp.where(line == 0, table[:, None, :], 0.0).astype(BF16)

    key = jnp.where(flat >= half, flat - half, flat)
    upper = jnp.broadcast_to(flat, (8, rows)).T[:, :1] >= half
    value = intensity_ref[...]
    value = jnp.concatenate(
        [jnp.where(upper, 0.0, value), jnp.where(upper, value, 0.0)], axis=1
    ).astype(BF16)
    step = 16 * slot_count
    ids = lax.broadcasted_iota(jnp.int32, (step, rows), 0)
    for at in range(0, half, step):
        pick = jnp.where(ids == key - at, 1.0, 0.0).astype(BF16)
        out = jnp.dot(pick, value, preferred_element_type=F32)
        for side in range(2):
            to = (side * half + at) // slot_count
            send_ref[to : to + 16, :slot_count, :] = (
                out[:, side * species : (side + 1) * species]
                .reshape(16, slot_count, species)
                .astype(BF16)
            )


def pack(owner, cell, intensity, devices, slot_count, wide):
    rows, species = intensity.shape

    def whole(shape):
        return pl.BlockSpec(shape, lambda: (0,) * len(shape))

    return pl.pallas_call(
        functools.partial(pack_body, wide),
        out_shape=[
            pltpu.HBM((devices, slot_count + 8, species), BF16),
            jax.ShapeDtypeStruct((1, rows), jnp.int32),
        ],
        in_specs=[whole((1, rows)), whole((1, rows)), whole((rows, species))],
        out_specs=[whole((devices, slot_count + 8, species)), whole((1, rows))],
        compiler_params=pltpu.CompilerParams(vmem_limit_bytes=48 << 20),
        name="pack_cells",
    )(owner, cell, intensity)


def place_body(slot_count, got_ref, code_ref, out_ref, total):
    sources, _, species = got_ref.shape
    tall, wide = code_ref.shape[1:]
    half = tall // 2
    keys = half * wide
    group = 4
    values = jnp.swapaxes(got_ref[:, :slot_count, :].astype(F32), 0, 1).astype(BF16)
    spots = got_ref[:, slot_count : slot_count + 8, :].astype(F32)[:, 0, :]
    along = spots.T
    ids = lax.broadcasted_iota(jnp.int32, (keys, sources), 0)
    for first in range(0, slot_count, group):
        hots, rows = [], []
        for slot in range(first, first + group):
            row = along[slot : slot + 1, :].astype(jnp.int32) - 1
            col = along[slot_count + slot : slot_count + slot + 1, :].astype(jnp.int32)
            cell = row * wide + col
            key = jnp.where(row >= half, cell - keys, cell)
            hots.append(jnp.where(ids == key, 1.0, 0.0).astype(BF16))
            upper = spots[:, slot : slot + 1] > half
            value = values[slot].astype(F32)
            rows.append(
                jnp.concatenate(
                    [jnp.where(upper, 0.0, value), jnp.where(upper, value, 0.0)], axis=1
                ).astype(BF16)
            )
        part = jnp.dot(
            jnp.concatenate(hots, axis=1),
            jnp.concatenate(rows, axis=0),
            preferred_element_type=F32,
        )
        if first == 0:
            total[...] = part
        else:
            total[...] += part
    lines = [
        total[
            r % half * wide : (r % half + 1) * wide,
            r // half * species : (r // half + 1) * species,
        ].T
        for r in range(tall)
    ]
    out_ref[:, :tall, :] = jnp.swapaxes(jnp.stack(lines), 0, 1).astype(BF16)
    out_ref[:, tall:, :] = code_ref[...]


def place(got, code, slot_count):
    _, tall, wide = code.shape
    species = got.shape[2]

    def whole(shape):
        return pl.BlockSpec(shape, lambda: (0,) * len(shape))

    return pl.pallas_call(
        functools.partial(place_body, slot_count),
        out_shape=pltpu.HBM((species, 2 * tall, wide), BF16),
        in_specs=[whole(got.shape), whole(code.shape)],
        out_specs=whole((species, 2 * tall, wide)),
        scratch_shapes=[pltpu.VMEM((tall * wide // 2, 2 * species), F32)],
        compiler_params=pltpu.CompilerParams(vmem_limit_bytes=40 << 20),
        name="place_cells",
    )(*in_hbm(got, code))


def pick_body(wide, index_ref, table_ref, *refs):
    out_ref = refs[-1]
    rows, lanes = out_ref.shape
    index = index_ref[...]
    if index.shape[1] != 1:
        index = jnp.broadcast_to(index, (8, rows)).T[:, :1]
    if wide:
        keys = table_ref.shape[1] // 2
        table = jnp.concatenate([table_ref[:, :keys], table_ref[:, keys:]], axis=0)
        dims = (((1,), (1,)), ((), ()))
    else:
        keys = table_ref.shape[0] // 2
        table = jnp.concatenate([table_ref[:keys, :], table_ref[keys:, :]], axis=1)
        dims = (((1,), (0,)), ((), ()))
    upper = index >= keys
    key = jnp.where(upper, index - keys, index)
    ids = lax.broadcasted_iota(jnp.int32, (index.shape[0], keys), 1)
    hot = jnp.where(ids == key, 1.0, 0.0).astype(BF16)
    both = lax.dot_general(hot, table, dims, preferred_element_type=F32)
    picked = jnp.where(upper, both[:, lanes:], both[:, :lanes])
    if len(refs) > 1:
        picked = picked * refs[0][...]
    out_ref[...] = picked.astype(BF16)


def pick(index, table, factors=None, wide=False, block=512):
    rows = index.size
    column = index.shape[1] == 1
    lanes = table.shape[0] if wide else table.shape[1]
    block_spec = pl.BlockSpec((block, lanes), lambda i: (i, 0))
    more = () if factors is None else (factors,)
    return pl.pallas_call(
        functools.partial(pick_body, wide),
        out_shape=jax.ShapeDtypeStruct((rows, lanes), BF16),
        grid=(rows // block,),
        in_specs=[
            pl.BlockSpec((block, 1), lambda i: (i, 0))
            if column
            else pl.BlockSpec((1, block), lambda i: (0, i)),
            pl.BlockSpec(table.shape, lambda i: (0, 0), pipeline_mode=pl.Buffered(1)),
        ]
        + [block_spec] * len(more),
        out_specs=block_spec,
        compiler_params=pltpu.CompilerParams(vmem_limit_bytes=40 << 20),
        name="pick_rows",
    )(*in_hbm(index, table), *more)


def other_core(values):
    return lax.ppermute(values, "core", [(0, 1), (1, 0)])


def local(
    covariates,
    w_in,
    b_in,
    w_out,
    b_out,
    owner,
    land_cell,
    row_taps,
    col_taps,
    rate,
    capacity,
    observed,
    surveyed,
):
    row_count = covariates.shape[0]
    tiles_y = lax.axis_size("y") * lax.axis_size("core")
    tiles_x = lax.axis_size("z") * lax.axis_size("x")
    devices = tiles_y * tiles_x
    slot_count = 2 * row_count // devices
    slots = devices * slot_count
    height, tile_width, species = observed.shape
    cell_count = height * tile_width
    core = lax.axis_index("core")
    theirs = other_core(covariates)
    intensity = forward(covariates, w_in, b_in, w_out, b_out)

    send, flat_slot = pack(
        owner.reshape(1, row_count),
        land_cell.reshape(1, row_count),
        intensity,
        devices,
        slot_count,
        tile_width,
    )
    got = lax.all_to_all(send, ALL, split_axis=0, concat_axis=0, tiled=True)
    send, own = lax.optimization_barrier((send, covariates))
    own_gates = gates(core[None], own, w_in, b_in)
    got, own_gates = lax.optimization_barrier((got, own_gates))
    got_row = got[:, slot_count, :slot_count].astype(jnp.int32)
    got_col = got[:, slot_count, slot_count : 2 * slot_count].astype(jnp.int32)
    cell_list = jnp.where(got_row > 0, (got_row - 1) * tile_width + got_col, -1).reshape(-1)

    code = jnp.where(surveyed[:, :, None] > 0, observed, -1).astype(BF16)
    code = code.reshape(cell_count, species).T.reshape(species, height, tile_width)
    send = place(got, code, slot_count)
    traits = jnp.concatenate(
        [normalize(row_taps), normalize(col_taps), rate[:, None], capacity[:, None]], axis=1
    )
    traits = jnp.pad(traits, ((0, 0), (0, 32 - traits.shape[1])))
    traits = lax.dynamic_slice_in_dim(traits, lax.axis_index(ALL), 1, axis=0)
    scale = 1.0 / math.sqrt(row_count * devices)
    got = lax.all_to_all(send, ALL, 0, 0, tiled=True)
    send, theirs = lax.optimization_barrier((send, theirs))
    their_gates = gates(core[None], theirs, w_in, b_in)
    got, their_gates = lax.optimization_barrier((got, their_gates))
    density, grad_start = raster(traits, got, scale, tiles_y, tiles_x)
    grad_start = lax.all_to_all(grad_start, ALL, 0, 0, tiled=True).reshape(species, cell_count)

    back_values = pick(cell_list[:, None], grad_start, wide=True)
    home_values = lax.all_to_all(
        back_values.reshape(devices, slot_count, species),
        ALL,
        split_axis=0,
        concat_axis=0,
        tiled=True,
    )
    home_values, density = lax.optimization_barrier((home_values, density))
    density = lax.all_to_all(density, ALL, 0, 0, tiled=True)
    dlog = pick(flat_slot, home_values.reshape(slots, species), intensity)
    peers = devices // 2
    pieces = backward(
        core[None],
        (covariates, theirs),
        (dlog, other_core(dlog)),
        (own_gates[0], their_gates[0]),
        (own_gates[1], their_gates[1]),
        w_out,
        peers,
    )
    pieces, density = lax.optimization_barrier((pieces, density))
    density = density.reshape(species, cell_count).T.reshape(height, tile_width, species)
    pieces = lax.all_to_all(pieces, ("y", "z", "x"), 0, 0)
    pieces, density = lax.optimization_barrier((pieces, density))
    pieces = jnp.sum(pieces, axis=0)
    hid, cov = w_in.shape[1], w_in.shape[0]
    rows_in = cov // devices
    in_rows = 2 * rows_in * (hid // 2 // species)
    grad_w_out = pieces[in_rows:]
    halves = pieces[:in_rows].reshape(4, hid // 8 // species, 2, rows_in, species)
    mine = lax.dynamic_index_in_dim(halves, core, 2, keepdims=False)
    sent_over = other_core(lax.dynamic_index_in_dim(halves, 1 - core, 2, keepdims=False))
    first, second = jnp.where(core == 0, mine, sent_over), jnp.where(core == 0, sent_over, mine)
    grad_w_in = jnp.stack([first, second], axis=1)
    grad_w_in = grad_w_in.transpose(3, 0, 1, 2, 4).reshape(rows_in, hid)
    return (density, grad_w_in, grad_w_out)


def solution(mesh):
    tiles_y, tiles_x = mesh.devices.shape
    split = Mesh(mesh.devices.reshape(tiles_y // 2, 2, tiles_x // 4, 4), ALL)
    in_specs = (
        P(ALL, None),
        P(),
        P(),
        P(),
        P(),
        P(ALL, None),
        P(ALL),
        P(),
        P(),
        P(),
        P(),
        P(TY, TX, None),
        P(TY, TX),
    )
    out_specs = (P(TY, TX, None), P(ALL, None), P(ALL, None))
    return jax.shard_map(local, mesh=split, in_specs=in_specs, out_specs=out_specs, check_vma=False)
```

```python
import functools
import math

import jax
import jax.numpy as jnp
from jax import lax
from jax.experimental import pallas as pl
from jax.experimental.pallas import tpu as pltpu
from jax.sharding import Mesh
from jax.sharding import PartitionSpec as P

STEPS = 4
REACH = 4
CHUNK = 128
TY = ("y", "core")
TX = ("z", "x")
ALL = TY + TX
F32 = jnp.float32
BF16 = jnp.bfloat16


def normalize(taps):
    return taps / jnp.sum(taps, axis=1, keepdims=True)


def raster_body(scale, species_ref, got_ref, density_ref, grad_ref, cells, mids, codes):
    rows, across, lanes = codes.shape
    tall = grad_ref.shape[1]
    taps_y = [species_ref[0, k] for k in range(9)]
    taps_x = [species_ref[0, 9 + k] for k in range(9)]
    rate, capacity = species_ref[0, 18], species_ref[0, 19]
    for slot in range(2):
        cells[slot, 0:REACH] = jnp.zeros((REACH, across, lanes), F32)
        cells[slot, REACH + rows :] = jnp.zeros((REACH, across, lanes), F32)
    for band in range(rows // tall):
        at = band * tall
        tiles = slice(band * across, (band + 1) * across)
        start = jnp.swapaxes(got_ref[tiles, 0:tall, :].astype(F32), 0, 1)
        cells[0, REACH + at : REACH + at + tall] = 0.1 + start
        codes[at : at + tall] = jnp.swapaxes(got_ref[tiles, tall : 2 * tall, :].astype(F32), 0, 1)
    block = (CHUNK, across, lanes)
    lane = lax.broadcasted_iota(jnp.int32, block, 2)
    tile = lax.broadcasted_iota(jnp.int32, block, 1)
    from_right = (lane < REACH) & (tile < across - 1)
    from_left = (lane >= lanes - REACH) & (tile > 0)

    def spread(along_x):
        came = lax.broadcasted_iota(jnp.int32, (2 * lanes, lanes), 0)
        goes = lax.broadcasted_iota(jnp.int32, (2 * lanes, lanes), 1)
        beside = jnp.where(came < lanes + lanes // 2, came, came - 2 * lanes)
        tap = jnp.where(came < lanes, came, beside) - goes + REACH
        matrix = jnp.zeros((2 * lanes, lanes), F32)
        for k in range(9):
            matrix = jnp.where(tap == k, along_x[k], matrix)
        high = matrix.astype(BF16)
        return high, (matrix - high.astype(F32)).astype(BF16)

    def disperse(slot, at, along_y, along_x):
        total = None
        for k in range(9):
            part = along_y[k] * cells[slot, pl.ds(at + k, CHUNK)]
            total = part if total is None else total + part
        right = pltpu.roll(total, across - 1, axis=1)
        left = pltpu.roll(total, 1, axis=1)
        edge = jnp.where(from_right, right, jnp.where(from_left, left, 0.0))
        both = jnp.concatenate([total, edge], axis=2).reshape(CHUNK * across, 2 * lanes)
        high = both.astype(BF16)
        low = (both - high.astype(F32)).astype(BF16)
        result = jnp.dot(high, along_x[0], preferred_element_type=F32)
        result = result + jnp.dot(low, along_x[0], preferred_element_type=F32)
        result = result + jnp.dot(high, along_x[1], preferred_element_type=F32)
        return result.reshape(block)

    forth, back = spread(taps_x), spread(taps_x[::-1])

    def each_chunk(do):
        def step(chunk, carry):
            do(chunk * CHUNK)
            return carry

        lax.fori_loop(0, rows // CHUNK, step, 0)

    def forward_step(step, carry):
        slot = step % 2

        def do(at):
            mid = disperse(slot, at, taps_y, forth)
            mids[step, pl.ds(at, CHUNK)] = mid
            field = mid * (1.0 + rate) / (1.0 + mid * (rate / capacity))
            cells[1 - slot, pl.ds(REACH + at, CHUNK)] = field

        each_chunk(do)
        return carry

    lax.fori_loop(0, STEPS, forward_step, 0)
    last = STEPS % 2

    def grown(grad, step, at):
        denom = 1.0 + mids[step, pl.ds(at, CHUNK)] * (rate / capacity)
        return grad * (1.0 + rate) / (denom * denom)

    def loss(at):
        field = cells[last, pl.ds(REACH + at, CHUNK)]
        code = codes[pl.ds(at, CHUNK)]
        grad = jnp.where(code >= 0.0, (1.0 - code / field) * scale, 0.0)
        cells[1 - last, pl.ds(REACH + at, CHUNK)] = grown(grad, STEPS - 1, at)

    each_chunk(loss)
    for band in range(rows // tall):
        at = band * tall
        density_ref[band * across : (band + 1) * across] = jnp.swapaxes(
            cells[last, REACH + at : REACH + at + tall], 0, 1
        )

    def backward_step(step, carry):
        slot = (1 - last + step) % 2

        def do(at):
            grad = disperse(slot, at, taps_y[::-1], back)
            cells[1 - slot, pl.ds(REACH + at, CHUNK)] = grown(grad, STEPS - 2 - step, at)

        each_chunk(do)
        return carry

    lax.fori_loop(0, STEPS - 1, backward_step, 0)
    slot = (1 - last + STEPS - 1) % 2

    def final(at):
        codes[pl.ds(at, CHUNK)] = disperse(slot, at, taps_y[::-1], back)

    each_chunk(final)
    for band in range(rows // tall):
        at = band * tall
        grad_ref[band * across : (band + 1) * across] = jnp.swapaxes(
            codes[at : at + tall], 0, 1
        ).astype(BF16)


def raster(species, got, scale, tiles_y, tiles_x):
    tiles, two, lanes = got.shape
    tall = two // 2
    rows = tiles_y * tall

    def whole(shape):
        return pl.BlockSpec(shape, lambda: (0,) * len(shape))

    return pl.pallas_call(
        functools.partial(raster_body, scale),
        out_shape=[
            pltpu.HBM((tiles, tall, lanes), F32),
            pltpu.HBM((tiles, tall, lanes), BF16),
        ],
        in_specs=[pl.BlockSpec(memory_space=pltpu.SMEM), whole(got.shape)],
        out_specs=[whole((tiles, tall, lanes))] * 2,
        scratch_shapes=[
            pltpu.VMEM((2, rows + 2 * REACH, tiles_x, lanes), F32),
            pltpu.VMEM((STEPS, rows, tiles_x, lanes), F32),
            pltpu.VMEM((rows, tiles_x, lanes), F32),
        ],
        compiler_params=pltpu.CompilerParams(vmem_limit_bytes=48 << 20),
        name="raster_steps",
    )(species, got)


def forward_body(x_ref, w_in_ref, b_in_ref, w_out_ref, b_out_ref, intensity_ref):
    chunk = 512
    x = x_ref[...]
    log_rate = b_out_ref[...]
    for at in range(0, w_in_ref.shape[1], chunk):
        pre = jnp.dot(x, w_in_ref[:, at : at + chunk], preferred_element_type=F32)
        pre = pre + b_in_ref[:, at : at + chunk]
        hidden = (pre / (1.0 + jnp.exp(-pre))).astype(BF16)
        log_rate = log_rate + jnp.dot(
            hidden, w_out_ref[at : at + chunk, :], preferred_element_type=F32
        )
    intensity_ref[...] = jnp.exp(log_rate)


def forward(x, w_in, b_in, w_out, b_out, block=512):
    rows, cov = x.shape
    hid, species = w_out.shape

    def whole(shape):
        return pl.BlockSpec(shape, lambda i: (0, 0), pipeline_mode=pl.Buffered(1))

    return pl.pallas_call(
        forward_body,
        out_shape=jax.ShapeDtypeStruct((rows, species), F32),
        grid=(rows // block,),
        in_specs=[
            pl.BlockSpec((block, cov), lambda i: (i, 0)),
            whole((cov, hid)),
            whole((1, hid)),
            whole((hid, species)),
            whole((1, species)),
        ],
        out_specs=pl.BlockSpec((block, species), lambda i: (i, 0)),
        compiler_params=pltpu.CompilerParams(vmem_limit_bytes=40 << 20),
        name="land_forward",
    )(*in_hbm(x, w_in), b_in[None, :], *in_hbm(w_out), b_out[None, :])


def gates_body(core_ref, x_ref, w_in_ref, b_in_ref, hidden_ref, slope_ref):
    pre = jnp.dot(x_ref[...], w_in_ref[...], preferred_element_type=F32) + b_in_ref[...]
    gate = 1.0 / (1.0 + jnp.exp(-pre))
    scaled = pre * gate
    hidden_ref[...] = scaled.astype(BF16)
    slope_ref[...] = gate + scaled * (1.0 - gate)


def gates(core, x, w_in, b_in):
    n_y = 4
    rows, cov = x.shape
    hid = w_in.shape[1]
    width = hid // n_y // 2
    block = pl.BlockSpec((rows, width), lambda j, c: (0, j))
    return pl.pallas_call(
        gates_body,
        out_shape=[
            pltpu.HBM((rows, hid // 2), BF16),
            pltpu.HBM((rows, hid // 2), F32),
        ],
        grid_spec=pltpu.PrefetchScalarGridSpec(
            num_scalar_prefetch=1,
            grid=(n_y,),
            in_specs=[
                pl.BlockSpec((rows, cov), lambda j, c: (0, 0), pipeline_mode=pl.Buffered(1)),
                pl.BlockSpec((cov, width), lambda j, c: (0, 2 * j + c[0])),
                pl.BlockSpec((1, width), lambda j, c: (0, 2 * j + c[0])),
            ],
            out_specs=[block, block],
        ),
        compiler_params=pltpu.CompilerParams(vmem_limit_bytes=40 << 20),
        name="land_gates",
    )(core, *in_hbm(x, w_in), b_in[None, :])


def backward_body(
    core_ref,
    x_own,
    x_other,
    dlog_own,
    dlog_other,
    hidden_own,
    hidden_other,
    slope_own,
    slope_other,
    w_out_ref,
    out_ref,
    in_acc,
    out_acc,
):
    j = pl.program_id(0)
    w_out = w_out_ref[...]

    def parts(x_ref, dlog_ref, hidden_ref, slope_ref):
        dlog = dlog_ref[...]
        dhidden = lax.dot_general(
            dlog, w_out, (((1,), (1,)), ((), ())), preferred_element_type=F32
        )
        dpre = (dhidden * slope_ref[...]).astype(BF16)
        rows = (((0,), (0,)), ((), ()))
        return (
            lax.dot_general(x_ref[...], dpre, rows, preferred_element_type=F32),
            lax.dot_general(hidden_ref[...], dlog, rows, preferred_element_type=F32),
        )

    in_acc[...], out_acc[...] = parts(x_own, dlog_own, hidden_own, slope_own)
    in_part, out_part = parts(x_other, dlog_other, hidden_other, slope_other)
    in_acc[...] += in_part
    out_acc[...] += out_part
    n_y = 4
    zx = out_ref.shape[0] // n_y
    tiles = in_acc.shape[1] // 128
    rows = in_acc.shape[0] // out_ref.shape[0] // 2
    units = out_acc.shape[0] // zx
    for y in range(n_y):
        for p in range(zx):
            for c in range(2):
                for k in range(tiles):
                    out_ref[
                        y * zx + p, pl.ds((j * tiles + k) * 2 * rows + c * rows, rows), :
                    ] = in_acc[
                        pl.ds((y * 2 * zx + c * zx + p) * rows, rows),
                        k * 128 : (k + 1) * 128,
                    ]
    base = 2 * rows * tiles * n_y
    for p in range(zx):
        out_ref[j * zx + p, base : base + units, :] = out_acc[p * units : (p + 1) * units, :]


def backward(core, x, dlog, hidden, slope, w_out, peers):
    n_y = 4
    rows, cov = x[0].shape
    hid, species = w_out.shape
    width = hid // n_y // 2
    send_rows = cov // peers * (hid // 2 // 128) + hid // 2 // peers

    def fixed(shape):
        return pl.BlockSpec(
            shape, lambda j, c: (0,) * len(shape), pipeline_mode=pl.Buffered(1)
        )

    grid_spec = pltpu.PrefetchScalarGridSpec(
        num_scalar_prefetch=1,
        grid=(n_y,),
        in_specs=[fixed((rows, cov))] * 2
        + [fixed((rows, species))] * 2
        + [pl.BlockSpec((rows, width), lambda j, c: (0, j))] * 4
        + [pl.BlockSpec((width, species), lambda j, c: (2 * j + c[0], 0))],
        out_specs=fixed((peers, send_rows, 128)),
        scratch_shapes=[pltpu.VMEM((cov, width), F32), pltpu.VMEM((width, species), F32)],
    )
    return pl.pallas_call(
        backward_body,
        out_shape=jax.ShapeDtypeStruct((peers, send_rows, 128), F32),
        grid_spec=grid_spec,
        compiler_params=pltpu.CompilerParams(vmem_limit_bytes=50 << 20),
        name="land_backward",
    )(core, *x, *dlog, *hidden, *slope, w_out)


def in_hbm(*arrays):
    return tuple(pltpu.with_memory_space_constraint(array, pltpu.HBM) for array in arrays)


def pack_body(wide, owner_ref, cell_ref, intensity_ref, send_ref, slot_ref):
    devices, tall, species = send_ref.shape
    slot_count = tall - 8
    rows = intensity_ref.shape[0]
    half = devices * slot_count // 2
    block = 256
    owner = owner_ref[...]
    hot = jnp.where(lax.broadcasted_iota(jnp.int32, (devices, rows), 0) == owner, 1.0, 0.0)
    first = lax.broadcasted_iota(jnp.int32, (block, block), 0)
    second = lax.broadcasted_iota(jnp.int32, (block, block), 1)
    earlier = jnp.where(first < second, 1.0, 0.0).astype(BF16)
    count = jnp.zeros((devices, 1), F32)
    parts = []
    for at in range(0, rows, block):
        here = hot[:, at : at + block]
        before = jnp.dot(here.astype(BF16), earlier, preferred_element_type=F32) + count
        parts.append(jnp.sum(before * here, axis=0, keepdims=True))
        count = count + jnp.sum(here, axis=1, keepdims=True)
    slot = jnp.concatenate(parts, axis=1).astype(jnp.int32)
    flat = owner * slot_count + slot
    slot_ref[...] = flat

    cell = cell_ref[...].astype(F32)
    row = jnp.floor(cell / wide)
    col = cell - row * wide
    taken = lax.broadcasted_iota(jnp.int32, (slot_count, rows), 0) == slot
    places = jnp.concatenate(
        [jnp.where(taken, row + 1.0, 0.0), jnp.where(taken, col, 0.0)], axis=0
    ).astype(BF16)
    table = lax.dot_general(
        places, hot.astype(BF16), (((1,), (1,)), ((), ())), preferred_element_type=F32
    ).T
    table = jnp.concatenate([table, jnp.zeros((devices, species - 2 * slot_count), F32)], axis=1)
    line = lax.broadcasted_iota(jnp.int32, (devices, 8, species), 1)
    send_ref[:, slot_count:, :] = jnp.where(line == 0, table[:, None, :], 0.0).astype(BF16)

    key = jnp.where(flat >= half, flat - half, flat)
    upper = jnp.broadcast_to(flat, (8, rows)).T[:, :1] >= half
    value = intensity_ref[...]
    value = jnp.concatenate(
        [jnp.where(upper, 0.0, value), jnp.where(upper, value, 0.0)], axis=1
    ).astype(BF16)
    step = 16 * slot_count
    ids = lax.broadcasted_iota(jnp.int32, (step, rows), 0)
    for at in range(0, half, step):
        pick = jnp.where(ids == key - at, 1.0, 0.0).astype(BF16)
        out = jnp.dot(pick, value, preferred_element_type=F32)
        for side in range(2):
            to = (side * half + at) // slot_count
            send_ref[to : to + 16, :slot_count, :] = (
                out[:, side * species : (side + 1) * species]
                .reshape(16, slot_count, species)
                .astype(BF16)
            )


def pack(owner, cell, intensity, devices, slot_count, wide):
    rows, species = intensity.shape

    def whole(shape):
        return pl.BlockSpec(shape, lambda: (0,) * len(shape))

    return pl.pallas_call(
        functools.partial(pack_body, wide),
        out_shape=[
            pltpu.HBM((devices, slot_count + 8, species), BF16),
            jax.ShapeDtypeStruct((1, rows), jnp.int32),
        ],
        in_specs=[whole((1, rows)), whole((1, rows)), whole((rows, species))],
        out_specs=[whole((devices, slot_count + 8, species)), whole((1, rows))],
        compiler_params=pltpu.CompilerParams(vmem_limit_bytes=48 << 20),
        name="pack_cells",
    )(owner, cell, intensity)


def place_body(slot_count, got_ref, code_ref, out_ref, total):
    sources, _, species = got_ref.shape
    tall, wide = code_ref.shape[1:]
    half = tall // 2
    keys = half * wide
    group = 4
    values = jnp.swapaxes(got_ref[:, :slot_count, :].astype(F32), 0, 1).astype(BF16)
    spots = got_ref[:, slot_count : slot_count + 8, :].astype(F32)[:, 0, :]
    along = spots.T
    ids = lax.broadcasted_iota(jnp.int32, (keys, sources), 0)
    for first in range(0, slot_count, group):
        hots, rows = [], []
        for slot in range(first, first + group):
            row = along[slot : slot + 1, :].astype(jnp.int32) - 1
            col = along[slot_count + slot : slot_count + slot + 1, :].astype(jnp.int32)
            cell = row * wide + col
            key = jnp.where(row >= half, cell - keys, cell)
            hots.append(jnp.where(ids == key, 1.0, 0.0).astype(BF16))
            upper = spots[:, slot : slot + 1] > half
            value = values[slot].astype(F32)
            rows.append(
                jnp.concatenate(
                    [jnp.where(upper, 0.0, value), jnp.where(upper, value, 0.0)], axis=1
                ).astype(BF16)
            )
        part = jnp.dot(
            jnp.concatenate(hots, axis=1),
            jnp.concatenate(rows, axis=0),
            preferred_element_type=F32,
        )
        if first == 0:
            total[...] = part
        else:
            total[...] += part
    lines = [
        total[
            r % half * wide : (r % half + 1) * wide,
            r // half * species : (r // half + 1) * species,
        ].T
        for r in range(tall)
    ]
    out_ref[:, :tall, :] = jnp.swapaxes(jnp.stack(lines), 0, 1).astype(BF16)
    out_ref[:, tall:, :] = code_ref[...]


def place(got, code, slot_count):
    _, tall, wide = code.shape
    species = got.shape[2]

    def whole(shape):
        return pl.BlockSpec(shape, lambda: (0,) * len(shape))

    return pl.pallas_call(
        functools.partial(place_body, slot_count),
        out_shape=pltpu.HBM((species, 2 * tall, wide), BF16),
        in_specs=[whole(got.shape), whole(code.shape)],
        out_specs=whole((species, 2 * tall, wide)),
        scratch_shapes=[pltpu.VMEM((tall * wide // 2, 2 * species), F32)],
        compiler_params=pltpu.CompilerParams(vmem_limit_bytes=40 << 20),
        name="place_cells",
    )(*in_hbm(got, code))


def pick_body(wide, index_ref, table_ref, *refs):
    out_ref = refs[-1]
    rows, lanes = out_ref.shape
    index = index_ref[...]
    if index.shape[1] != 1:
        index = jnp.broadcast_to(index, (8, rows)).T[:, :1]
    if wide:
        keys = table_ref.shape[1] // 2
        table = jnp.concatenate([table_ref[:, :keys], table_ref[:, keys:]], axis=0)
        dims = (((1,), (1,)), ((), ()))
    else:
        keys = table_ref.shape[0] // 2
        table = jnp.concatenate([table_ref[:keys, :], table_ref[keys:, :]], axis=1)
        dims = (((1,), (0,)), ((), ()))
    upper = index >= keys
    key = jnp.where(upper, index - keys, index)
    ids = lax.broadcasted_iota(jnp.int32, (index.shape[0], keys), 1)
    hot = jnp.where(ids == key, 1.0, 0.0).astype(BF16)
    both = lax.dot_general(hot, table, dims, preferred_element_type=F32)
    picked = jnp.where(upper, both[:, lanes:], both[:, :lanes])
    if len(refs) > 1:
        picked = picked * refs[0][...]
    out_ref[...] = picked.astype(BF16)


def pick(index, table, factors=None, wide=False, block=512):
    rows = index.size
    column = index.shape[1] == 1
    lanes = table.shape[0] if wide else table.shape[1]
    block_spec = pl.BlockSpec((block, lanes), lambda i: (i, 0))
    more = () if factors is None else (factors,)
    return pl.pallas_call(
        functools.partial(pick_body, wide),
        out_shape=jax.ShapeDtypeStruct((rows, lanes), BF16),
        grid=(rows // block,),
        in_specs=[
            pl.BlockSpec((block, 1), lambda i: (i, 0))
            if column
            else pl.BlockSpec((1, block), lambda i: (0, i)),
            pl.BlockSpec(table.shape, lambda i: (0, 0), pipeline_mode=pl.Buffered(1)),
        ]
        + [block_spec] * len(more),
        out_specs=block_spec,
        compiler_params=pltpu.CompilerParams(vmem_limit_bytes=40 << 20),
        name="pick_rows",
    )(index, *in_hbm(table), *more)


def other_core(values):
    return lax.ppermute(values, "core", [(0, 1), (1, 0)])


def local(
    covariates,
    w_in,
    b_in,
    w_out,
    b_out,
    owner,
    land_cell,
    row_taps,
    col_taps,
    rate,
    capacity,
    observed,
    surveyed,
):
    row_count = covariates.shape[0]
    tiles_y = lax.axis_size("y") * lax.axis_size("core")
    tiles_x = lax.axis_size("z") * lax.axis_size("x")
    devices = tiles_y * tiles_x
    slot_count = 2 * row_count // devices
    slots = devices * slot_count
    height, tile_width, species = observed.shape
    cell_count = height * tile_width
    core = lax.axis_index("core")
    theirs = other_core(covariates)
    intensity = forward(covariates, w_in, b_in, w_out, b_out)

    send, flat_slot = pack(
        owner.reshape(1, row_count),
        land_cell.reshape(1, row_count),
        intensity,
        devices,
        slot_count,
        tile_width,
    )
    got = lax.all_to_all(send, ALL, split_axis=0, concat_axis=0, tiled=True)
    send, own = lax.optimization_barrier((send, covariates))
    own_gates = gates(core[None], own, w_in, b_in)
    got, own_gates = lax.optimization_barrier((got, own_gates))
    got_row = got[:, slot_count, :slot_count].astype(jnp.int32)
    got_col = got[:, slot_count, slot_count : 2 * slot_count].astype(jnp.int32)
    cell_list = jnp.where(got_row > 0, (got_row - 1) * tile_width + got_col, -1).reshape(-1)

    code = jnp.where(surveyed[:, :, None] > 0, observed, -1).astype(BF16)
    code = code.reshape(cell_count, species).T.reshape(species, height, tile_width)
    send = place(got, code, slot_count)
    traits = jnp.concatenate(
        [normalize(row_taps), normalize(col_taps), rate[:, None], capacity[:, None]], axis=1
    )
    traits = jnp.pad(traits, ((0, 0), (0, 32 - traits.shape[1])))
    traits = lax.dynamic_slice_in_dim(traits, lax.axis_index(ALL), 1, axis=0)
    scale = 1.0 / math.sqrt(row_count * devices)
    got = lax.all_to_all(send, ALL, 0, 0, tiled=True)
    send, theirs = lax.optimization_barrier((send, theirs))
    their_gates = gates(core[None], theirs, w_in, b_in)
    got, their_gates = lax.optimization_barrier((got, their_gates))
    density, grad_start = raster(traits, got, scale, tiles_y, tiles_x)
    grad_start = lax.all_to_all(grad_start, ALL, 0, 0, tiled=True).reshape(species, cell_count)

    back_values = pick(cell_list[:, None], grad_start, wide=True)
    home_values = lax.all_to_all(
        back_values.reshape(devices, slot_count, species),
        ALL,
        split_axis=0,
        concat_axis=0,
        tiled=True,
    )
    home_values, density = lax.optimization_barrier((home_values, density))
    density = lax.all_to_all(density, ALL, 0, 0, tiled=True)
    dlog = pick(flat_slot, home_values.reshape(slots, species), intensity)
    peers = devices // 2
    pieces = backward(
        core[None],
        (covariates, theirs),
        (dlog, other_core(dlog)),
        (own_gates[0], their_gates[0]),
        (own_gates[1], their_gates[1]),
        w_out,
        peers,
    )
    pieces, density = lax.optimization_barrier((pieces, density))
    density = density.reshape(species, cell_count).T.reshape(height, tile_width, species)
    pieces = lax.all_to_all(pieces, ("y", "z", "x"), 0, 0)
    pieces, density = lax.optimization_barrier((pieces, density))
    pieces = jnp.sum(pieces, axis=0)
    hid, cov = w_in.shape[1], w_in.shape[0]
    rows_in = cov // devices
    in_rows = 2 * rows_in * (hid // 2 // species)
    grad_w_out = pieces[in_rows:]
    halves = pieces[:in_rows].reshape(4, hid // 8 // species, 2, rows_in, species)
    mine = lax.dynamic_index_in_dim(halves, core, 2, keepdims=False)
    sent_over = other_core(lax.dynamic_index_in_dim(halves, 1 - core, 2, keepdims=False))
    first, second = jnp.where(core == 0, mine, sent_over), jnp.where(core == 0, sent_over, mine)
    grad_w_in = jnp.stack([first, second], axis=1)
    grad_w_in = grad_w_in.transpose(3, 0, 1, 2, 4).reshape(rows_in, hid)
    return (density, grad_w_in, grad_w_out)


def solution(mesh):
    tiles_y, tiles_x = mesh.devices.shape
    split = Mesh(mesh.devices.reshape(tiles_y // 2, 2, tiles_x // 4, 4), ALL)
    in_specs = (
        P(ALL, None),
        P(),
        P(),
        P(),
        P(),
        P(ALL, None),
        P(ALL),
        P(),
        P(),
        P(),
        P(),
        P(TY, TX, None),
        P(TY, TX),
    )
    out_specs = (P(TY, TX, None), P(ALL, None), P(ALL, None))
    return jax.shard_map(local, mesh=split, in_specs=in_specs, out_specs=out_specs, check_vma=False)
```

```python
import functools
import math

import jax
import jax.numpy as jnp
from jax import lax
from jax.experimental import pallas as pl
from jax.experimental.pallas import tpu as pltpu
from jax.sharding import Mesh
from jax.sharding import PartitionSpec as P

STEPS = 4
REACH = 4
CHUNK = 128
TY = ("y", "core")
TX = ("z", "x")
ALL = TY + TX
F32 = jnp.float32
BF16 = jnp.bfloat16


def normalize(taps):
    return taps / jnp.sum(taps, axis=1, keepdims=True)


def raster_body(scale, species_ref, got_ref, density_ref, grad_ref, cells, mids, codes):
    rows, across, lanes = codes.shape
    tall = grad_ref.shape[1]
    taps_y = [species_ref[0, k] for k in range(9)]
    taps_x = [species_ref[0, 9 + k] for k in range(9)]
    rate, capacity = species_ref[0, 18], species_ref[0, 19]
    for slot in range(2):
        cells[slot, 0:REACH] = jnp.zeros((REACH, across, lanes), F32)
        cells[slot, REACH + rows :] = jnp.zeros((REACH, across, lanes), F32)
    for band in range(rows // tall):
        at = band * tall
        tiles = slice(band * across, (band + 1) * across)
        start = jnp.swapaxes(got_ref[tiles, 0:tall, :].astype(F32), 0, 1)
        cells[0, REACH + at : REACH + at + tall] = 0.1 + start
        codes[at : at + tall] = jnp.swapaxes(got_ref[tiles, tall : 2 * tall, :].astype(F32), 0, 1)
    block = (CHUNK, across, lanes)
    lane = lax.broadcasted_iota(jnp.int32, block, 2)
    tile = lax.broadcasted_iota(jnp.int32, block, 1)
    from_right = (lane < REACH) & (tile < across - 1)
    from_left = (lane >= lanes - REACH) & (tile > 0)

    def spread(along_x):
        came = lax.broadcasted_iota(jnp.int32, (2 * lanes, lanes), 0)
        goes = lax.broadcasted_iota(jnp.int32, (2 * lanes, lanes), 1)
        beside = jnp.where(came < lanes + lanes // 2, came, came - 2 * lanes)
        tap = jnp.where(came < lanes, came, beside) - goes + REACH
        matrix = jnp.zeros((2 * lanes, lanes), F32)
        for k in range(9):
            matrix = jnp.where(tap == k, along_x[k], matrix)
        high = matrix.astype(BF16)
        return high, (matrix - high.astype(F32)).astype(BF16)

    def disperse(slot, at, along_y, along_x):
        total = None
        for k in range(9):
            part = along_y[k] * cells[slot, pl.ds(at + k, CHUNK)]
            total = part if total is None else total + part
        right = pltpu.roll(total, across - 1, axis=1)
        left = pltpu.roll(total, 1, axis=1)
        edge = jnp.where(from_right, right, jnp.where(from_left, left, 0.0))
        both = jnp.concatenate([total, edge], axis=2).reshape(CHUNK * across, 2 * lanes)
        high = both.astype(BF16)
        low = (both - high.astype(F32)).astype(BF16)
        result = jnp.dot(high, along_x[0], preferred_element_type=F32)
        result = result + jnp.dot(low, along_x[0], preferred_element_type=F32)
        result = result + jnp.dot(high, along_x[1], preferred_element_type=F32)
        return result.reshape(block)

    forth, back = spread(taps_x), spread(taps_x[::-1])

    def each_chunk(do):
        def step(chunk, carry):
            do(chunk * CHUNK)
            return carry

        lax.fori_loop(0, rows // CHUNK, step, 0)

    def forward_step(step, carry):
        slot = step % 2

        def do(at):
            mid = disperse(slot, at, taps_y, forth)
            mids[step, pl.ds(at, CHUNK)] = mid
            field = mid * (1.0 + rate) / (1.0 + mid * (rate / capacity))
            cells[1 - slot, pl.ds(REACH + at, CHUNK)] = field

        each_chunk(do)
        return carry

    lax.fori_loop(0, STEPS, forward_step, 0)
    last = STEPS % 2

    def grown(grad, step, at):
        denom = 1.0 + mids[step, pl.ds(at, CHUNK)] * (rate / capacity)
        return grad * (1.0 + rate) / (denom * denom)

    def loss(at):
        field = cells[last, pl.ds(REACH + at, CHUNK)]
        code = codes[pl.ds(at, CHUNK)]
        grad = jnp.where(code >= 0.0, (1.0 - code / field) * scale, 0.0)
        cells[1 - last, pl.ds(REACH + at, CHUNK)] = grown(grad, STEPS - 1, at)

    each_chunk(loss)
    for band in range(rows // tall):
        at = band * tall
        density_ref[band * across : (band + 1) * across] = jnp.swapaxes(
            cells[last, REACH + at : REACH + at + tall], 0, 1
        )

    def backward_step(step, carry):
        slot = (1 - last + step) % 2

        def do(at):
            grad = disperse(slot, at, taps_y[::-1], back)
            cells[1 - slot, pl.ds(REACH + at, CHUNK)] = grown(grad, STEPS - 2 - step, at)

        each_chunk(do)
        return carry

    lax.fori_loop(0, STEPS - 1, backward_step, 0)
    slot = (1 - last + STEPS - 1) % 2

    def final(at):
        codes[pl.ds(at, CHUNK)] = disperse(slot, at, taps_y[::-1], back)

    each_chunk(final)
    for band in range(rows // tall):
        at = band * tall
        grad_ref[band * across : (band + 1) * across] = jnp.swapaxes(
            codes[at : at + tall], 0, 1
        ).astype(BF16)


def raster(species, got, scale, tiles_y, tiles_x):
    tiles, two, lanes = got.shape
    tall = two // 2
    rows = tiles_y * tall

    def whole(shape):
        return pl.BlockSpec(shape, lambda: (0,) * len(shape))

    return pl.pallas_call(
        functools.partial(raster_body, scale),
        out_shape=[
            pltpu.HBM((tiles, tall, lanes), F32),
            pltpu.HBM((tiles, tall, lanes), BF16),
        ],
        in_specs=[pl.BlockSpec(memory_space=pltpu.SMEM), whole(got.shape)],
        out_specs=[whole((tiles, tall, lanes))] * 2,
        scratch_shapes=[
            pltpu.VMEM((2, rows + 2 * REACH, tiles_x, lanes), F32),
            pltpu.VMEM((STEPS, rows, tiles_x, lanes), F32),
            pltpu.VMEM((rows, tiles_x, lanes), F32),
        ],
        compiler_params=pltpu.CompilerParams(vmem_limit_bytes=48 << 20),
        name="raster_steps",
    )(species, got)


def forward_body(x_ref, w_in_ref, b_in_ref, w_out_ref, b_out_ref, intensity_ref):
    chunk = 512
    x = x_ref[...]
    log_rate = b_out_ref[...]
    for at in range(0, w_in_ref.shape[1], chunk):
        pre = jnp.dot(x, w_in_ref[:, at : at + chunk], preferred_element_type=F32)
        pre = pre + b_in_ref[:, at : at + chunk]
        hidden = (pre / (1.0 + jnp.exp(-pre))).astype(BF16)
        log_rate = log_rate + jnp.dot(
            hidden, w_out_ref[at : at + chunk, :], preferred_element_type=F32
        )
    intensity_ref[...] = jnp.exp(log_rate)


def forward(x, w_in, b_in, w_out, b_out, block=512):
    rows, cov = x.shape
    hid, species = w_out.shape

    def whole(shape):
        return pl.BlockSpec(shape, lambda i: (0, 0), pipeline_mode=pl.Buffered(1))

    return pl.pallas_call(
        forward_body,
        out_shape=jax.ShapeDtypeStruct((rows, species), F32),
        grid=(rows // block,),
        in_specs=[
            pl.BlockSpec((block, cov), lambda i: (i, 0)),
            whole((cov, hid)),
            whole((1, hid)),
            whole((hid, species)),
            whole((1, species)),
        ],
        out_specs=pl.BlockSpec((block, species), lambda i: (i, 0)),
        compiler_params=pltpu.CompilerParams(vmem_limit_bytes=40 << 20),
        name="land_forward",
    )(*in_hbm(x, w_in), b_in[None, :], *in_hbm(w_out), b_out[None, :])


def gates_body(core_ref, x_ref, w_in_ref, b_in_ref, hidden_ref, slope_ref):
    pre = jnp.dot(x_ref[...], w_in_ref[...], preferred_element_type=F32) + b_in_ref[...]
    gate = 1.0 / (1.0 + jnp.exp(-pre))
    scaled = pre * gate
    hidden_ref[...] = scaled.astype(BF16)
    slope_ref[...] = gate + scaled * (1.0 - gate)


def gates(core, x, w_in, b_in):
    n_y = 4
    rows, cov = x.shape
    hid = w_in.shape[1]
    width = hid // n_y // 2
    block = pl.BlockSpec((rows, width), lambda j, c: (0, j))
    return pl.pallas_call(
        gates_body,
        out_shape=[
            pltpu.HBM((rows, hid // 2), BF16),
            pltpu.HBM((rows, hid // 2), F32),
        ],
        grid_spec=pltpu.PrefetchScalarGridSpec(
            num_scalar_prefetch=1,
            grid=(n_y,),
            in_specs=[
                pl.BlockSpec((rows, cov), lambda j, c: (0, 0), pipeline_mode=pl.Buffered(1)),
                pl.BlockSpec((cov, width), lambda j, c: (0, 2 * j + c[0])),
                pl.BlockSpec((1, width), lambda j, c: (0, 2 * j + c[0])),
            ],
            out_specs=[block, block],
        ),
        compiler_params=pltpu.CompilerParams(vmem_limit_bytes=40 << 20),
        name="land_gates",
    )(core, *in_hbm(x, w_in), b_in[None, :])


def backward_body(
    core_ref,
    x_own,
    x_other,
    dlog_own,
    dlog_other,
    hidden_own,
    hidden_other,
    slope_own,
    slope_other,
    w_out_ref,
    out_ref,
    in_acc,
    out_acc,
):
    j = pl.program_id(0)
    w_out = w_out_ref[...]

    def parts(x_ref, dlog_ref, hidden_ref, slope_ref):
        dlog = dlog_ref[...]
        dhidden = lax.dot_general(
            dlog, w_out, (((1,), (1,)), ((), ())), preferred_element_type=F32
        )
        dpre = (dhidden * slope_ref[...]).astype(BF16)
        rows = (((0,), (0,)), ((), ()))
        return (
            lax.dot_general(x_ref[...], dpre, rows, preferred_element_type=F32),
            lax.dot_general(hidden_ref[...], dlog, rows, preferred_element_type=F32),
        )

    in_acc[...], out_acc[...] = parts(x_own, dlog_own, hidden_own, slope_own)
    in_part, out_part = parts(x_other, dlog_other, hidden_other, slope_other)
    in_acc[...] += in_part
    out_acc[...] += out_part
    n_y = 4
    zx = out_ref.shape[0] // n_y
    tiles = in_acc.shape[1] // 128
    rows = in_acc.shape[0] // out_ref.shape[0] // 2
    units = out_acc.shape[0] // zx
    for y in range(n_y):
        for p in range(zx):
            for c in range(2):
                for k in range(tiles):
                    out_ref[
                        y * zx + p, pl.ds((j * tiles + k) * 2 * rows + c * rows, rows), :
                    ] = in_acc[
                        pl.ds((y * 2 * zx + c * zx + p) * rows, rows),
                        k * 128 : (k + 1) * 128,
                    ]
    base = 2 * rows * tiles * n_y
    for p in range(zx):
        out_ref[j * zx + p, base : base + units, :] = out_acc[p * units : (p + 1) * units, :]


def backward(core, x, dlog, hidden, slope, w_out, peers):
    n_y = 4
    rows, cov = x[0].shape
    hid, species = w_out.shape
    width = hid // n_y // 2
    send_rows = cov // peers * (hid // 2 // 128) + hid // 2 // peers

    def fixed(shape):
        return pl.BlockSpec(
            shape, lambda j, c: (0,) * len(shape), pipeline_mode=pl.Buffered(1)
        )

    grid_spec = pltpu.PrefetchScalarGridSpec(
        num_scalar_prefetch=1,
        grid=(n_y,),
        in_specs=[fixed((rows, cov))] * 2
        + [fixed((rows, species))] * 2
        + [pl.BlockSpec((rows, width), lambda j, c: (0, j))] * 4
        + [pl.BlockSpec((width, species), lambda j, c: (2 * j + c[0], 0))],
        out_specs=fixed((peers, send_rows, 128)),
        scratch_shapes=[pltpu.VMEM((cov, width), F32), pltpu.VMEM((width, species), F32)],
    )
    return pl.pallas_call(
        backward_body,
        out_shape=jax.ShapeDtypeStruct((peers, send_rows, 128), F32),
        grid_spec=grid_spec,
        compiler_params=pltpu.CompilerParams(vmem_limit_bytes=50 << 20),
        name="land_backward",
    )(core, *x, *dlog, *hidden, *slope, w_out)


def in_hbm(*arrays):
    return tuple(pltpu.with_memory_space_constraint(array, pltpu.HBM) for array in arrays)


def pack_body(wide, owner_ref, cell_ref, intensity_ref, send_ref, slot_ref):
    devices, tall, species = send_ref.shape
    slot_count = tall - 8
    rows = intensity_ref.shape[0]
    half = devices * slot_count // 2
    block = 256
    owner = owner_ref[...]
    hot = jnp.where(lax.broadcasted_iota(jnp.int32, (devices, rows), 0) == owner, 1.0, 0.0)
    first = lax.broadcasted_iota(jnp.int32, (block, block), 0)
    second = lax.broadcasted_iota(jnp.int32, (block, block), 1)
    earlier = jnp.where(first < second, 1.0, 0.0).astype(BF16)
    count = jnp.zeros((devices, 1), F32)
    parts = []
    for at in range(0, rows, block):
        here = hot[:, at : at + block]
        before = jnp.dot(here.astype(BF16), earlier, preferred_element_type=F32) + count
        parts.append(jnp.sum(before * here, axis=0, keepdims=True))
        count = count + jnp.sum(here, axis=1, keepdims=True)
    slot = jnp.concatenate(parts, axis=1).astype(jnp.int32)
    flat = owner * slot_count + slot
    slot_ref[...] = flat

    cell = cell_ref[...].astype(F32)
    row = jnp.floor(cell / wide)
    col = cell - row * wide
    taken = lax.broadcasted_iota(jnp.int32, (slot_count, rows), 0) == slot
    places = jnp.concatenate(
        [jnp.where(taken, row + 1.0, 0.0), jnp.where(taken, col, 0.0)], axis=0
    ).astype(BF16)
    table = lax.dot_general(
        places, hot.astype(BF16), (((1,), (1,)), ((), ())), preferred_element_type=F32
    ).T
    table = jnp.concatenate([table, jnp.zeros((devices, species - 2 * slot_count), F32)], axis=1)
    line = lax.broadcasted_iota(jnp.int32, (devices, 8, species), 1)
    send_ref[:, slot_count:, :] = jnp.where(line == 0, table[:, None, :], 0.0).astype(BF16)

    key = jnp.where(flat >= half, flat - half, flat)
    upper = jnp.broadcast_to(flat, (8, rows)).T[:, :1] >= half
    value = intensity_ref[...]
    value = jnp.concatenate(
        [jnp.where(upper, 0.0, value), jnp.where(upper, value, 0.0)], axis=1
    ).astype(BF16)
    step = 16 * slot_count
    ids = lax.broadcasted_iota(jnp.int32, (step, rows), 0)
    for at in range(0, half, step):
        pick = jnp.where(ids == key - at, 1.0, 0.0).astype(BF16)
        out = jnp.dot(pick, value, preferred_element_type=F32)
        for side in range(2):
            to = (side * half + at) // slot_count
            send_ref[to : to + 16, :slot_count, :] = (
                out[:, side * species : (side + 1) * species]
                .reshape(16, slot_count, species)
                .astype(BF16)
            )


def pack(owner, cell, intensity, devices, slot_count, wide):
    rows, species = intensity.shape

    def whole(shape):
        return pl.BlockSpec(shape, lambda: (0,) * len(shape))

    return pl.pallas_call(
        functools.partial(pack_body, wide),
        out_shape=[
            pltpu.HBM((devices, slot_count + 8, species), BF16),
            jax.ShapeDtypeStruct((1, rows), jnp.int32),
        ],
        in_specs=[whole((1, rows)), whole((1, rows)), whole((rows, species))],
        out_specs=[whole((devices, slot_count + 8, species)), whole((1, rows))],
        compiler_params=pltpu.CompilerParams(vmem_limit_bytes=48 << 20),
        name="pack_cells",
    )(owner, cell, intensity)


def place_body(slot_count, got_ref, code_ref, out_ref, total):
    sources, _, species = got_ref.shape
    tall, wide = code_ref.shape[1:]
    half = tall // 2
    keys = half * wide
    group = 4
    values = jnp.swapaxes(got_ref[:, :slot_count, :].astype(F32), 0, 1).astype(BF16)
    spots = got_ref[:, slot_count : slot_count + 8, :].astype(F32)[:, 0, :]
    along = spots.T
    ids = lax.broadcasted_iota(jnp.int32, (keys, sources), 0)
    for first in range(0, slot_count, group):
        hots, rows = [], []
        for slot in range(first, first + group):
            row = along[slot : slot + 1, :].astype(jnp.int32) - 1
            col = along[slot_count + slot : slot_count + slot + 1, :].astype(jnp.int32)
            cell = row * wide + col
            key = jnp.where(row >= half, cell - keys, cell)
            hots.append(jnp.where(ids == key, 1.0, 0.0).astype(BF16))
            upper = spots[:, slot : slot + 1] > half
            value = values[slot].astype(F32)
            rows.append(
                jnp.concatenate(
                    [jnp.where(upper, 0.0, value), jnp.where(upper, value, 0.0)], axis=1
                ).astype(BF16)
            )
        part = jnp.dot(
            jnp.concatenate(hots, axis=1),
            jnp.concatenate(rows, axis=0),
            preferred_element_type=F32,
        )
        if first == 0:
            total[...] = part
        else:
            total[...] += part
    lines = [
        total[
            r % half * wide : (r % half + 1) * wide,
            r // half * species : (r // half + 1) * species,
        ].T
        for r in range(tall)
    ]
    out_ref[:, :tall, :] = jnp.swapaxes(jnp.stack(lines), 0, 1).astype(BF16)
    out_ref[:, tall:, :] = code_ref[...]


def place(got, code, slot_count):
    _, tall, wide = code.shape
    species = got.shape[2]

    def whole(shape):
        return pl.BlockSpec(shape, lambda: (0,) * len(shape))

    return pl.pallas_call(
        functools.partial(place_body, slot_count),
        out_shape=pltpu.HBM((species, 2 * tall, wide), BF16),
        in_specs=[whole(got.shape), whole(code.shape)],
        out_specs=whole((species, 2 * tall, wide)),
        scratch_shapes=[pltpu.VMEM((tall * wide // 2, 2 * species), F32)],
        compiler_params=pltpu.CompilerParams(vmem_limit_bytes=40 << 20),
        name="place_cells",
    )(*in_hbm(got, code))


def pick_body(wide, index_ref, table_ref, *refs):
    out_ref = refs[-1]
    rows, lanes = out_ref.shape
    index = index_ref[...]
    if index.shape[1] != 1:
        index = jnp.broadcast_to(index, (8, rows)).T[:, :1]
    if wide:
        keys = table_ref.shape[1] // 2
        table = jnp.concatenate([table_ref[:, :keys], table_ref[:, keys:]], axis=0)
        dims = (((1,), (1,)), ((), ()))
    else:
        keys = table_ref.shape[0] // 2
        table = jnp.concatenate([table_ref[:keys, :], table_ref[keys:, :]], axis=1)
        dims = (((1,), (0,)), ((), ()))
    upper = index >= keys
    key = jnp.where(upper, index - keys, index)
    ids = lax.broadcasted_iota(jnp.int32, (index.shape[0], keys), 1)
    hot = jnp.where(ids == key, 1.0, 0.0).astype(BF16)
    both = lax.dot_general(hot, table, dims, preferred_element_type=F32)
    picked = jnp.where(upper, both[:, lanes:], both[:, :lanes])
    if len(refs) > 1:
        picked = picked * refs[0][...]
    out_ref[...] = picked.astype(BF16)


def pick(index, table, factors=None, wide=False, block=1024):
    rows = index.size
    column = index.shape[1] == 1
    lanes = table.shape[0] if wide else table.shape[1]
    block_spec = pl.BlockSpec((block, lanes), lambda i: (i, 0))
    more = () if factors is None else (factors,)
    return pl.pallas_call(
        functools.partial(pick_body, wide),
        out_shape=jax.ShapeDtypeStruct((rows, lanes), BF16),
        grid=(rows // block,),
        in_specs=[
            pl.BlockSpec((block, 1), lambda i: (i, 0))
            if column
            else pl.BlockSpec((1, block), lambda i: (0, i)),
            pl.BlockSpec(table.shape, lambda i: (0, 0), pipeline_mode=pl.Buffered(1)),
        ]
        + [block_spec] * len(more),
        out_specs=block_spec,
        compiler_params=pltpu.CompilerParams(vmem_limit_bytes=40 << 20),
        name="pick_rows",
    )(index, *in_hbm(table), *more)


def other_core(values):
    return lax.ppermute(values, "core", [(0, 1), (1, 0)])


def local(
    covariates,
    w_in,
    b_in,
    w_out,
    b_out,
    owner,
    land_cell,
    row_taps,
    col_taps,
    rate,
    capacity,
    observed,
    surveyed,
):
    row_count = covariates.shape[0]
    tiles_y = lax.axis_size("y") * lax.axis_size("core")
    tiles_x = lax.axis_size("z") * lax.axis_size("x")
    devices = tiles_y * tiles_x
    slot_count = 2 * row_count // devices
    slots = devices * slot_count
    height, tile_width, species = observed.shape
    cell_count = height * tile_width
    core = lax.axis_index("core")
    theirs = other_core(covariates)
    intensity = forward(covariates, w_in, b_in, w_out, b_out)

    send, flat_slot = pack(
        owner.reshape(1, row_count),
        land_cell.reshape(1, row_count),
        intensity,
        devices,
        slot_count,
        tile_width,
    )
    got = lax.all_to_all(send, ALL, split_axis=0, concat_axis=0, tiled=True)
    send, own = lax.optimization_barrier((send, covariates))
    own_gates = gates(core[None], own, w_in, b_in)
    got, own_gates = lax.optimization_barrier((got, own_gates))
    got_row = got[:, slot_count, :slot_count].astype(jnp.int32)
    got_col = got[:, slot_count, slot_count : 2 * slot_count].astype(jnp.int32)
    cell_list = jnp.where(got_row > 0, (got_row - 1) * tile_width + got_col, -1).reshape(-1)

    code = jnp.where(surveyed[:, :, None] > 0, observed, -1).astype(BF16)
    code = code.reshape(cell_count, species).T.reshape(species, height, tile_width)
    send = place(got, code, slot_count)
    traits = jnp.concatenate(
        [normalize(row_taps), normalize(col_taps), rate[:, None], capacity[:, None]], axis=1
    )
    traits = jnp.pad(traits, ((0, 0), (0, 32 - traits.shape[1])))
    traits = lax.dynamic_slice_in_dim(traits, lax.axis_index(ALL), 1, axis=0)
    scale = 1.0 / math.sqrt(row_count * devices)
    got = lax.all_to_all(send, ALL, 0, 0, tiled=True)
    send, theirs = lax.optimization_barrier((send, theirs))
    their_gates = gates(core[None], theirs, w_in, b_in)
    got, their_gates = lax.optimization_barrier((got, their_gates))
    density, grad_start = raster(traits, got, scale, tiles_y, tiles_x)
    grad_start = lax.all_to_all(grad_start, ALL, 0, 0, tiled=True).reshape(species, cell_count)

    back_values = pick(cell_list[:, None], grad_start, wide=True)
    home_values = lax.all_to_all(
        back_values.reshape(devices, slot_count, species),
        ALL,
        split_axis=0,
        concat_axis=0,
        tiled=True,
    )
    home_values, density = lax.optimization_barrier((home_values, density))
    density = lax.all_to_all(density, ALL, 0, 0, tiled=True)
    dlog = pick(flat_slot, home_values.reshape(slots, species), intensity)
    peers = devices // 2
    pieces = backward(
        core[None],
        (covariates, theirs),
        (dlog, other_core(dlog)),
        (own_gates[0], their_gates[0]),
        (own_gates[1], their_gates[1]),
        w_out,
        peers,
    )
    pieces, density = lax.optimization_barrier((pieces, density))
    density = density.reshape(species, cell_count).T.reshape(height, tile_width, species)
    pieces = lax.all_to_all(pieces, ("y", "z", "x"), 0, 0)
    pieces, density = lax.optimization_barrier((pieces, density))
    pieces = jnp.sum(pieces, axis=0)
    hid, cov = w_in.shape[1], w_in.shape[0]
    rows_in = cov // devices
    in_rows = 2 * rows_in * (hid // 2 // species)
    grad_w_out = pieces[in_rows:]
    halves = pieces[:in_rows].reshape(4, hid // 8 // species, 2, rows_in, species)
    mine = lax.dynamic_index_in_dim(halves, core, 2, keepdims=False)
    sent_over = other_core(lax.dynamic_index_in_dim(halves, 1 - core, 2, keepdims=False))
    first, second = jnp.where(core == 0, mine, sent_over), jnp.where(core == 0, sent_over, mine)
    grad_w_in = jnp.stack([first, second], axis=1)
    grad_w_in = grad_w_in.transpose(3, 0, 1, 2, 4).reshape(rows_in, hid)
    return (density, grad_w_in, grad_w_out)


def solution(mesh):
    tiles_y, tiles_x = mesh.devices.shape
    split = Mesh(mesh.devices.reshape(tiles_y // 2, 2, tiles_x // 4, 4), ALL)
    in_specs = (
        P(ALL, None),
        P(),
        P(),
        P(),
        P(),
        P(ALL, None),
        P(ALL),
        P(),
        P(),
        P(),
        P(),
        P(TY, TX, None),
        P(TY, TX),
    )
    out_specs = (P(TY, TX, None), P(ALL, None), P(ALL, None))
    return jax.shard_map(local, mesh=split, in_specs=in_specs, out_specs=out_specs, check_vma=False)
```
